32 devices in a mesh: dp: 16 (over z, y, x), mp: 2 (over core).
Axes of the slice: x: 2, y: 2, z: 4, core: 2. Of those that a mesh axis runs over, the one named last changes fastest.
Arguments:
- tokens: bfloat16 [36864, 768], P(('dp', 'mp')), may hold values from -6 to 6
- lengths: int32 [64], P('dp'), may hold values from 256 to 576, as said below
- gain_attn: float32 [768], replicated, may hold values from 0.5 to 1.5
- w_query: bfloat16 [768, 768], P(None, 'mp'), may hold values from -0.21875 to 0.21875
- w_key: bfloat16 [768, 768], P(None, 'mp'), may hold values from -0.21875 to 0.21875
- w_value: bfloat16 [768, 768], P(None, 'mp'), may hold values from -0.21875 to 0.21875
- w_out: bfloat16 [768, 768], P('mp'), may hold values from -1.75 to 1.75
- gain_ffn: float32 [768], replicated, may hold values from 0.5 to 1.5
- w_gate: bfloat16 [768, 2048], P(None, 'mp'), may hold values from -0.21875 to 0.21875
- w_up: bfloat16 [768, 2048], P(None, 'mp'), may hold values from -0.21875 to 0.21875
- w_down: bfloat16 [2048, 768], P('mp'), may hold values from -0.125 to 0.125
- cotangent: bfloat16 [36864, 768], P(('dp', 'mp')), may hold values from -6 to 6
Outputs:
- output: bfloat16 [36864, 768], P(('dp', 'mp'))
- grad_input: float32 [36864, 768], P(('dp', 'mp'))
- grad_gain_attn: float32 [768], replicated
- grad_query: float32 [768, 768], P('dp', 'mp')
- grad_key: float32 [768, 768], P('dp', 'mp')
- grad_value: float32 [768, 768], P('dp', 'mp')
- grad_out: float32 [768, 768], P('mp', 'dp')
- grad_gain_ffn: float32 [768], replicated
- grad_gate: float32 [768, 2048], P('dp', 'mp')
- grad_up: float32 [768, 2048], P('dp', 'mp')
- grad_down: float32 [2048, 768], P('mp', 'dp')
The draws below stay inside these ranges and needn't reach their ends.
Inputs may be any that keep to these rules, and one draw needn't show every extreme that they name: `lengths`: each item's count of valid tokens, the class token first; exactly half of the 64 items have 576 and the other half 256.
All inputs are finite; a program needn't handle non-finite values.
Results may differ from the reference program's by a relative error of at most 0.013.
Values may be sent and summed in bfloat16 or wider, within the bound.
No kernel may reach another device: no remote copies, remote signals or barrier semaphores. Data moves between devices by JAX's collectives and lax.ppermute only.
A program may use at most 192 MiB of HBM per device.

```python
import jax
import jax.numpy as jnp
from jax import lax

D = 768
HEADS = 12
HEAD = 64
FF = 2048
SLOTS = 576
SHORT = 256
ITEMS_DEV = 4
ITEMS = 64
TOKENS = 36864
N_DP = 16


def draw_lengths(key, part):
    order = jax.random.permutation(key, ITEMS)
    return jnp.where(order < ITEMS // 2, SLOTS, SHORT).astype(jnp.int32)


def with_spikes(drawn, own_key, source, target, shards_of, factor):
    def block_of(position):
        return (jnp.arange(drawn.shape[position]) // (drawn.shape[position] // shards_of)).reshape((-1,) + (1,) * (drawn.ndim - 1 - position))

    near = jax.random.permutation(own_key, shards_of)[block_of(target)]
    other_side = (block_of(target) + shards_of // 2) % shards_of
    return jnp.where((block_of(source) == near) | (block_of(source) == other_side), factor * drawn, drawn)


def level_of(stream_key, dims, split, smallest, top_value):
    level = 1.0
    for position, blocks in split:
        heights = jax.random.uniform(jax.random.fold_in(jax.random.fold_in(stream_key, 6), position), (blocks,), jnp.float32, smallest / len(split), top_value / len(split))
        level = level * jnp.repeat(jnp.exp(heights), dims[position] // blocks).reshape((-1,) + (1,) * (len(dims) - 1 - position))
    return level


def noise(own_key, extent, width, bound, pieces=(), held_as=jnp.bfloat16):
    array = width * jax.random.normal(own_key, extent, jnp.float32)
    if pieces:
        array = array * level_of(own_key, extent, pieces, -0.22, 0.18)
    return jnp.clip(array, -bound, bound).astype(held_as)


def heavy_noise(key, dims, spread, reach, shards, heavy, held_as=jnp.bfloat16):
    drawn = spread * jax.random.normal(key, dims, jnp.float32)
    if shards:
        drawn = drawn * level_of(key, dims, shards, -0.22, 0.18)
    return jnp.clip(with_spikes(drawn, jax.random.fold_in(key, 3), *heavy), -reach, reach).astype(held_as)


def setup_inputs(seed: int = 0) -> dict:
    splits = jax.random.split(jax.random.key(seed), 13)
    return {
        "tokens": noise(splits[0], (TOKENS, D), 1.0, 6.0, ((0, 32),)),
        "lengths": draw_lengths(jax.random.fold_in(splits[12], 71), 0),
        "gain_attn": jnp.clip(1.0 + 0.1 * jax.random.normal(splits[2], (D,), jnp.float32), 0.5, 1.5),
        "w_query": noise(splits[3], (D, D), D ** -0.5, 0.21875, ((1, 2),)),
        "w_key": noise(splits[4], (D, D), D ** -0.5, 0.21875, ((1, 2),)),
        "w_value": noise(splits[5], (D, D), D ** -0.5, 0.21875, ((1, 2),)),
        "w_out": noise(splits[6], (D, D), (D // 64) ** -0.5, 1.75, ((0, 2),)),
        "gain_ffn": jnp.clip(1.0 + 0.1 * jax.random.normal(splits[7], (D,), jnp.float32), 0.5, 1.5),
        "w_gate": noise(splits[8], (D, FF), D ** -0.5, 0.21875, ((1, 2),)),
        "w_up": noise(splits[9], (D, FF), D ** -0.5, 0.21875, ((1, 2),)),
        "w_down": noise(splits[10], (FF, D), FF ** -0.5, 0.125, ((0, 2),)),
        "cotangent": heavy_noise(splits[11], (TOKENS, D), 1.0, 6.0, ((0, 32),), (0, 1, 32, 2.75)),
    }


@jax.custom_vjp
def low(v):
    return lax.optimization_barrier(v.astype(jnp.bfloat16)).astype(jnp.float32)

@jax.custom_vjp
def low_back(v):
    return v

def low_keep(v):
    return (low(v), None)

def low_pass(kept, grad):
    return (grad,)

def back_keep(v):
    return (v, None)

def back_low(kept, grad):
    return (low(grad),)
low.defvjp(low_keep, low_pass)
low_back.defvjp(back_keep, back_low)
EPS = 1e-05
THETA = 10000.0
HIGHEST = lax.Precision.HIGHEST

def tables(row_count):
    places = (jnp.arange(row_count) % SLOTS).astype(jnp.float32)
    inv_freq = THETA ** (-(2.0 * jnp.arange(HEAD // 2).astype(jnp.float32)) / HEAD)
    angles = places[:, None] * inv_freq[None, :]
    return (jnp.cos(angles), jnp.sin(angles))

def rotate(values, cosine, sine):
    half_width = values.shape[-1] // 2
    first_half = values[..., :half_width]
    second = values[..., half_width:]
    cos_b = cosine[:, None, :]
    sin_b = sine[:, None, :]
    return jnp.concatenate([first_half * cos_b - second * sin_b, second * cos_b + first_half * sin_b], -1)

def matmul(left, right):
    return jnp.dot(left, right, precision=HIGHEST)

def layer(block, item_lens, gain_attn, w_query, w_key, w_value, w_out, gain_ffn, w_gate, w_up, w_down):
    row_count = block.shape[0]
    inv_rms_a = lax.rsqrt(lax.optimization_barrier(jnp.mean(block * block, -1, keepdims=True)) + EPS)
    normed_a = low(block * inv_rms_a * gain_attn)
    cosine, sine = tables(row_count)
    queries = low_back(matmul(normed_a, w_query)).reshape(row_count, HEADS, HEAD)
    key_heads = low_back(matmul(normed_a, w_key)).reshape(row_count, HEADS, HEAD)
    values = low(low_back(matmul(normed_a, w_value))).reshape(row_count, HEADS, HEAD)
    queries = low(rotate(queries, cosine, sine))
    key_heads = low(rotate(key_heads, cosine, sine))
    places = jnp.arange(SLOTS)
    score_scale = HEAD ** (-0.5)

    def attend(item_args):
        q_item, k_item, v_item, length = item_args
        scores = jnp.einsum('qhd,khd->hqk', q_item, k_item, precision=HIGHEST) * score_scale
        allowed = (places[None, :] <= places[:, None]) & (places[None, :] < length)
        scores = low_back(jnp.where(allowed[None], scores, -1e+30))
        soft_probs = jax.nn.softmax(scores, -1)
        return jnp.einsum('hqk,khd->qhd', low(soft_probs), v_item, precision=HIGHEST)
    item_shape = (row_count // SLOTS, SLOTS, HEADS, HEAD)
    mixed_heads = lax.map(jax.checkpoint(attend), (queries.reshape(item_shape), key_heads.reshape(item_shape), values.reshape(item_shape), item_lens))
    mixed_heads = low_back(low(mixed_heads.reshape(row_count, HEADS * HEAD)))
    middle = block + low_back(matmul(mixed_heads, w_out))
    inv_rms_f = lax.rsqrt(lax.optimization_barrier(jnp.mean(middle * middle, -1, keepdims=True)) + EPS)
    normed_f = low(middle * inv_rms_f * gain_ffn)
    gate_pre = low_back(matmul(normed_f, w_gate))
    up_pre = low_back(matmul(normed_f, w_up))
    hidden = low(jax.nn.silu(gate_pre) * up_pre)
    final_rows = middle + low_back(matmul(hidden, w_down))
    row_index = jnp.arange(row_count)
    valid_rows = row_index % SLOTS < item_lens[row_index // SLOTS]
    return jnp.where(valid_rows[:, None], final_rows, 0.0)

def reference(tokens, lengths, gain_attn, w_query, w_key, w_value, w_out, gain_ffn, w_gate, w_up, w_down, cotangent):
    weights = tuple((weight.astype(jnp.float32) for weight in (gain_attn, w_query, w_key, w_value, w_out, gain_ffn, w_gate, w_up, w_down)))
    blocks = tokens.astype(jnp.float32).reshape(N_DP, ITEMS_DEV * SLOTS, D)
    len_blocks = lengths.reshape(N_DP, ITEMS_DEV)
    cot_blocks = cotangent.astype(jnp.float32).reshape(N_DP, ITEMS_DEV * SLOTS, D)

    def block_step(totals, block_args):
        block, item_lens, grad_rows = block_args

        def forward(inputs, *params):
            return layer(inputs, item_lens, *params)
        result, pull_back = jax.vjp(forward, block, *weights)
        grad_list = pull_back(grad_rows)
        totals = tuple((total + update for total, update in zip(totals, grad_list[1:])))
        return (totals, (result.astype(jnp.bfloat16), grad_list[0]))
    zero_grads = tuple((jnp.zeros(weight.shape, jnp.float32) for weight in weights))
    totals, (outputs, grads_in) = lax.scan(block_step, zero_grads, (blocks, len_blocks, cot_blocks))
    return (outputs.reshape(-1, D), grads_in.reshape(-1, D), totals[0], totals[1], totals[2], totals[3], totals[4], totals[5], totals[6], totals[7], totals[8])
```

```python
import functools

import jax
import jax.numpy as jnp
import numpy as np
from jax import lax
from jax.experimental import pallas as pl
from jax.experimental.pallas import tpu as pltpu
from jax.sharding import PartitionSpec as P

HEAD = 64
PAIR = 2 * HEAD
SLOTS = 576
EPS = 1e-05
THETA = 10000.0
ROWS = 384
CHUNK = 512
F32 = jnp.float32
BF16 = jnp.bfloat16
NEG = -1e30
BLOCKS = ((512, 64), (256, 256), (0, 256))
MIB = 1 << 20


def dot(left, right):
    return jnp.dot(left, right, preferred_element_type=F32)


def dot_nt(left, right):
    return lax.dot_general(left, right, (((1,), (1,)), ((), ())), preferred_element_type=F32)


def params(mib):
    return pltpu.CompilerParams(vmem_limit_bytes=mib * MIB)


def cost(flops, moved, special=0):
    return pl.CostEstimate(flops=int(flops), bytes_accessed=int(moved), transcendentals=int(special))


def sds(shape, dtype):
    return jax.ShapeDtypeStruct(shape, dtype)


def whole(shape):
    zeros = (0,) * len(shape)
    return pl.BlockSpec(shape, lambda *_: zeros, pipeline_mode=pl.Buffered(1))


def rows_of(width, rows=ROWS):
    return pl.BlockSpec((rows, width), lambda i, *_: (i, 0))


def position_tables(row_count):
    inv_freq = np.float32(THETA) ** (
        -(np.float32(2.0) * np.arange(HEAD // 2, dtype=np.float32)) / np.float32(HEAD)
    )
    places = (np.arange(row_count) % SLOTS).astype(np.float32)
    angles = (places[:, None] * inv_freq[None, :].astype(np.float32)).astype(np.float32)
    cosine, sine = np.cos(angles), np.sin(angles)
    cos_t = np.tile(cosine, (1, PAIR // cosine.shape[1]))
    sin_t = np.tile(np.concatenate([-sine, sine], 1), (1, 2))
    return cos_t.astype(np.float32), sin_t.astype(np.float32)


def swap_halves(values):
    lane = lax.broadcasted_iota(jnp.int32, values.shape, 1)
    return jnp.where(
        lane % HEAD < HEAD // 2,
        pltpu.roll(values, PAIR - HEAD // 2, 1),
        pltpu.roll(values, HEAD // 2, 1),
    )


def relative_order(dp):
    return [b0 + 2 * b1 + 4 * z for b0 in range(2) for b1 in range(2) for z in range(dp // 4)]


def store_transposed(value, scratch, out_ref, me_ref, dp):
    width = value.shape[1]
    group = width // dp
    if group % 16:
        out_ref[...] = value.T
        return
    scratch[...] = value.T
    for place, relative in enumerate(relative_order(dp)):
        start = pl.multiple_of(group * jnp.bitwise_xor(me_ref[0], relative), 16)
        out_ref[group * place : group * place + group, :] = scratch[pl.ds(start, group), :]


def finish_transposed(array, me, dp):
    group = array.shape[0] // dp
    if group % 16 == 0:
        return array
    index = jnp.bitwise_xor(me, jnp.asarray(relative_order(dp), jnp.int32))
    return jnp.take(array.reshape(dp, group, -1), index, axis=0).reshape(array.shape)


def qkv_kernel(
    first, dp, me_ref, x_ref, gain_ref, wq_ref, wk_ref, wv_ref, cos_ref, sin_ref, q_ref, k_ref, v_ref, *rest
):
    if first:
        na_ref, nat_ref, scratch = rest
        rows = x_ref[...].astype(F32)
        inv = lax.rsqrt(jnp.mean(rows * rows, -1, keepdims=True) + EPS)
        normed = (rows * inv * gain_ref[...]).astype(BF16)
        na_ref[...] = normed
    else:
        normed = x_ref[...]
    q = dot(normed, wq_ref[...])
    k = dot(normed, wk_ref[...])
    v = dot(normed, wv_ref[...])
    cos_v, sin_v = cos_ref[...], sin_ref[...]
    for start in range(0, q.shape[1], PAIR):
        cols = slice(start, start + PAIR)
        qp, kp = q[:, cols], k[:, cols]
        q_ref[:, cols] = ((qp * cos_v + swap_halves(qp) * sin_v) * HEAD**-0.5).astype(BF16)
        k_ref[:, cols] = (kp * cos_v + swap_halves(kp) * sin_v).astype(BF16)
    v_ref[...] = v.astype(BF16)
    if first:
        store_transposed(normed, scratch, nat_ref, me_ref, dp)


def qkv(first, dp, me, x, gain, weights, tables):
    count, width = x.shape
    cols = weights[0].shape[1]
    out_specs = [rows_of(cols)] * 3
    out_shape = [sds((count, cols), BF16)] * 3
    scratch = []
    if first:
        out_specs += [rows_of(width), pl.BlockSpec((width, ROWS), lambda i, *_: (0, i))]
        out_shape += [sds((count, width), BF16), sds((width, count), BF16)]
        scratch = [pltpu.VMEM((width, ROWS), BF16)]
    return pl.pallas_call(
        functools.partial(qkv_kernel, first, dp),
        grid_spec=pltpu.PrefetchScalarGridSpec(
            num_scalar_prefetch=1,
            grid=(count // ROWS,),
            in_specs=[rows_of(width), whole((1, width))]
            + [whole(weights[0].shape)] * 3
            + [rows_of(PAIR)] * 2,
            out_specs=out_specs,
            scratch_shapes=scratch,
        ),
        out_shape=out_shape,
        compiler_params=params(32),
        cost_estimate=cost(6 * count * width * cols, 4 * count * width + 6 * width * cols + 6 * count * cols),
        name="qkv_first" if first else "qkv_other",
    )(me, x, gain, *weights, *tables)


def attention_tasks(items):
    return [(i, h, q0, qb) for i in range(items) for q0, qb in BLOCKS for h in range(2)]


def pipelined(tasks, first, second, third):
    made, ready = {}, {}
    for step in range(len(tasks) + 2):
        if step < len(tasks):
            made[step] = first(tasks[step])
        if 0 <= step - 1 < len(tasks):
            ready[step - 1] = second(tasks[step - 1], made.pop(step - 1))
        if 0 <= step - 2 < len(tasks):
            third(tasks[step - 2], ready.pop(step - 2))


def causal(shape):
    key = lax.broadcasted_iota(jnp.int32, shape, 0)
    query = lax.broadcasted_iota(jnp.int32, shape, 1)
    return key <= query


def attention_kernel(items, q_ref, k_ref, v_ref, o_ref, lse_ref, acc):
    side = lax.broadcasted_iota(jnp.int32, (SLOTS, PAIR), 1) // HEAD
    v_t = {}

    def scores(task):
        i, h, q0, qb = task
        base = i * SLOTS
        q = jnp.where(side[:qb] == h, q_ref[base + q0 : base + q0 + qb, :], 0).astype(BF16)
        diag = dot_nt(k_ref[base + q0 : base + q0 + qb, :], q)
        return diag, (dot_nt(k_ref[base : base + q0, :], q) if q0 else None)

    def soften(task, made):
        i, h, q0, qb = task
        diag, past = made
        diag = jnp.where(causal(diag.shape), diag, NEG)
        top = jnp.max(diag, 0, keepdims=True)
        if q0:
            top = jnp.maximum(top, jnp.max(past, 0, keepdims=True))
        diag = jnp.exp(diag - top)
        total = jnp.sum(diag, 0, keepdims=True)
        if q0:
            past = jnp.exp(past - top)
            total = total + jnp.sum(past, 0, keepdims=True)
            past = past.astype(BF16)
        lse_ref[0, 2 * i + h : 2 * i + h + 1, q0 : q0 + qb] = top + jnp.log(total)
        return diag.astype(BF16), past, total

    def mix(task, made):
        i, h, q0, qb = task
        diag, past, total = made
        if i not in v_t:
            v_t[i] = v_ref[i * SLOTS : (i + 1) * SLOTS, :].T
        own = v_t[i][HEAD * h : HEAD * h + HEAD]
        out = dot(own[:, q0 : q0 + qb], diag)
        if q0:
            out = out + dot(own[:, :q0], past)
        acc[i, HEAD * h : HEAD * h + HEAD, q0 : q0 + qb] = out * (1.0 / total)

    pipelined(attention_tasks(items), scores, soften, mix)
    for i in range(items):
        o_ref[i * SLOTS : (i + 1) * SLOTS, :] = acc[i].T.astype(BF16)


def attention(q, k, v):
    count, cols = q.shape
    items, pairs = count // SLOTS, cols // PAIR
    block = pl.BlockSpec((count, PAIR), lambda p: (0, p))
    area = pairs * items * 2 * SLOTS * SLOTS
    return pl.pallas_call(
        functools.partial(attention_kernel, items),
        grid=(pairs,),
        in_specs=[block] * 3,
        out_specs=[block, pl.BlockSpec((1, 2 * items, SLOTS), lambda p: (p, 0, 0))],
        out_shape=[sds((count, cols), BF16), sds((pairs, 2 * items, SLOTS), F32)],
        scratch_shapes=[pltpu.VMEM((items, PAIR, SLOTS), F32)],
        compiler_params=params(40),
        cost_estimate=cost(8 * area * PAIR, 8 * count * cols, area),
        name="attention",
    )(q, k, v)


def attention_back_kernel(
    items, q_ref, k_ref, v_ref, d_ref, lse_ref, cos_ref, sin_ref, dq_ref, dk_ref, dv_ref, dq_t, dk_acc, dv_acc
):
    side = lax.broadcasted_iota(jnp.int32, (SLOTS, PAIR), 1) // HEAD
    k_t = {}

    def scores(task):
        i, h, q0, qb = task
        base, end = i * SLOTS, i * SLOTS + q0 + qb
        q = jnp.where(side[:qb] == h, q_ref[base + q0 : end, :], 0).astype(BF16)
        d = jnp.where(side[:qb] == h, d_ref[base + q0 : end, :], 0).astype(BF16)
        return q, d, dot_nt(k_ref[base:end, :], q), dot_nt(v_ref[base:end, :], d)

    def soften(task, made):
        i, h, q0, qb = task
        q, d, s, dp = made
        lse = lse_ref[0, 2 * i + h : 2 * i + h + 1, q0 : q0 + qb]
        p = jnp.exp(s[q0:] - lse)
        p = jnp.where(causal(p.shape), p, 0.0)
        if q0:
            p = jnp.concatenate([jnp.exp(s[:q0] - lse), p], 0)
        ds = (p * (dp - jnp.sum(p * dp, 0, keepdims=True))).astype(BF16)
        return q, d, p.astype(BF16), ds

    def mix(task, made):
        i, h, q0, qb = task
        q, d, p, ds = made
        end = q0 + qb
        if i not in k_t:
            k_t[i] = k_ref[i * SLOTS : (i + 1) * SLOTS, :].T
        dv, dk = dot(p, d), dot(ds, q)
        if end == SLOTS and h == 0:
            dv_acc[i] = dv
            dk_acc[i] = dk
        else:
            dv_acc[i, :end, :] += dv
            dk_acc[i, :end, :] += dk
        dq_t[i, HEAD * h : HEAD * h + HEAD, q0:end] = dot(k_t[i][HEAD * h : HEAD * h + HEAD, :end], ds)

    pipelined(attention_tasks(items), scores, soften, mix)
    cos_v, sin_v = cos_ref[...], sin_ref[...]
    for i in range(items):
        own = slice(i * SLOTS, (i + 1) * SLOTS)
        dq = dq_t[i].T * HEAD**-0.5
        dq_ref[own, :] = (dq * cos_v - swap_halves(dq) * sin_v).astype(BF16)
        dk = dk_acc[i]
        dk_ref[own, :] = (dk * cos_v - swap_halves(dk) * sin_v).astype(BF16)
        dv_ref[own, :] = dv_acc[i].astype(BF16)


def attention_back(q, k, v, d, lse, tables):
    count, cols = q.shape
    items, pairs = count // SLOTS, cols // PAIR
    block = pl.BlockSpec((count, PAIR), lambda p: (0, p))
    area = pairs * items * 2 * SLOTS * SLOTS
    return pl.pallas_call(
        functools.partial(attention_back_kernel, items),
        grid=(pairs,),
        in_specs=[block] * 4
        + [pl.BlockSpec((1, 2 * items, SLOTS), lambda p: (p, 0, 0))]
        + [whole((SLOTS, PAIR))] * 2,
        out_specs=[block] * 3,
        out_shape=[sds((count, cols), BF16)] * 3,
        scratch_shapes=[pltpu.VMEM((items, PAIR, SLOTS), F32)]
        + [pltpu.VMEM((items, SLOTS, PAIR), F32)] * 2,
        compiler_params=params(40),
        cost_estimate=cost(20 * area * PAIR, 14 * count * cols, area),
        name="attention_back",
    )(q, k, v, d, lse, *tables)


def row_is_valid(lens_ref, items):
    row = pl.program_id(0) * ROWS + lax.broadcasted_iota(jnp.int32, (ROWS, 1), 0)
    valid = row < 0
    for i in range(items):
        valid = valid | ((row >= i * SLOTS) & (row < i * SLOTS + lens_ref[i]))
    return valid


def middle_kernel(
    items, dp, me_ref, lens_ref, oa_ref, ob_ref, wa_ref, wb_ref, x_ref, cot_ref, gain_ref,
    h1_ref, nf_ref, nft_ref, eb_ref, ebt_ref, scratch
):
    branch = dot(oa_ref[...], wa_ref[...]) + dot(ob_ref[...], wb_ref[...])
    h1 = x_ref[...].astype(F32) + branch
    h1_ref[...] = h1
    inv = lax.rsqrt(jnp.mean(h1 * h1, -1, keepdims=True) + EPS)
    normed = (h1 * inv * gain_ref[...]).astype(BF16)
    nf_ref[...] = normed
    e = jnp.where(row_is_valid(lens_ref, items), cot_ref[...].astype(F32), 0.0).astype(BF16)
    eb_ref[...] = e
    store_transposed(normed, scratch, nft_ref, me_ref, dp)
    store_transposed(e, scratch, ebt_ref, me_ref, dp)


def middle(dp, me, lens, o, w_out, x, cot, gain):
    count, width = x.shape
    cols = w_out[0].shape[0]
    turned = pl.BlockSpec((width, ROWS), lambda i, *_: (0, i))
    return pl.pallas_call(
        functools.partial(middle_kernel, count // SLOTS, dp),
        grid_spec=pltpu.PrefetchScalarGridSpec(
            num_scalar_prefetch=2,
            grid=(count // ROWS,),
            in_specs=[rows_of(cols)] * 2
            + [whole(w_out[0].shape)] * 2
            + [rows_of(width)] * 2
            + [whole((1, width))],
            out_specs=[rows_of(width), rows_of(width), turned, rows_of(width), turned],
            scratch_shapes=[pltpu.VMEM((width, ROWS), BF16)],
        ),
        out_shape=[
            sds((count, width), F32),
            sds((count, width), BF16),
            sds((width, count), BF16),
            sds((count, width), BF16),
            sds((width, count), BF16),
        ],
        compiler_params=params(32),
        cost_estimate=cost(4 * count * width * cols, 18 * count * width),
        name="middle",
    )(me, lens, *o, *w_out, x, cot, gain)


def split_store(values, quarter, b0, b1, outs):
    send_a, keep_a, send_b, keep_b = outs
    cut = values.shape[1] // 2
    (send_a if b0 else keep_a)[b1] = values[:, :cut].astype(BF16)
    (send_b if b1 else keep_b)[b0] = values[:, cut:].astype(BF16)


def ffn_kernel(final, nf_ref, nft_ref, eb_ref, ebt_ref, wg_ref, wu_ref, wd_ref, *rest):
    if final:
        recv_ref, hid_ref, dg_ref, du_ref, *outs = rest
    else:
        hid_ref, dg_ref, du_ref, out_ref = rest
    count, width = nf_ref.shape
    block = 192
    wg, wu, wd = wg_ref[...], wu_ref[...], wd_ref[...]

    def products(start):
        own = slice(start, start + block)
        normed, e = nf_ref[own, :], eb_ref[own, :]
        return dot(normed, wg), dot(normed, wu), dot_nt(e, wd)

    def point(start, made):
        own = slice(start, start + block)
        g, u, dh = made
        sig = jax.nn.sigmoid(g)
        silu = g * sig
        hid_ref[own, :] = (silu * u).astype(BF16)
        du_ref[own, :] = (dh * silu).astype(BF16)
        dg_ref[own, :] = (dh * u * (sig + silu * (1.0 - sig))).astype(BF16)

    made = None
    for start in range(0, count + block, block):
        upcoming = products(start) if start < count else None
        if made is not None:
            point(start - block, made)
        made = upcoming

    hid, dg, du = hid_ref[...], dg_ref[...], du_ref[...]
    quarter = width // 4
    for place in range(4):
        own = slice(place * quarter, place * quarter + quarter)
        grads = [dot(nft_ref[own, :], dg), dot(nft_ref[own, :], du), dot(ebt_ref[own, :], hid)]
        values = jnp.concatenate(grads, 1)
        if final:
            values = values + recv_ref[own, :].astype(F32)
            split_store(values, quarter, place // 2, place % 2, outs)
        else:
            out_ref[own, :] = values.astype(BF16)


def ffn(nf, nft, eb, ebt, wg, wu, wd, first, chunks, recv=None):
    count, width = nf.shape
    final = recv is not None
    wide = 3 * CHUNK
    in_specs = [whole((count, width)), whole((width, count))] * 2 + [
        pl.BlockSpec((width, CHUNK), lambda c: (0, c + first)),
        pl.BlockSpec((width, CHUNK), lambda c: (0, c + first)),
        pl.BlockSpec((CHUNK, width), lambda c: (c + first, 0)),
    ]
    out_specs = [pl.BlockSpec((count, CHUNK), lambda c: (0, c))] * 3
    out_shape = [sds((count, CHUNK * chunks), BF16)] * 3
    args = [nf, nft, eb, ebt, wg, wu, wd]
    if final:
        in_specs.append(pl.BlockSpec((width, wide), lambda c: (0, c + first)))
        args.append(recv)
        out_specs += [pl.BlockSpec((2, width // 4, wide // 2), lambda c: (0, 0, c))] * 4
        out_shape += [sds((2, width // 4, wide // 2 * chunks), BF16)] * 4
    else:
        out_specs.append(pl.BlockSpec((width, wide), lambda c: (0, c)))
        out_shape.append(sds((width, wide * chunks), BF16))
    return pl.pallas_call(
        functools.partial(ffn_kernel, final),
        grid=(chunks,),
        in_specs=in_specs,
        out_specs=out_specs,
        out_shape=out_shape,
        compiler_params=params(56),
        cost_estimate=cost(12 * count * width * CHUNK * chunks, 8 * count * width + 12 * width * CHUNK * chunks),
        name="ffn_final" if final else "ffn_other",
    )(*args)


def ffn_back_kernel(
    dp, parts, me_ref, h1_ref, eb_ref, gain_ref, wg_refs, wu_refs, wo_refs, dg_refs, du_refs,
    dh1_ref, abt_ref, do_refs, dgain_ref, scratch
):
    dnf = None
    for which, ((side, start, size), dg_ref, du_ref) in enumerate(zip(parts, dg_refs, du_refs)):
        term = dot_nt(dg_ref[...], wg_refs[side][:, start : start + size])
        term = term + dot_nt(du_ref[...], wu_refs[side][:, start : start + size])
        dnf = term if dnf is None else dnf + term
    h1 = h1_ref[...]
    inv = lax.rsqrt(jnp.mean(h1 * h1, -1, keepdims=True) + EPS)
    unit = h1 * inv
    weighted = dnf * gain_ref[...]
    dh1 = eb_ref[...].astype(F32) + inv * (weighted - unit * jnp.mean(weighted * unit, -1, keepdims=True))
    dh1_ref[...] = dh1
    gain_part = jnp.sum(dnf * unit, 0, keepdims=True)

    @pl.when(pl.program_id(0) == 0)
    def _():
        dgain_ref[...] = gain_part

    @pl.when(pl.program_id(0) != 0)
    def _():
        dgain_ref[...] += gain_part

    rounded = dh1.astype(BF16)
    for do_ref, wo_ref in zip(do_refs, wo_refs):
        do_ref[...] = dot_nt(rounded, wo_ref[...]).astype(BF16)
    store_transposed(rounded, scratch, abt_ref, me_ref, dp)


def ffn_back(dp, me, h1, eb, gain, wg, wu, wo, parts, dg, du):
    count, width = h1.shape
    cols = wo[0].shape[0]
    turned = pl.BlockSpec((width, ROWS), lambda i, *_: (0, i))
    deep = sum(size for _, _, size in parts)
    return pl.pallas_call(
        functools.partial(ffn_back_kernel, dp, parts),
        grid_spec=pltpu.PrefetchScalarGridSpec(
            num_scalar_prefetch=1,
            grid=(count // ROWS,),
            in_specs=[
                rows_of(width),
                rows_of(width),
                whole((1, width)),
                [whole(w.shape) for w in wg],
                [whole(w.shape) for w in wu],
                [whole(w.shape) for w in wo],
                [rows_of(d.shape[1]) for d in dg],
                [rows_of(d.shape[1]) for d in du],
            ],
            out_specs=[rows_of(width), turned, [rows_of(cols)] * 2, whole((1, width))],
            scratch_shapes=[pltpu.VMEM((width, ROWS), BF16)],
        ),
        out_shape=[
            sds((count, width), F32),
            sds((width, count), BF16),
            [sds((count, cols), BF16)] * 2,
            sds((1, width), F32),
        ],
        compiler_params=params(48),
        cost_estimate=cost(4 * count * width * (deep + cols), 20 * count * width + 4 * count * deep),
        name="ffn_back",
    )(me, h1, eb, gain, list(wg), list(wu), list(wo), list(dg), list(du))


def weight_grad_kernel(final, turned_ref, right_refs, recv_refs, *out_refs):
    width = turned_ref.shape[0]
    quarter = width // 4
    right = jnp.concatenate([r[...] for r in right_refs], 1) if len(right_refs) > 1 else right_refs[0][...]
    for place in range(4):
        own = slice(place * quarter, place * quarter + quarter)
        values = dot(turned_ref[own, :], right)
        if final:
            values = values + recv_refs[0][own, :].astype(F32)
            split_store(values, quarter, place // 2, place % 2, out_refs)
        else:
            out_refs[0][own, :] = values.astype(BF16)


def weight_grad(turned, right, recv=None):
    width, count = turned.shape
    cols = sum(r.shape[1] for r in right)
    final = recv is not None
    if final:
        out_shape = [sds((2, width // 4, cols // 2), BF16)] * 4
        recv = [recv]
    else:
        out_shape = [sds((width, cols), BF16)]
        recv = []
    return pl.pallas_call(
        functools.partial(weight_grad_kernel, final),
        out_shape=out_shape,
        compiler_params=params(48),
        cost_estimate=cost(2 * width * count * cols, 2 * count * (width + cols) + 4 * width * cols),
        name="weight_grad_final" if final else "weight_grad_other",
    )(turned, list(right), recv)


def attn_in_back_kernel(x_ref, dh1_ref, gain_ref, w_refs, d_refs, gin_ref, dgain_ref):
    dna = None
    for d_ref, w_ref in zip(d_refs, w_refs):
        term = dot_nt(d_ref[...], w_ref[...])
        dna = term if dna is None else dna + term
    rows = x_ref[...].astype(F32)
    inv = lax.rsqrt(jnp.mean(rows * rows, -1, keepdims=True) + EPS)
    unit = rows * inv
    weighted = dna * gain_ref[...]
    gin_ref[...] = dh1_ref[...] + inv * (weighted - unit * jnp.mean(weighted * unit, -1, keepdims=True))
    gain_part = jnp.sum(dna * unit, 0, keepdims=True)

    @pl.when(pl.program_id(0) == 0)
    def _():
        dgain_ref[...] = gain_part

    @pl.when(pl.program_id(0) != 0)
    def _():
        dgain_ref[...] += gain_part


def attn_in_back(x, dh1, gain, weights, grads):
    count, width = x.shape
    cols = weights[0].shape[1]
    return pl.pallas_call(
        attn_in_back_kernel,
        grid=(count // ROWS,),
        in_specs=[
            rows_of(width),
            rows_of(width),
            whole((1, width)),
            [whole(w.shape) for w in weights],
            [rows_of(cols)] * len(grads),
        ],
        out_specs=[rows_of(width), whole((1, width))],
        out_shape=[sds((count, width), F32), sds((1, width), F32)],
        compiler_params=params(32),
        cost_estimate=cost(2 * count * width * cols * len(grads), 10 * count * width + 2 * count * cols * len(grads)),
        name="attn_in_back",
    )(x, dh1, gain, list(weights), list(grads))


def output_kernel(items, parts, lens_ref, h1_ref, wd_refs, hid_refs, out_ref):
    total = h1_ref[...]
    for (side, start, size), hid_ref in zip(parts, hid_refs):
        total = total + dot(hid_ref[...], wd_refs[side][start : start + size, :])
    out_ref[...] = jnp.where(row_is_valid(lens_ref, items), total, 0.0).astype(BF16)


def layer_output(lens, h1, wd, parts, hid):
    count, width = h1.shape
    deep = sum(size for _, _, size in parts)
    return pl.pallas_call(
        functools.partial(output_kernel, count // SLOTS, parts),
        grid_spec=pltpu.PrefetchScalarGridSpec(
            num_scalar_prefetch=1,
            grid=(count // ROWS,),
            in_specs=[rows_of(width), [whole(w.shape) for w in wd], [rows_of(h.shape[1]) for h in hid]],
            out_specs=rows_of(width),
        ),
        out_shape=sds((count, width), BF16),
        compiler_params=params(40),
        cost_estimate=cost(2 * count * width * deep, 6 * count * width + 2 * count * deep),
        name="layer_output",
    )(lens, h1, list(wd), list(hid))


def second_kernel(keep_a, recv_a, keep_b, recv_b, send_a, send_b):
    send_a[...] = (keep_a[1].astype(F32) + recv_a[1].astype(F32)).astype(BF16)
    send_b[...] = (keep_b[1].astype(F32) + recv_b[1].astype(F32)).astype(BF16)


def third_kernel(keep_a, recv_a, last_a, keep_b, recv_b, last_b, keep_ref, send_refs):
    group, cut = keep_ref.shape[0], keep_a.shape[2]
    for z in range(len(send_refs) + 1):
        own = slice(z * group, z * group + group)
        for cols, keep, recv, last in (
            (slice(0, cut), keep_a, recv_a, last_a),
            (slice(cut, 2 * cut), keep_b, recv_b, last_b),
        ):
            total = keep[0, own, :].astype(F32) + recv[0, own, :].astype(F32) + last[own, :].astype(F32)
            if z:
                send_refs[z - 1][:, cols] = total.astype(BF16)
            else:
                keep_ref[:, cols] = total


def reduce_over_dp(pieces, dp):
    send_a, keep_a, send_b, keep_b = pieces

    def swap(array, relative):
        return lax.ppermute(array, "dp", [(i, i ^ relative) for i in range(dp)])

    _, quarter, cut = send_a.shape
    recv_a, recv_b = swap(send_a, 1), swap(send_b, 2)
    next_a, next_b = pl.pallas_call(
        second_kernel,
        out_shape=[sds((quarter, cut), BF16)] * 2,
        compiler_params=params(24),
        cost_estimate=cost(quarter * cut * 2, quarter * cut * 12),
        name="second_sum",
    )(keep_a, recv_a, keep_b, recv_b)
    last_a, last_b = swap(next_a, 2), swap(next_b, 1)
    far = dp // 4
    group = quarter // far
    kept, sends = pl.pallas_call(
        third_kernel,
        out_shape=[sds((group, 2 * cut), F32), [sds((group, 2 * cut), BF16)] * (far - 1)],
        compiler_params=params(24),
        cost_estimate=cost(quarter * cut * 4, quarter * cut * 16),
        name="third_sum",
    )(keep_a, recv_a, last_a, keep_b, recv_b, last_b)
    total = kept
    for z, send in enumerate(sends):
        total = total + swap(send, 4 * (z + 1)).astype(F32)
    return total


def sum_everywhere(values, dp, mp):
    for axis, size in (("mp", mp), ("dp", dp)):
        bit = 1
        while bit < size:
            values = values + lax.ppermute(values, axis, [(i, i ^ bit) for i in range(size)])
            bit *= 2
    return values


def local(
    dp, mp, tokens, lengths, gain_attn, w_query, w_key, w_value, w_out, gain_ffn, w_gate, w_up, w_down, cotangent
):
    count, width = tokens.shape
    items = count // SLOTS
    me = lax.axis_index("dp").astype(jnp.int32)[None]
    lens = lax.dynamic_slice(lengths, (lax.axis_index("mp") * items,), (items,))
    gain_a, gain_f = gain_attn[None, :], gain_ffn[None, :]

    def other(array):
        return lax.ppermute(array, "mp", [(0, 1), (1, 0)])

    wq, wk, wv, wo, wg, wu, wd = (
        (w, other(w)) for w in (w_query, w_key, w_value, w_out, w_gate, w_up, w_down)
    )
    tables = tuple(jnp.asarray(t) for t in position_tables(count))

    q0, k0, v0, na, nat = qkv(True, dp, me, tokens, gain_a, (wq[0], wk[0], wv[0]), tables)
    q1, k1, v1 = qkv(False, dp, me, na, gain_a, (wq[1], wk[1], wv[1]), tables)
    nat = finish_transposed(nat, me, dp)
    o0, lse0 = attention(q0, k0, v0)
    o1, lse1 = attention(q1, k1, v1)
    h1, nf, nft, eb, ebt = middle(dp, me, lens, (o0, o1), wo, tokens, cotangent, gain_f)
    nft, ebt = finish_transposed(nft, me, dp), finish_transposed(ebt, me, dp)

    half = w_gate.shape[1]
    chunks = half // CHUNK
    hid, dg, du, parts, ffn_pieces = [], [], [], [], []
    h, g, u, there = ffn(nf, nft, eb, ebt, wg[1], wu[1], wd[1], 0, chunks)
    hid.append(h), dg.append(g), du.append(u), parts.append((1, 0, half))
    back = other(there)
    for c in range(chunks):
        h, g, u, *pieces = ffn(nf, nft, eb, ebt, wg[0], wu[0], wd[0], c, 1, back)
        hid.append(h), dg.append(g), du.append(u), parts.append((0, c * CHUNK, CHUNK))
        ffn_pieces.append(reduce_over_dp(pieces, dp))

    dh1, abt, (do0, do1), dgain_f = ffn_back(dp, me, h1, eb, gain_f, wg, wu, wo, tuple(parts), dg, du)
    abt = finish_transposed(abt, me, dp)
    out_there = weight_grad(abt, (o1,))[0]
    back_out = other(out_there)
    d1 = attention_back(q1, k1, v1, do1, lse1, tables)
    qkv_there = weight_grad(nat, d1)[0]
    back_qkv = other(qkv_there)
    out_piece = reduce_over_dp(weight_grad(abt, (o0,), back_out), dp)
    d0 = attention_back(q0, k0, v0, do0, lse0, tables)
    qkv_piece = reduce_over_dp(weight_grad(nat, d0, back_qkv), dp)
    grad_input, dgain_a = attn_in_back(
        tokens, dh1, gain_a, (wq[0], wk[0], wv[0], wq[1], wk[1], wv[1]), (*d0, *d1)
    )
    output = layer_output(lens, h1, wd, tuple(parts), hid)
    gains = sum_everywhere(jnp.concatenate([dgain_a, dgain_f], 0), dp, mp)

    cols = w_query.shape[1]
    gq, gk, gv = (qkv_piece[:, i * cols : (i + 1) * cols] for i in range(3))
    g_gate, g_up, g_down = (
        jnp.concatenate([p[:, i * CHUNK : (i + 1) * CHUNK] for p in ffn_pieces], 1) for i in range(3)
    )
    return (
        output, grad_input, gains[0], gq, gk, gv, out_piece.T, gains[1], g_gate, g_up, g_down.T,
    )


def solution(mesh):
    in_specs = (
        P(("dp", "mp"), None),
        P("dp"),
        P(),
        P(None, "mp"),
        P(None, "mp"),
        P(None, "mp"),
        P("mp", None),
        P(),
        P(None, "mp"),
        P(None, "mp"),
        P("mp", None),
        P(("dp", "mp"), None),
    )
    out_specs = (
        P(("dp", "mp"), None),
        P(("dp", "mp"), None),
        P(),
        P("dp", "mp"),
        P("dp", "mp"),
        P("dp", "mp"),
        P("mp", "dp"),
        P(),
        P("dp", "mp"),
        P("dp", "mp"),
        P("mp", "dp"),
    )
    body = functools.partial(local, mesh.shape["dp"], mesh.shape["mp"])
    return jax.shard_map(body, mesh=mesh, in_specs=in_specs, out_specs=out_specs, check_vma=False)
```

```python
import functools

import jax
import jax.numpy as jnp
import numpy as np
from jax import lax
from jax.experimental import pallas as pl
from jax.experimental.pallas import tpu as pltpu
from jax.sharding import PartitionSpec as P

HEAD = 64
PAIR = 2 * HEAD
SLOTS = 576
EPS = 1e-05
THETA = 10000.0
ROWS = 384
CHUNK = 512
F32 = jnp.float32
BF16 = jnp.bfloat16
NEG = -1e30
BLOCKS = ((512, 64), (256, 256), (0, 256))
MIB = 1 << 20


def hbm(shape, dtype):
    return pltpu.HBM(shape, dtype)


def vmem(shape, dtype):
    return pltpu.VMEM(shape, dtype)


def on_chip(tree):
    return jax.tree.map(lambda a: pltpu.with_memory_space_constraint(a, pltpu.VMEM), tree)


def off_chip(tree):
    return jax.tree.map(lambda a: pltpu.with_memory_space_constraint(a, pltpu.HBM), tree)


def copy(source, target, sem):
    made = pltpu.make_async_copy(source, target, sem)
    made.start()
    return made


ANY = pl.BlockSpec(memory_space=pl.ANY)
CHIP = pl.BlockSpec(memory_space=pltpu.VMEM)
SCALAR = pl.BlockSpec(memory_space=pltpu.SMEM)


def dot(left, right):
    return jnp.dot(left, right, preferred_element_type=F32)


def dot_nt(left, right):
    return lax.dot_general(left, right, (((1,), (1,)), ((), ())), preferred_element_type=F32)


def params(mib):
    return pltpu.CompilerParams(vmem_limit_bytes=mib * MIB)


def cost(flops, moved, special=0):
    return pl.CostEstimate(flops=int(flops), bytes_accessed=int(moved), transcendentals=int(special))


def sds(shape, dtype):
    return jax.ShapeDtypeStruct(shape, dtype)


def position_tables(row_count):
    inv_freq = np.float32(THETA) ** (
        -(np.float32(2.0) * np.arange(HEAD // 2, dtype=np.float32)) / np.float32(HEAD)
    )
    places = (np.arange(row_count) % SLOTS).astype(np.float32)
    angles = (places[:, None] * inv_freq[None, :].astype(np.float32)).astype(np.float32)
    cosine, sine = np.cos(angles), np.sin(angles)
    cos_t = np.tile(cosine, (1, PAIR // cosine.shape[1]))
    sin_t = np.tile(np.concatenate([-sine, sine], 1), (1, 2))
    return cos_t.astype(np.float32), sin_t.astype(np.float32)


def swap_halves(values):
    lane = lax.broadcasted_iota(jnp.int32, values.shape, 1)
    return jnp.where(
        lane % HEAD < HEAD // 2,
        pltpu.roll(values, PAIR - HEAD // 2, 1),
        pltpu.roll(values, HEAD // 2, 1),
    )


def relative_order(dp):
    return [b0 + 2 * b1 + 4 * z for b0 in range(2) for b1 in range(2) for z in range(dp // 4)]


def store_transposed(value, scratch, out_ref, me_ref, dp):
    width = value.shape[1]
    group = width // dp
    if group % 16:
        out_ref[...] = value.T
        return
    scratch[...] = value.T
    for place, relative in enumerate(relative_order(dp)):
        start = pl.multiple_of(group * jnp.bitwise_xor(me_ref[0], relative), 16)
        out_ref[group * place : group * place + group, :] = scratch[pl.ds(start, group), :]


def finish_transposed(array, me, dp):
    group = array.shape[0] // dp
    if group % 16 == 0:
        return array
    index = jnp.bitwise_xor(me[0], jnp.asarray(relative_order(dp), jnp.int32))
    return jnp.take(array.reshape(dp, group, -1), index, axis=0).reshape(array.shape)


class Copies:
    def __init__(self, sems):
        self.sems, self.made = sems, []

    def start(self, source, target):
        self.made.append(copy(source, target, self.sems.at[len(self.made)]))
        return self.made[-1]

    def wait(self):
        for c in self.made:
            c.wait()


def row_blocks(count):
    return [slice(start, start + ROWS) for start in range(0, count, ROWS)]


def prepare_kernel(
    items, dp, me_ref, lens_ref, gain_ref, x_hbm, cot_hbm, na_ref, nat_ref, eb_ref, ebt_ref, x, cot, turn, sems
):
    arrive = Copies(sems)
    blocks = row_blocks(x.shape[0])
    inputs = [
        (arrive.start(x_hbm.at[own, :], x.at[own, :]), arrive.start(cot_hbm.at[own, :], cot.at[own, :]))
        for own in blocks
    ]
    for own, (x_in, cot_in) in zip(blocks, inputs):
        x_in.wait()
        rows = x[own, :].astype(F32)
        inv = lax.rsqrt(jnp.mean(rows * rows, -1, keepdims=True) + EPS)
        normed = (rows * inv * gain_ref[...][None, :]).astype(BF16)
        na_ref[own, :] = normed
        store_transposed(normed, turn.at[0], nat_ref.at[:, own], me_ref, dp)
        cot_in.wait()
        valid = row_is_valid(me_ref, lens_ref, items, own.start)
        e = jnp.where(valid, cot[own, :].astype(F32), 0.0).astype(BF16)
        eb_ref[own, :] = e
        store_transposed(e, turn.at[1], ebt_ref.at[:, own], me_ref, dp)


def prepare(dp, me, lens, x, cot, gain):
    count, width = x.shape
    return pl.pallas_call(
        functools.partial(prepare_kernel, count // SLOTS, dp),
        in_specs=[SCALAR, SCALAR, CHIP, ANY, ANY],
        out_specs=[CHIP] * 4,
        out_shape=[vmem((count, width), BF16), vmem((width, count), BF16)] * 2,
        scratch_shapes=[
            pltpu.VMEM((count, width), BF16),
            pltpu.VMEM((count, width), BF16),
            pltpu.VMEM((2, width, ROWS), BF16),
            pltpu.SemaphoreType.DMA((2 * (count // ROWS),)),
        ],
        compiler_params=params(24),
        cost_estimate=cost(10 * count * width, 12 * count * width),
        name="prepare",
    )(me, lens, on_chip(gain), *off_chip((x, cot)))


def attention_tasks(items):
    return [(i, h, q0, qb) for i in range(items) for q0, qb in BLOCKS for h in range(2)]


def pipelined(tasks, first, second, third):
    made, ready = {}, {}
    for step in range(len(tasks) + 2):
        if step < len(tasks):
            made[step] = first(tasks[step])
        if 0 <= step - 1 < len(tasks):
            ready[step - 1] = second(tasks[step - 1], made.pop(step - 1))
        if 0 <= step - 2 < len(tasks):
            third(tasks[step - 2], ready.pop(step - 2))


def causal(shape):
    key = lax.broadcasted_iota(jnp.int32, shape, 0)
    query = lax.broadcasted_iota(jnp.int32, shape, 1)
    return key <= query


def attend(items, q_ref, k_ref, v_ref, own_cols, o_ref, lse_ref, pair, acc):
    side = lax.broadcasted_iota(jnp.int32, (SLOTS, PAIR), 1) // HEAD
    v_t = {}

    def scores(task):
        i, h, q0, qb = task
        base = i * SLOTS
        q = jnp.where(side[:qb] == h, q_ref[base + q0 : base + q0 + qb, own_cols], 0).astype(BF16)
        diag = dot_nt(k_ref[base + q0 : base + q0 + qb, own_cols], q)
        return diag, (dot_nt(k_ref[base : base + q0, own_cols], q) if q0 else None)

    def soften(task, made):
        i, h, q0, qb = task
        diag, past = made
        diag = jnp.where(causal(diag.shape), diag, NEG)
        top = jnp.max(diag, 0, keepdims=True)
        if q0:
            top = jnp.maximum(top, jnp.max(past, 0, keepdims=True))
        diag = jnp.exp(diag - top)
        total = jnp.sum(diag, 0, keepdims=True)
        if q0:
            past = jnp.exp(past - top)
            total = total + jnp.sum(past, 0, keepdims=True)
            past = past.astype(BF16)
        lse_ref[pair, 2 * i + h : 2 * i + h + 1, q0 : q0 + qb] = top + jnp.log(total)
        return diag.astype(BF16), past, total

    def mix(task, made):
        i, h, q0, qb = task
        diag, past, total = made
        if i not in v_t:
            v_t[i] = v_ref[i * SLOTS : (i + 1) * SLOTS, own_cols].T
        own = v_t[i][HEAD * h : HEAD * h + HEAD]
        out = dot(own[:, q0 : q0 + qb], diag)
        if q0:
            out = out + dot(own[:, :q0], past)
        acc[i, HEAD * h : HEAD * h + HEAD, q0 : q0 + qb] = out * (1.0 / total)

    pipelined(attention_tasks(items), scores, soften, mix)
    for i in range(items):
        o_ref[i * SLOTS : (i + 1) * SLOTS, own_cols] = acc[i].T.astype(BF16)


def front_kernel(
    dp, me_ref, gain_ref, na_ref, cos_hbm, sin_hbm, w_hbm, wo_hbm, x_hbm,
    q_hbm, k_hbm, v_hbm, h1_hbm, o_ref, lse_ref, nf_ref, nft_ref,
    q_ref, k_ref, v_ref, h1_ref, acc, weights, wo, x, cosine, sine, turn, sems, out_sems,
):
    arrive = Copies(sems)
    leaving = ((q_ref, q_hbm), (k_ref, k_hbm), (v_ref, v_hbm))
    count, width = na_ref.shape
    items, cols = count // SLOTS, wo_hbm[0].shape[0]
    half = cols // PAIR
    early = [arrive.start(cos_hbm, cosine), arrive.start(sin_hbm, sine)]
    for p in range(2 * half):
        for j in range(3):
            source = w_hbm[p // half][j].at[:, (p % half) * PAIR : (p % half + 1) * PAIR]
            early.append(arrive.start(source, weights.at[:, (3 * p + j) * PAIR : (3 * p + j + 1) * PAIR]))
    late = [arrive.start(w, wo.at[i * cols : (i + 1) * cols, :]) for i, w in enumerate(wo_hbm)]
    late.append(arrive.start(x_hbm, x))
    for c in early:
        c.wait()

    @pl.loop(0, 2 * half)
    def _(pair):
        own_cols = pl.ds(pl.multiple_of(pair * PAIR, PAIR), PAIR)
        own_weights = weights[:, pl.ds(pl.multiple_of(pair * 3 * PAIR, PAIR), 3 * PAIR)]
        for own in row_blocks(count):
            qkv = dot(na_ref[own, :], own_weights)
            cos_v, sin_v = cosine[own, :], sine[own, :]
            q, k = qkv[:, :PAIR], qkv[:, PAIR : 2 * PAIR]
            q_ref[own, own_cols] = ((q * cos_v + swap_halves(q) * sin_v) * HEAD**-0.5).astype(BF16)
            k_ref[own, own_cols] = (k * cos_v + swap_halves(k) * sin_v).astype(BF16)
            v_ref[own, own_cols] = qkv[:, 2 * PAIR :].astype(BF16)
        for j, (source, target) in enumerate(leaving):
            copy(source.at[:, own_cols], target.at[:, own_cols], out_sems.at[3 * pair + j])
        attend(items, q_ref, k_ref, v_ref, own_cols, o_ref, lse_ref, pair, acc)

    for c in late:
        c.wait()
    blocks = row_blocks(count)
    branch = dot(o_ref[blocks[0], :], wo[...])
    for i, own in enumerate(blocks):
        upcoming = dot(o_ref[blocks[i + 1], :], wo[...]) if i + 1 < len(blocks) else None
        rows = x[own, :].astype(F32) + branch
        h1_ref[own, :] = rows
        inv = lax.rsqrt(jnp.mean(rows * rows, -1, keepdims=True) + EPS)
        normed = (rows * inv * gain_ref[...][None, :]).astype(BF16)
        nf_ref[own, :] = normed
        store_transposed(normed, turn, nft_ref.at[:, own], me_ref, dp)
        branch = upcoming
        copy(h1_ref.at[own, :], h1_hbm.at[own, :], out_sems.at[6 * half + i])
    for p in range(2 * half):
        own_cols = slice(p * PAIR, (p + 1) * PAIR)
        for j, (source, target) in enumerate(leaving):
            pltpu.make_async_copy(source.at[:, own_cols], target.at[:, own_cols], out_sems.at[3 * p + j]).wait()
    for i, own in enumerate(blocks):
        pltpu.make_async_copy(h1_ref.at[own, :], h1_hbm.at[own, :], out_sems.at[6 * half + i]).wait()


def front(dp, me, na, tables, gain, w, wo, x):
    count, width = na.shape
    items, cols = count // SLOTS, wo[0].shape[0]
    half = cols // PAIR
    area = 2 * half * items * 2 * SLOTS * SLOTS
    return pl.pallas_call(
        functools.partial(front_kernel, dp),
        in_specs=[SCALAR, CHIP, CHIP, ANY, ANY, [[ANY] * 3] * 2, [ANY] * 2, ANY],
        out_specs=[ANY] * 4 + [CHIP] * 4,
        out_shape=[hbm((count, width), BF16)] * 3
        + [
            hbm((count, width), F32), vmem((count, width), BF16),
            vmem((2 * half, 2 * items, SLOTS), F32),
            vmem((count, width), BF16), vmem((width, count), BF16),
        ],
        scratch_shapes=[pltpu.VMEM((count, width), BF16)] * 3
        + [
            pltpu.VMEM((count, width), F32),
            pltpu.VMEM((items, PAIR, SLOTS), F32),
            pltpu.VMEM((width, 6 * cols), BF16),
            pltpu.VMEM((2 * cols, width), BF16),
            pltpu.VMEM((count, width), BF16),
            pltpu.VMEM((count, PAIR), F32),
            pltpu.VMEM((count, PAIR), F32),
            pltpu.VMEM((width, ROWS), BF16),
            pltpu.SemaphoreType.DMA((6 * half + 8,)),
            pltpu.SemaphoreType.DMA((6 * half + count // ROWS,)),
        ],
        compiler_params=params(34),
        cost_estimate=cost(8 * count * width * width + 8 * area * PAIR, 24 * count * width, area),
        name="front",
    )(me, *on_chip((gain, na)), *off_chip(tables), [list(off_chip(w[0])), list(w[1])], [off_chip(wo[0]), wo[1]], off_chip(x))


def attention_back_kernel(
    final, first, d_ref, lse_ref, nat_ref, cos_hbm, sin_hbm, q_hbm, k_hbm, v_hbm, *rest
):
    q_ref, k_ref, v_ref, dq_t, dk_acc, dv_acc, cosine, sine, right, sems, row_sems = rest[-11:]
    if final:
        recv_ref, dq_ref, dk_ref, dv_ref, *outs = rest[:-11]
    else:
        dq_ref, dk_ref, dv_ref, out_ref = rest[:-11]
    count, cols = dq_ref.shape
    items = count // SLOTS
    arrive = Copies(sems)
    arrive.start(cos_hbm.at[:SLOTS, :], cosine)
    arrive.start(sin_hbm.at[:SLOTS, :], sine)
    arriving = ((q_hbm, q_ref), (k_hbm, k_ref), (v_hbm, v_ref))
    for p in range(cols // PAIR):
        source_cols = slice((p + first) * PAIR, (p + first + 1) * PAIR)
        for j, (source, target) in enumerate(arriving):
            copy(source.at[:, source_cols], target.at[:, p * PAIR : (p + 1) * PAIR], row_sems.at[3 * p + j])
    arrive.wait()
    side = lax.broadcasted_iota(jnp.int32, (SLOTS, PAIR), 1) // HEAD
    quarter = nat_ref.shape[0] // 4

    @pl.loop(0, cols // PAIR)
    def _(pair):
        own_cols = pl.ds(pl.multiple_of(pair * PAIR, PAIR), PAIR)
        from_cols = pl.ds(pl.multiple_of((pair + first) * PAIR, PAIR), PAIR)
        for j, (source, target) in enumerate(arriving):
            pltpu.make_async_copy(source.at[:, from_cols], target.at[:, own_cols], row_sems.at[3 * pair + j]).wait()
        k_t = {}

        def scores(task):
            i, h, q0, qb = task
            base, end = i * SLOTS, i * SLOTS + q0 + qb
            q = jnp.where(side[:qb] == h, q_ref[base + q0 : end, own_cols], 0).astype(BF16)
            d = jnp.where(side[:qb] == h, d_ref[base + q0 : end, from_cols], 0).astype(BF16)
            return q, d, dot_nt(k_ref[base:end, own_cols], q), dot_nt(v_ref[base:end, own_cols], d)

        def soften(task, made):
            i, h, q0, qb = task
            q, d, s, dp = made
            lse = lse_ref[pair + first, 2 * i + h : 2 * i + h + 1, q0 : q0 + qb]
            p = jnp.exp(s[q0:] - lse)
            p = jnp.where(causal(p.shape), p, 0.0)
            if q0:
                p = jnp.concatenate([jnp.exp(s[:q0] - lse), p], 0)
            ds = (p * (dp - jnp.sum(p * dp, 0, keepdims=True))).astype(BF16)
            return q, d, p.astype(BF16), ds

        def mix(task, made):
            i, h, q0, qb = task
            q, d, p, ds = made
            end = q0 + qb
            if i not in k_t:
                k_t[i] = k_ref[i * SLOTS : (i + 1) * SLOTS, own_cols].T
            dv, dk = dot(p, d), dot(ds, q)
            if end == SLOTS and h == 0:
                dv_acc[i] = dv
                dk_acc[i] = dk
            else:
                dv_acc[i, :end, :] += dv
                dk_acc[i, :end, :] += dk
            dq_t[i, HEAD * h : HEAD * h + HEAD, q0:end] = dot(k_t[i][HEAD * h : HEAD * h + HEAD, :end], ds)

        pipelined(attention_tasks(items), scores, soften, mix)
        cos_v, sin_v = cosine[...], sine[...]
        for i in range(items):
            own = slice(i * SLOTS, (i + 1) * SLOTS)
            dq = dq_t[i].T * HEAD**-0.5
            dq = (dq * cos_v - swap_halves(dq) * sin_v).astype(BF16)
            dk = dk_acc[i]
            dk = (dk * cos_v - swap_halves(dk) * sin_v).astype(BF16)
            dv = dv_acc[i].astype(BF16)
            for j, (ref, value) in enumerate(((dq_ref, dq), (dk_ref, dk), (dv_ref, dv))):
                ref[own, own_cols] = value
                right[own, j * PAIR : (j + 1) * PAIR] = value
        wide = pl.ds(pl.multiple_of(pair * 3 * PAIR, PAIR), 3 * PAIR)
        for place in range(4):
            own = slice(place * quarter, place * quarter + quarter)
            values = dot(nat_ref[own, :], right[...])
            if final:
                outs[place][:, wide] = (values + recv_ref[own, wide].astype(F32)).astype(BF16)
            else:
                out_ref[own, wide] = values.astype(BF16)


def attention_back(q, k, v, d, lse, tables, nat, first, recv=None):
    count, width = q.shape
    cols = width // 2
    items, pairs = count // SLOTS, cols // PAIR
    area = pairs * items * 2 * SLOTS * SLOTS
    final = recv is not None
    args = [*on_chip((d, lse, nat)), *off_chip((*tables, q, k, v))]
    out_shape = [vmem((count, cols), BF16)] * 3
    if final:
        args.append(on_chip(recv))
        out_shape += [vmem((width // 4, 3 * cols), BF16)] * 4
    else:
        out_shape.append(vmem((width, 3 * cols), BF16))
    return pl.pallas_call(
        functools.partial(attention_back_kernel, final, first),
        in_specs=[CHIP] * 3 + [ANY] * 5 + [CHIP] * (len(args) - 8),
        out_specs=[CHIP] * len(out_shape),
        out_shape=out_shape,
        scratch_shapes=[pltpu.VMEM((count, cols), BF16)] * 3
        + [pltpu.VMEM((items, PAIR, SLOTS), F32)]
        + [pltpu.VMEM((items, SLOTS, PAIR), F32)] * 2
        + [pltpu.VMEM((SLOTS, PAIR), F32)] * 2
        + [pltpu.VMEM((count, 3 * PAIR), BF16), pltpu.SemaphoreType.DMA((2,)), pltpu.SemaphoreType.DMA((3 * pairs,))],
        compiler_params=params(28),
        cost_estimate=cost(20 * area * PAIR + 6 * count * width * cols, 16 * count * cols, area),
        name="attention_back_final" if final else "attention_back_other",
    )(*args)


def row_is_valid(me_ref, lens_ref, items, start):
    row = start + lax.broadcasted_iota(jnp.int32, (ROWS, 1), 0)
    valid = row < 0
    for i in range(items):
        valid = valid | ((row >= i * SLOTS) & (row < i * SLOTS + lens_ref[me_ref[1] * items + i]))
    return valid


def split_store(values, cols, total, b0, b1, outs):
    send_a, keep_a, send_b, keep_b = outs
    cut = total // 2
    if cols.start < cut:
        part = values[:, : min(cols.stop, cut) - cols.start].astype(BF16)
        (send_a if b0 else keep_a)[b1, :, cols.start : min(cols.stop, cut)] = part
    if cols.stop > cut:
        start = max(cols.start, cut)
        part = values[:, start - cols.start :].astype(BF16)
        (send_b if b1 else keep_b)[b0, :, start - cut : cols.stop - cut] = part


def ffn_kernel(final, column, blocks, nf_ref, nft_ref, eb_ref, ebt_ref, wg_hbm, wu_hbm, wd_hbm, *rest):
    wg, wu, wd, hid, in_sems, out_sems = rest[-6:]
    if final:
        recv_ref, hid_hbm, dg_ref, du_ref, *outs = rest[:-6]
    else:
        hid_hbm, dg_ref, du_ref, out_ref = rest[:-6]
    width = nft_ref.shape[0]
    chunk = pl.ds(column, CHUNK)
    arrive, sent = Copies(in_sems), Copies(out_sems)
    waits = [
        arrive.start(wg_hbm.at[:, chunk], wg),
        arrive.start(wu_hbm.at[:, chunk], wu),
        arrive.start(wd_hbm.at[chunk, :], wd),
    ]

    def products(own):
        made = []
        for ref, weight, multiply in ((nf_ref, wg, dot), (nf_ref, wu, dot), (eb_ref, wd, dot_nt)):
            if waits:
                waits.pop(0).wait()
            made.append(multiply(ref[own, :], weight[...]))
        return made

    def point(own, made):
        g, u, dh = made
        sig = 0.5 * jnp.tanh(0.5 * g) + 0.5
        silu = g * sig
        hid[own, :] = (silu * u).astype(BF16)
        sent.start(hid.at[own, :], hid_hbm.at[own, :])
        du_ref[own, :] = (dh * silu).astype(BF16)
        dg_ref[own, :] = (dh * u * (sig + silu * (1.0 - sig))).astype(BF16)

    made = None
    for i in range(len(blocks) + 1):
        upcoming = products(blocks[i]) if i < len(blocks) else None
        if made is not None:
            point(blocks[i - 1], made)
        made = upcoming
    quarter = width // 4
    for place in range(4):
        own = slice(place * quarter, place * quarter + quarter)
        grads = [dot(nft_ref[own, :], dg_ref[...]), dot(nft_ref[own, :], du_ref[...]), dot(ebt_ref[own, :], hid[...])]
        for j, values in enumerate(grads):
            cols = slice(j * CHUNK, (j + 1) * CHUNK)
            if final:
                split_store(values + recv_ref[own, cols].astype(F32), cols, 3 * CHUNK, place // 2, place % 2, outs)
            else:
                out_ref[own, cols] = values.astype(BF16)
    sent.wait()


def ffn(nf, nft, eb, ebt, wg, wu, wd, chunk, recv=None, spare=0):
    count, width = nf.shape
    final = recv is not None
    wide = 3 * CHUNK
    sizes = [512 * count // 1152, 384 * count // 1152]
    edges = [0, sizes[0], sum(sizes), count]
    blocks = [slice(i, j) for i, j in zip(edges, edges[1:])]
    weights = off_chip((wg, wu, wd)) if final else (wg, wu, wd)
    args = [*on_chip((nf, nft, eb, ebt)), *weights]
    out_shape = [hbm((count, CHUNK), BF16)] + [vmem((count, CHUNK), BF16)] * 2
    if final:
        args.append(on_chip(recv))
        out_shape += [vmem((2, width // 4, wide // 2 + spare), BF16)] * 4
    else:
        out_shape.append(vmem((width, wide), BF16))
    return pl.pallas_call(
        functools.partial(ffn_kernel, final, chunk * CHUNK, blocks),
        in_specs=[CHIP] * 4 + [ANY] * 3 + [CHIP] * (len(args) - 7),
        out_specs=[ANY] + [CHIP] * (len(out_shape) - 1),
        out_shape=out_shape,
        scratch_shapes=[pltpu.VMEM((width, CHUNK), BF16)] * 2
        + [
            pltpu.VMEM((CHUNK, width), BF16),
            pltpu.VMEM((count, CHUNK), BF16),
            pltpu.SemaphoreType.DMA((3,)),
            pltpu.SemaphoreType.DMA((3,)),
        ],
        compiler_params=params(24),
        cost_estimate=cost(12 * count * width * CHUNK, 8 * count * width + 12 * width * CHUNK),
        name="ffn_final" if final else "ffn_other",
    )(*args)


def norm_back_rows(rows, d_normed, gain):
    inv = lax.rsqrt(jnp.mean(rows * rows, -1, keepdims=True) + EPS)
    unit = rows * inv
    weighted = d_normed * gain
    d_rows = inv * (weighted - unit * jnp.mean(weighted * unit, -1, keepdims=True))
    return d_rows, jnp.sum(d_normed * unit, 0, keepdims=True)


def ffn_back_kernel(
    dp, me_ref, gain_ref, h1_hbm, eb_ref, o_ref, d_refs, wg_hbm, wu_hbm, wo_hbm,
    dh1_ref, do_ref, dgain_ref, there_ref, here_ref, h1_ref, weights, wo, turn, abt, in_sems,
):
    count, width = h1_ref.shape
    cols, half = wo_hbm[0].shape[0], wg_hbm[0].shape[1]
    arrive = Copies(in_sems)
    w_in = [arrive.start(w, weights.at[i]) for i, w in enumerate((*wg_hbm, *wu_hbm))]
    wo_in = [arrive.start(w, wo.at[i * cols : (i + 1) * cols, :]) for i, w in enumerate(wo_hbm)]
    blocks = row_blocks(count)
    h1_in = [arrive.start(h1_hbm.at[own, :], h1_ref.at[own, :]) for own in blocks]
    per = len(d_refs) // len(w_in)

    def product(i):
        total = None
        for j, w in enumerate(w_in):
            if i == 0:
                w.wait()
            left = jnp.concatenate([d[blocks[i], :] for d in d_refs[j * per : (j + 1) * per]], 1)
            term = dot_nt(left, weights[j])
            total = term if total is None else total + term
        return total

    dnf, gain_total = product(0), None
    for c in wo_in:
        c.wait()
    for i, own in enumerate(blocks):
        upcoming = product(i + 1) if i + 1 < len(blocks) else None
        h1_in[i].wait()
        d_rows, gain_part = norm_back_rows(h1_ref[own, :], dnf, gain_ref[...][None, :])
        gain_total = gain_part if gain_total is None else gain_total + gain_part
        back = eb_ref[own, :].astype(F32) + d_rows
        dh1_ref[own, :] = back
        rounded = back.astype(BF16)
        do_ref[own, :] = dot_nt(rounded, wo[...]).astype(BF16)
        store_transposed(rounded, turn, abt.at[:, own], me_ref, dp)
        dnf = upcoming
    dgain_ref[...] = gain_total
    quarter = width // 4
    for start in range(0, width, quarter):
        own = slice(start, start + quarter)
        total = dot(abt[own, :], o_ref[...])
        there_ref[own, :] = total[:, cols:].astype(BF16)
        here_ref[own, :] = total[:, :cols].astype(BF16)


def ffn_back(dp, me, h1, eb, gain, wg, wu, wo, o, d):
    count, width = h1.shape
    half, cols = wg[0].shape[1], wo[0].shape[0]
    return pl.pallas_call(
        functools.partial(ffn_back_kernel, dp),
        in_specs=[SCALAR, CHIP, ANY, CHIP, CHIP, [CHIP] * len(d), [ANY] * 2, [ANY] * 2, [ANY] * 2],
        out_specs=[CHIP] * 5,
        out_shape=[
            vmem((count, width), F32),
            vmem((count, 2 * cols), BF16),
            vmem((1, width), F32),
            vmem((width, cols), BF16),
            vmem((width, cols), BF16),
        ],
        scratch_shapes=[
            pltpu.VMEM((count, width), F32),
            pltpu.VMEM((4, width, half), BF16),
            pltpu.VMEM((2 * cols, width), BF16),
            pltpu.VMEM((width, ROWS), BF16),
            pltpu.VMEM((width, count), BF16),
            pltpu.SemaphoreType.DMA((6 + count // ROWS,)),
        ],
        compiler_params=params(26),
        cost_estimate=cost(4 * count * width * (2 * half + 2 * cols), 20 * count * width + 8 * count * half),
        name="ffn_back",
    )(
        me, on_chip(gain), off_chip(h1), *on_chip((eb, o)), list(on_chip(d)),
        [off_chip(wg[0]), wg[1]], [off_chip(wu[0]), wu[1]], [off_chip(wo[0]), wo[1]],
    )


def join_kernel(here_ref, recv_ref, *rest):
    outs = rest[4:8]
    quarter, cut = here_ref.shape[0] // 4, here_ref.shape[1] // 2
    spare = slice(outs[0].shape[2] - cut, outs[0].shape[2])
    for place in range(4):
        own = slice(place * quarter, place * quarter + quarter)
        values = here_ref[own, :].astype(F32) + recv_ref[own, :].astype(F32)
        b0, b1 = place // 2, place % 2
        (outs[0] if b0 else outs[1])[b1, :, spare] = values[:, :cut].astype(BF16)
        (outs[2] if b1 else outs[3])[b0, :, spare] = values[:, cut:].astype(BF16)


def join(here, recv, pieces):
    return pl.pallas_call(
        join_kernel,
        in_specs=[CHIP] * 2 + [CHIP] * 4,
        out_specs=[CHIP] * 4,
        out_shape=[vmem(p.shape, BF16) for p in pieces],
        input_output_aliases={2 + i: i for i in range(4)},
        compiler_params=params(16),
        cost_estimate=cost(here.size, 6 * here.size),
        name="join",
    )(*on_chip((here, recv)), *on_chip(pieces))


def finish_kernel(
    items, me_ref, lens_ref, gain_ref, dh1_ref, d_refs, x_hbm, w_hbm, h1_hbm, wd_hbm, hid_hbm,
    gin_hbm, out_hbm, dgain_ref, weights, x, gin, h1, wd, hid, out, in_sems, out_sems
):
    arrive, sent = Copies(in_sems), Copies(out_sems)
    cols, per = w_hbm[0].shape[1], 3
    w_in = [
        arrive.start(w, weights.at[i // per, :, (i % per) * cols : (i % per + 1) * cols]) for i, w in enumerate(w_hbm)
    ]
    blocks = row_blocks(x.shape[0])
    x_in = [arrive.start(x_hbm.at[own, :], x.at[own, :]) for own in blocks]
    half, size = wd_hbm[0].shape[0], hid_hbm[0].shape[1]
    wd_in = [arrive.start(w, wd.at[i * half : (i + 1) * half, :]) for i, w in enumerate(wd_hbm)]
    row_in = [
        [arrive.start(h.at[own, :], hid.at[own, j * size : (j + 1) * size]) for j, h in enumerate(hid_hbm)]
        + [arrive.start(h1_hbm.at[own, :], h1.at[own, :])]
        for own in blocks
    ]

    def product(i):
        total = None
        for j in range(len(w_in) // per):
            if i == 0:
                for c in w_in[j * per : (j + 1) * per]:
                    c.wait()
            left = jnp.concatenate([d[blocks[i], :] for d in d_refs[j * per : (j + 1) * per]], 1)
            term = dot_nt(left, weights[j])
            total = term if total is None else total + term
        return total

    def down(i):
        if i == 0:
            for c in wd_in:
                c.wait()
        for c in row_in[i]:
            c.wait()
        return dot(hid[blocks[i], :], wd[...])

    dna, gain_total, total = product(0), None, None
    for i, own in enumerate(blocks):
        upcoming = product(i + 1) if i + 1 < len(blocks) else None
        if i + 1 == len(blocks):
            total = down(0)
        x_in[i].wait()
        d_rows, gain_part = norm_back_rows(x[own, :].astype(F32), dna, gain_ref[...][None, :])
        gain_total = gain_part if gain_total is None else gain_total + gain_part
        gin[own, :] = dh1_ref[own, :] + d_rows
        sent.start(gin.at[own, :], gin_hbm.at[own, :])
        dna = upcoming
    dgain_ref[...] = gain_total
    for i, own in enumerate(blocks):
        upcoming = down(i + 1) if i + 1 < len(blocks) else None
        total = total + h1[own, :]
        out[own, :] = jnp.where(row_is_valid(me_ref, lens_ref, items, own.start), total, 0.0).astype(BF16)
        sent.start(out.at[own, :], out_hbm.at[own, :])
        total = upcoming
    sent.wait()


def finish(me, lens, x, dh1, gain, weights, grads, h1, wd, hid):
    count, width = x.shape
    cols, half = weights[0].shape[1], wd[0].shape[0]
    deep, mine, steps = cols * len(weights), len(weights) // 2, count // ROWS
    return pl.pallas_call(
        functools.partial(finish_kernel, count // SLOTS),
        in_specs=[SCALAR, SCALAR, CHIP, CHIP, [CHIP] * len(grads), ANY, [ANY] * len(weights), ANY, [ANY] * 2, [ANY] * len(hid)],
        out_specs=[ANY, ANY, CHIP],
        out_shape=[hbm((count, width), F32), hbm((count, width), BF16), vmem((1, width), F32)],
        scratch_shapes=[
            pltpu.VMEM((2, width, deep // 2), BF16),
            pltpu.VMEM((count, width), BF16),
            pltpu.VMEM((count, width), F32),
            pltpu.VMEM((count, width), F32),
            pltpu.VMEM((2 * half, width), BF16),
            pltpu.VMEM((count, 2 * half), BF16),
            pltpu.VMEM((count, width), BF16),
            pltpu.SemaphoreType.DMA((len(weights) + 2 + steps * (2 + len(hid)),)),
            pltpu.SemaphoreType.DMA((2 * steps,)),
        ],
        compiler_params=params(40),
        cost_estimate=cost(2 * count * width * (deep + 2 * half), 16 * count * width + 2 * count * (deep + 2 * half)),
        name="finish",
    )(
        me, lens, *on_chip((gain, dh1)), list(on_chip(grads)), off_chip(x),
        [*off_chip(weights[:mine]), *weights[mine:]], off_chip(h1), [off_chip(wd[0]), wd[1]], list(off_chip(hid)),
    )


def second_kernel(keep_a, recv_a, keep_b, recv_b, send_a, send_b):
    send_a[...] = (keep_a[1].astype(F32) + recv_a[1].astype(F32)).astype(BF16)
    send_b[...] = (keep_b[1].astype(F32) + recv_b[1].astype(F32)).astype(BF16)


def third_kernel(keep_a, recv_a, last_a, keep_b, recv_b, last_b, keep_ref, send_refs):
    group, cut = keep_ref.shape[0], keep_a.shape[2]
    for z in range(len(send_refs) + 1):
        own = slice(z * group, z * group + group)
        for cols, keep, recv, last in (
            (slice(0, cut), keep_a, recv_a, last_a),
            (slice(cut, 2 * cut), keep_b, recv_b, last_b),
        ):
            total = keep[0, own, :].astype(F32) + recv[0, own, :].astype(F32) + last[own, :].astype(F32)
            if z:
                send_refs[z - 1][:, cols] = total.astype(BF16)
            else:
                keep_ref[:, cols] = total


def swap_dp(array, dp, relative):
    return lax.ppermute(array, "dp", [(i, i ^ relative) for i in range(dp)])


def first_swaps(pieces, dp):
    return swap_dp(pieces[0], dp, 1), swap_dp(pieces[2], dp, 2)


def second_swaps(pieces, recv, dp):
    _, keep_a, _, keep_b = pieces
    _, quarter, cut = keep_a.shape
    next_a, next_b = pl.pallas_call(
        second_kernel,
        out_shape=[sds((quarter, cut), BF16)] * 2,
        compiler_params=params(24),
        cost_estimate=cost(quarter * cut * 2, quarter * cut * 12),
        name="second_sum",
    )(keep_a, recv[0], keep_b, recv[1])
    return swap_dp(next_a, dp, 2), swap_dp(next_b, dp, 1)


def third_swaps(pieces, recv, last, dp):
    _, keep_a, _, keep_b = pieces
    _, quarter, cut = keep_a.shape
    far = dp // 4
    group = quarter // far
    kept, sends = pl.pallas_call(
        third_kernel,
        out_shape=[sds((group, 2 * cut), F32), [sds((group, 2 * cut), BF16)] * (far - 1)],
        compiler_params=params(24),
        cost_estimate=cost(quarter * cut * 4, quarter * cut * 16),
        name="third_sum",
    )(keep_a, recv[0], last[0], keep_b, recv[1], last[1])
    return kept, tuple(swap_dp(send, dp, 4 * (z + 1)) for z, send in enumerate(sends))


def direct_kernel(keep, recv_refs, keep_ref, send_refs):
    group = keep_ref.shape[0]
    for z in range(len(send_refs) + 1):
        own = slice(z * group, z * group + group)
        total = keep[own, :].astype(F32)
        for recv in recv_refs:
            total = total + recv[own, :].astype(F32)
        if z:
            send_refs[z - 1][...] = total.astype(BF16)
        else:
            keep_ref[...] = total


def direct_swaps(pieces, dp):
    return tuple(swap_dp(piece, dp, relative) for piece, relative in zip(pieces[1:], (2, 1, 3)))


def direct_far_swaps(keep, recv, dp):
    quarter, cols = keep.shape
    far = dp // 4
    group = quarter // far
    kept, sends = pl.pallas_call(
        direct_kernel,
        out_shape=[sds((group, cols), F32), [sds((group, cols), BF16)] * (far - 1)],
        compiler_params=params(24),
        cost_estimate=cost(quarter * cols * 4, quarter * cols * 10),
        name="direct_sum",
    )(keep, list(recv))
    return kept, tuple(swap_dp(send, dp, 4 * (z + 1)) for z, send in enumerate(sends))


def last_kernel(kept, far_refs, outs):
    for p in range(kept.shape[1] // (3 * PAIR)):
        for j, out in enumerate(outs):
            own = slice((3 * p + j) * PAIR, (3 * p + j + 1) * PAIR)
            total = kept[:, own]
            for far in far_refs:
                total = total + far[:, own].astype(F32)
            out[:, p * PAIR : (p + 1) * PAIR] = total


def last_sum(kept, far):
    group, cols = kept.shape
    return pl.pallas_call(
        lambda kept, far_refs, *outs: last_kernel(kept, far_refs, outs),
        out_shape=[sds((group, cols // 3), F32)] * 3,
        compiler_params=params(16),
        name="last_sum",
    )(kept, list(far))


def total_of(kept, arrived):
    for part in arrived:
        kept = kept + part.astype(F32)
    return kept


fence = lax.optimization_barrier


def swap_sum(values, dp, relatives):
    count = 1 << len(relatives)
    terms = [values]
    for r in range(1, count):
        relative = sum(bit for i, bit in enumerate(relatives) if r >> i & 1)
        terms.append(swap_dp(values, dp, relative))
    while len(terms) > 1:
        terms = [terms[i] + terms[i + 1] for i in range(0, len(terms), 2)]
    return terms[0]


def local(
    dp, mp, tokens, lengths, gain_attn, w_query, w_key, w_value, w_out, gain_ffn, w_gate, w_up, w_down, cotangent
):
    count, width = tokens.shape
    me = jnp.stack([lax.axis_index("dp"), lax.axis_index("mp")]).astype(jnp.int32)
    gain_a, gain_f = gain_attn, gain_ffn

    def other(array):
        return lax.ppermute(array, "mp", [(0, 1), (1, 0)])

    wq, wk, wv, wo, wg, wu, wd = (
        (w, other(w)) for w in (w_query, w_key, w_value, w_out, w_gate, w_up, w_down)
    )
    tables = tuple(jnp.asarray(t) for t in position_tables(count))

    na, nat, eb, ebt = prepare(dp, me, lengths, tokens, cotangent, gain_a)
    na, wq, wk, wv = fence((na, wq, wk, wv))
    nat, ebt = finish_transposed(nat, me, dp), finish_transposed(ebt, me, dp)
    q, k, v, h1, o, lse, nf, nft = front(
        dp, me, na, tables, gain_f, ((wq[0], wk[0], wv[0]), (wq[1], wk[1], wv[1])), wo, tokens
    )
    nft = finish_transposed(nft, me, dp)

    half = w_gate.shape[1]
    chunks = half // CHUNK
    made, back = [], []
    for c in range(chunks):
        nf, made = fence((nf, made))
        *rest, there = ffn(nf, nft, eb, ebt, wg[1], wu[1], wd[1], c)
        made.append(rest)
        back.append(other(there))
    theirs = made
    made, pieces, recv = [], [], []
    for c in range(chunks):
        nf, here, theirs, made = fence((nf, back[c], theirs, made))
        spare = w_out.shape[0] // 2 if c == chunks - 1 else 0
        *rest, sa, ka, sb, kb = ffn(nf, nft, eb, ebt, wg[0], wu[0], wd[0], c, here, spare)
        made.append(rest)
        pieces.append((sa, ka, sb, kb))
        recv.append(first_swaps(pieces[-1], dp) if c < chunks - 1 else None)
    h1, recv, made, theirs = fence((h1, recv[:-1], made, theirs))
    last = [second_swaps(p, r, dp) for p, r in zip(pieces, recv)]
    parts = made + theirs
    hid = [p[0] for p in parts]
    dh1, do, dgain_f, out_there, out_here = ffn_back(
        dp, me, h1, eb, gain_f, wg, wu, wo, o, [p[1] for p in parts] + [p[2] for p in parts]
    )
    out_there, out_here, last, do = fence((out_there, out_here, last, do))
    back_out = other(out_there)
    third = [third_swaps(p, r, l, dp) for p, r, l in zip(pieces, recv, last)]
    pieces[-1] = join(out_here, back_out, pieces[-1])
    recv.append(first_swaps(pieces[-1], dp))
    heads = w_query.shape[1] // PAIR
    do, pieces = fence((do, pieces))
    *d1, qkv_there = attention_back(q, k, v, do, lse, tables, nat, heads)
    qkv_there, d1, recv, third, do = fence((qkv_there, d1, recv, third, do))
    back_qkv = other(qkv_there)
    last_last = second_swaps(pieces[-1], recv[-1], dp)
    *d0, keep_q, s1, s2, s3 = attention_back(q, k, v, do, lse, tables, nat, 0, back_qkv)
    d0, s1, s2, s3, last_last = fence((d0, s1, s2, s3, last_last))
    recv_q = direct_swaps((keep_q, s1, s2, s3), dp)
    third.append(third_swaps(pieces[-1], recv[-1], last_last, dp))
    grad_input, output, dgain_a = finish(
        me, lengths, tokens, dh1, gain_a, (wq[0], wk[0], wv[0], wq[1], wk[1], wv[1]), (*d0, *d1), h1, wd, hid
    )
    dgain_a, recv_q, third = fence((dgain_a, recv_q, third))
    kept_q, far_q = direct_far_swaps(keep_q, recv_q, dp)
    gains = jnp.concatenate([dgain_a, dgain_f], 0)
    gains = gains + other(gains)
    gains = swap_sum(gains, dp, (1, 2))
    gains = swap_sum(gains, dp, [1 << i for i in range(2, dp.bit_length() - 1)])
    gq, gk, gv = last_sum(kept_q, far_q)
    summed = [total_of(*t) for t in third]
    wide = 3 * CHUNK
    ffn_pieces, out_cols = [], []
    for p in summed:
        cut = p.shape[1] // 2
        ffn_pieces.append(jnp.concatenate([p[:, : wide // 2], p[:, cut : cut + wide // 2]], 1))
        if cut > wide // 2:
            out_cols = [p[:, wide // 2 : cut], p[:, cut + wide // 2 :]]
    out_piece = jnp.concatenate(out_cols, 1)

    g_gate, g_up, g_down = (
        jnp.concatenate([p[:, i * CHUNK : (i + 1) * CHUNK] for p in ffn_pieces], 1) for i in range(3)
    )
    return (
        output, grad_input, gains[0], gq, gk, gv, out_piece.T, gains[1], g_gate, g_up, g_down.T,
    )


def solution(mesh):
    in_specs = (
        P(("dp", "mp"), None),
        P("dp"),
        P(),
        P(None, "mp"),
        P(None, "mp"),
        P(None, "mp"),
        P("mp", None),
        P(),
        P(None, "mp"),
        P(None, "mp"),
        P("mp", None),
        P(("dp", "mp"), None),
    )
    out_specs = (
        P(("dp", "mp"), None),
        P(("dp", "mp"), None),
        P(),
        P("dp", "mp"),
        P("dp", "mp"),
        P("dp", "mp"),
        P("mp", "dp"),
        P(),
        P("dp", "mp"),
        P("dp", "mp"),
        P("mp", "dp"),
    )
    body = functools.partial(local, mesh.shape["dp"], mesh.shape["mp"])
    return jax.shard_map(body, mesh=mesh, in_specs=in_specs, out_specs=out_specs, check_vma=False)
```

```python
import functools

import jax
import jax.numpy as jnp
import numpy as np
from jax import lax
from jax.experimental import pallas as pl
from jax.experimental.pallas import tpu as pltpu
from jax.sharding import PartitionSpec as P

HEAD = 64
PAIR = 2 * HEAD
SLOTS = 576
EPS = 1e-05
THETA = 10000.0
ROWS = 384
CHUNK = 512
F32 = jnp.float32
BF16 = jnp.bfloat16
NEG = -1e30
BLOCKS = ((512, 64), (256, 256), (0, 256))
MIB = 1 << 20


def hbm(shape, dtype):
    return pltpu.HBM(shape, dtype)


def vmem(shape, dtype):
    return pltpu.VMEM(shape, dtype)


def on_chip(tree):
    return jax.tree.map(lambda a: pltpu.with_memory_space_constraint(a, pltpu.VMEM), tree)


def off_chip(tree):
    return jax.tree.map(lambda a: pltpu.with_memory_space_constraint(a, pltpu.HBM), tree)


def copy(source, target, sem):
    made = pltpu.make_async_copy(source, target, sem)
    made.start()
    return made


ANY = pl.BlockSpec(memory_space=pl.ANY)
CHIP = pl.BlockSpec(memory_space=pltpu.VMEM)
SCALAR = pl.BlockSpec(memory_space=pltpu.SMEM)


def dot(left, right):
    return jnp.dot(left, right, preferred_element_type=F32)


def dot_nt(left, right):
    return lax.dot_general(left, right, (((1,), (1,)), ((), ())), preferred_element_type=F32)


def params(mib):
    return pltpu.CompilerParams(vmem_limit_bytes=mib * MIB)


def cost(flops, moved, special=0):
    return pl.CostEstimate(flops=int(flops), bytes_accessed=int(moved), transcendentals=int(special))


def sds(shape, dtype):
    return jax.ShapeDtypeStruct(shape, dtype)


def position_tables(row_count):
    inv_freq = np.float32(THETA) ** (
        -(np.float32(2.0) * np.arange(HEAD // 2, dtype=np.float32)) / np.float32(HEAD)
    )
    places = (np.arange(row_count) % SLOTS).astype(np.float32)
    angles = (places[:, None] * inv_freq[None, :].astype(np.float32)).astype(np.float32)
    cosine, sine = np.cos(angles), np.sin(angles)
    cos_t = np.tile(cosine, (1, PAIR // cosine.shape[1]))
    sin_t = np.tile(np.concatenate([-sine, sine], 1), (1, 2))
    return cos_t.astype(np.float32), sin_t.astype(np.float32)


def swap_halves(values):
    lane = lax.broadcasted_iota(jnp.int32, values.shape, 1)
    return jnp.where(
        lane % HEAD < HEAD // 2,
        pltpu.roll(values, PAIR - HEAD // 2, 1),
        pltpu.roll(values, HEAD // 2, 1),
    )


def relative_order(dp):
    return [b0 + 2 * b1 + 4 * z for b0 in range(2) for b1 in range(2) for z in range(dp // 4)]


def store_transposed(value, scratch, out_ref, me_ref, dp):
    width = value.shape[1]
    group = width // dp
    if group % 16:
        out_ref[...] = value.T
        return
    scratch[...] = value.T
    for place, relative in enumerate(relative_order(dp)):
        start = pl.multiple_of(group * jnp.bitwise_xor(me_ref[0], relative), 16)
        out_ref[group * place : group * place + group, :] = scratch[pl.ds(start, group), :]


def finish_transposed(array, me, dp):
    group = array.shape[0] // dp
    if group % 16 == 0:
        return array
    index = jnp.bitwise_xor(me[0], jnp.asarray(relative_order(dp), jnp.int32))
    return jnp.take(array.reshape(dp, group, -1), index, axis=0).reshape(array.shape)


class Copies:
    def __init__(self, sems):
        self.sems, self.made = sems, []

    def start(self, source, target):
        self.made.append(copy(source, target, self.sems.at[len(self.made)]))
        return self.made[-1]

    def wait(self):
        for c in self.made:
            c.wait()


def row_blocks(count):
    return [slice(start, start + ROWS) for start in range(0, count, ROWS)]


def prepare_kernel(
    items, dp, me_ref, lens_ref, gain_hbm, x_hbm, cot_hbm, na_ref, nat_ref, eb_ref, ebt_ref, gain_ref, x, cot, turn, sems
):
    arrive = Copies(sems)
    gain_in = arrive.start(gain_hbm, gain_ref)
    blocks = row_blocks(x.shape[0])
    inputs = [
        (arrive.start(x_hbm.at[own, :], x.at[own, :]), arrive.start(cot_hbm.at[own, :], cot.at[own, :]))
        for own in blocks
    ]
    gain_in.wait()
    for own, (x_in, cot_in) in zip(blocks, inputs):
        x_in.wait()
        rows = x[own, :].astype(F32)
        inv = lax.rsqrt(jnp.mean(rows * rows, -1, keepdims=True) + EPS)
        normed = (rows * inv * gain_ref[...][None, :]).astype(BF16)
        na_ref[own, :] = normed
        store_transposed(normed, turn.at[0], nat_ref.at[:, own], me_ref, dp)
        cot_in.wait()
        valid = row_is_valid(me_ref, lens_ref, items, own.start, own.stop - own.start)
        e = jnp.where(valid, cot[own, :].astype(F32), 0.0).astype(BF16)
        eb_ref[own, :] = e
        store_transposed(e, turn.at[1], ebt_ref.at[:, own], me_ref, dp)


def prepare(dp, me, lens, x, cot, gain):
    count, width = x.shape
    return pl.pallas_call(
        functools.partial(prepare_kernel, count // SLOTS, dp),
        in_specs=[SCALAR, SCALAR, ANY, ANY, ANY],
        out_specs=[CHIP] * 4,
        out_shape=[vmem((count, width), BF16), vmem((width, count), BF16)] * 2,
        scratch_shapes=[
            pltpu.VMEM((width,), F32),
            pltpu.VMEM((count, width), BF16),
            pltpu.VMEM((count, width), BF16),
            pltpu.VMEM((2, width, ROWS), BF16),
            pltpu.SemaphoreType.DMA((1 + 2 * (count // ROWS),)),
        ],
        compiler_params=params(14),
        cost_estimate=cost(10 * count * width, 12 * count * width),
        name="prepare",
    )(me, lens, *off_chip((gain, x, cot)))


def attention_tasks(items):
    return [(i, h, q0, qb) for i in range(items) for q0, qb in BLOCKS for h in range(2)]


def pipelined(tasks, first, second, third):
    made, ready = {}, {}
    for step in range(len(tasks) + 2):
        if step < len(tasks):
            made[step] = first(tasks[step])
        if 0 <= step - 1 < len(tasks):
            ready[step - 1] = second(tasks[step - 1], made.pop(step - 1))
        if 0 <= step - 2 < len(tasks):
            third(tasks[step - 2], ready.pop(step - 2))


def causal(shape):
    key = lax.broadcasted_iota(jnp.int32, shape, 0)
    query = lax.broadcasted_iota(jnp.int32, shape, 1)
    return key <= query


def attend(items, q_ref, k_ref, v_ref, own_cols, o_ref, lse_ref, pair, acc):
    side = lax.broadcasted_iota(jnp.int32, (SLOTS, PAIR), 1) // HEAD
    v_t = {}

    def scores(task):
        i, h, q0, qb = task
        base = i * SLOTS
        q = jnp.where(side[:qb] == h, q_ref[base + q0 : base + q0 + qb, own_cols], 0).astype(BF16)
        diag = dot_nt(k_ref[base + q0 : base + q0 + qb, own_cols], q)
        return diag, (dot_nt(k_ref[base : base + q0, own_cols], q) if q0 else None)

    def soften(task, made):
        i, h, q0, qb = task
        diag, past = made
        diag = jnp.where(causal(diag.shape), diag, NEG)
        top = jnp.max(diag, 0, keepdims=True)
        if q0:
            top = jnp.maximum(top, jnp.max(past, 0, keepdims=True))
        diag = jnp.exp(diag - top)
        total = jnp.sum(diag, 0, keepdims=True)
        if q0:
            past = jnp.exp(past - top)
            total = total + jnp.sum(past, 0, keepdims=True)
            past = past.astype(BF16)
        lse_ref[pair, 2 * i + h : 2 * i + h + 1, q0 : q0 + qb] = top + jnp.log(total)
        return diag.astype(BF16), past, total

    def mix(task, made):
        i, h, q0, qb = task
        diag, past, total = made
        if i not in v_t:
            v_t[i] = v_ref[i * SLOTS : (i + 1) * SLOTS, own_cols].T
        own = v_t[i][HEAD * h : HEAD * h + HEAD]
        out = dot(own[:, q0 : q0 + qb], diag)
        if q0:
            out = out + dot(own[:, :q0], past)
        acc[i, HEAD * h : HEAD * h + HEAD, q0 : q0 + qb] = out * (1.0 / total)

    pipelined(attention_tasks(items), scores, soften, mix)
    for i in range(items):
        o_ref[i * SLOTS : (i + 1) * SLOTS, own_cols] = acc[i].T.astype(BF16)


def front_kernel(
    dp, me_ref, gain_hbm, na_ref, cos_hbm, sin_hbm, w_hbm, wo_hbm, x_hbm,
    q_hbm, k_hbm, v_hbm, h1_hbm, o_ref, lse_ref, nf_ref, nft_ref,
    gain_ref, q_ref, k_ref, v_ref, h1_ref, acc, weights, wo, x, cosine, sine, turn, sems, out_sems,
):
    arrive = Copies(sems)
    leaving = ((q_ref, q_hbm), (k_ref, k_hbm), (v_ref, v_hbm))
    count, width = na_ref.shape
    items, cols = count // SLOTS, wo_hbm[0].shape[0]
    half = cols // PAIR
    early = [arrive.start(cos_hbm, cosine), arrive.start(sin_hbm, sine)]
    for p in range(2 * half):
        for j in range(3):
            source = w_hbm[p // half][j].at[:, (p % half) * PAIR : (p % half + 1) * PAIR]
            early.append(arrive.start(source, weights.at[:, (3 * p + j) * PAIR : (3 * p + j + 1) * PAIR]))
    late = [arrive.start(w, wo.at[i * cols : (i + 1) * cols, :]) for i, w in enumerate(wo_hbm)]
    late += [arrive.start(x_hbm, x), arrive.start(gain_hbm, gain_ref)]
    for c in early:
        c.wait()

    @pl.loop(0, 2 * half)
    def _(pair):
        own_cols = pl.ds(pl.multiple_of(pair * PAIR, PAIR), PAIR)
        own_weights = weights[:, pl.ds(pl.multiple_of(pair * 3 * PAIR, PAIR), 3 * PAIR)]
        for own in row_blocks(count):
            qkv = dot(na_ref[own, :], own_weights)
            cos_v, sin_v = cosine[own, :], sine[own, :]
            q, k = qkv[:, :PAIR], qkv[:, PAIR : 2 * PAIR]
            q_ref[own, own_cols] = ((q * cos_v + swap_halves(q) * sin_v) * HEAD**-0.5).astype(BF16)
            k_ref[own, own_cols] = (k * cos_v + swap_halves(k) * sin_v).astype(BF16)
            v_ref[own, own_cols] = qkv[:, 2 * PAIR :].astype(BF16)
        for j, (source, target) in enumerate(leaving):
            copy(source.at[:, own_cols], target.at[:, own_cols], out_sems.at[3 * pair + j])
        attend(items, q_ref, k_ref, v_ref, own_cols, o_ref, lse_ref, pair, acc)

    for c in late:
        c.wait()
    blocks = row_blocks(count)
    branch = dot(o_ref[blocks[0], :], wo[...])
    for i, own in enumerate(blocks):
        upcoming = dot(o_ref[blocks[i + 1], :], wo[...]) if i + 1 < len(blocks) else None
        rows = x[own, :].astype(F32) + branch
        h1_ref[own, :] = rows
        inv = lax.rsqrt(jnp.mean(rows * rows, -1, keepdims=True) + EPS)
        normed = (rows * inv * gain_ref[...][None, :]).astype(BF16)
        nf_ref[own, :] = normed
        store_transposed(normed, turn, nft_ref.at[:, own], me_ref, dp)
        branch = upcoming
        copy(h1_ref.at[own, :], h1_hbm.at[own, :], out_sems.at[6 * half + i])
    for p in range(2 * half):
        own_cols = slice(p * PAIR, (p + 1) * PAIR)
        for j, (source, target) in enumerate(leaving):
            pltpu.make_async_copy(source.at[:, own_cols], target.at[:, own_cols], out_sems.at[3 * p + j]).wait()
    for i, own in enumerate(blocks):
        pltpu.make_async_copy(h1_ref.at[own, :], h1_hbm.at[own, :], out_sems.at[6 * half + i]).wait()


def front(dp, me, na, tables, gain, w, wo, x):
    count, width = na.shape
    items, cols = count // SLOTS, wo[0].shape[0]
    half = cols // PAIR
    area = 2 * half * items * 2 * SLOTS * SLOTS
    return pl.pallas_call(
        functools.partial(front_kernel, dp),
        in_specs=[SCALAR, ANY, CHIP, ANY, ANY, [[ANY] * 3] * 2, [ANY] * 2, ANY],
        out_specs=[ANY] * 4 + [CHIP] * 4,
        out_shape=[hbm((count, width), BF16)] * 3
        + [
            hbm((count, width), F32), vmem((count, width), BF16),
            vmem((2 * half, 2 * items, SLOTS), F32),
            vmem((count, width), BF16), vmem((width, count), BF16),
        ],
        scratch_shapes=[pltpu.VMEM((width,), F32)]
        + [pltpu.VMEM((count, width), BF16)] * 3
        + [
            pltpu.VMEM((count, width), F32),
            pltpu.VMEM((items, PAIR, SLOTS), F32),
            pltpu.VMEM((width, 6 * cols), BF16),
            pltpu.VMEM((2 * cols, width), BF16),
            pltpu.VMEM((count, width), BF16),
            pltpu.VMEM((count, PAIR), F32),
            pltpu.VMEM((count, PAIR), F32),
            pltpu.VMEM((width, ROWS), BF16),
            pltpu.SemaphoreType.DMA((6 * half + 6,)),
            pltpu.SemaphoreType.DMA((6 * half + count // ROWS,)),
        ],
        compiler_params=params(28),
        cost_estimate=cost(8 * count * width * width + 8 * area * PAIR, 24 * count * width, area),
        name="front",
    )(me, off_chip(gain), on_chip(na), *off_chip(tables), [list(off_chip(w[0])), list(w[1])], [off_chip(wo[0]), wo[1]], off_chip(x))


def attention_back_kernel(
    final, first, d_ref, lse_ref, nat_ref, cos_hbm, sin_hbm, q_hbm, k_hbm, v_hbm, *rest
):
    q_ref, k_ref, v_ref, dq_t, dk_acc, dv_acc, cosine, sine, right, sems, row_sems = rest[-11:]
    if final:
        recv_ref, here_ref, there_ref, dq_ref, dk_ref, dv_ref, *outs = rest[:-11]
    else:
        dq_ref, dk_ref, dv_ref, out_ref = rest[:-11]
    count, cols = dq_ref.shape
    items = count // SLOTS
    arrive = Copies(sems)
    arrive.start(cos_hbm.at[:SLOTS, :], cosine)
    arrive.start(sin_hbm.at[:SLOTS, :], sine)
    arriving = ((q_hbm, q_ref), (k_hbm, k_ref), (v_hbm, v_ref))
    for p in range(cols // PAIR):
        source_cols = slice((p + first) * PAIR, (p + first + 1) * PAIR)
        for j, (source, target) in enumerate(arriving):
            copy(source.at[:, source_cols], target.at[:, p * PAIR : (p + 1) * PAIR], row_sems.at[3 * p + j])
    arrive.wait()
    side = lax.broadcasted_iota(jnp.int32, (SLOTS, PAIR), 1) // HEAD
    quarter = nat_ref.shape[0] // 4

    if final:
        send_a, keep_a, send_b, keep_b = outs
        for place in range(4):
            own = slice(place * quarter, place * quarter + quarter)
            values = (here_ref[own, :].astype(F32) + there_ref[own, :].astype(F32)).astype(BF16)
            b0, b1 = place // 2, place % 2
            (send_a if b0 else keep_a)[b1, :, 3 * cols :] = values[: quarter // 2]
            (send_b if b1 else keep_b)[b0, :, 3 * cols :] = values[quarter // 2 :]

    @pl.loop(0, cols // PAIR)
    def _(pair):
        own_cols = pl.ds(pl.multiple_of(pair * PAIR, PAIR), PAIR)
        from_cols = pl.ds(pl.multiple_of((pair + first) * PAIR, PAIR), PAIR)
        for j, (source, target) in enumerate(arriving):
            pltpu.make_async_copy(source.at[:, from_cols], target.at[:, own_cols], row_sems.at[3 * pair + j]).wait()
        k_t = {}

        def scores(task):
            i, h, q0, qb = task
            base, end = i * SLOTS, i * SLOTS + q0 + qb
            q = jnp.where(side[:qb] == h, q_ref[base + q0 : end, own_cols], 0).astype(BF16)
            d = jnp.where(side[:qb] == h, d_ref[base + q0 : end, from_cols], 0).astype(BF16)
            return q, d, dot_nt(k_ref[base:end, own_cols], q), dot_nt(v_ref[base:end, own_cols], d)

        def soften(task, made):
            i, h, q0, qb = task
            q, d, s, dp = made
            lse = lse_ref[pair + first, 2 * i + h : 2 * i + h + 1, q0 : q0 + qb]
            p = jnp.exp(s[q0:] - lse)
            p = jnp.where(causal(p.shape), p, 0.0)
            if q0:
                p = jnp.concatenate([jnp.exp(s[:q0] - lse), p], 0)
            ds = (p * (dp - jnp.sum(p * dp, 0, keepdims=True))).astype(BF16)
            return q, d, p.astype(BF16), ds

        def mix(task, made):
            i, h, q0, qb = task
            q, d, p, ds = made
            end = q0 + qb
            if i not in k_t:
                k_t[i] = k_ref[i * SLOTS : (i + 1) * SLOTS, own_cols].T
            dv, dk = dot(p, d), dot(ds, q)
            if end == SLOTS and h == 0:
                dv_acc[i] = dv
                dk_acc[i] = dk
            else:
                dv_acc[i, :end, :] += dv
                dk_acc[i, :end, :] += dk
            dq_t[i, HEAD * h : HEAD * h + HEAD, q0:end] = dot(k_t[i][HEAD * h : HEAD * h + HEAD, :end], ds)

        pipelined(attention_tasks(items), scores, soften, mix)
        cos_v, sin_v = cosine[...], sine[...]
        for i in range(items):
            own = slice(i * SLOTS, (i + 1) * SLOTS)
            dq = dq_t[i].T * HEAD**-0.5
            dq = (dq * cos_v - swap_halves(dq) * sin_v).astype(BF16)
            dk = dk_acc[i]
            dk = (dk * cos_v - swap_halves(dk) * sin_v).astype(BF16)
            dv = dv_acc[i].astype(BF16)
            for j, (ref, value) in enumerate(((dq_ref, dq), (dk_ref, dk), (dv_ref, dv))):
                ref[own, own_cols] = value
                right[own, j * PAIR : (j + 1) * PAIR] = value
        wide = pl.ds(pl.multiple_of(pair * 3 * PAIR, PAIR), 3 * PAIR)
        for place in range(4):
            own = slice(place * quarter, place * quarter + quarter)
            values = dot(nat_ref[own, :], right[...])
            if final:
                send_a, keep_a, send_b, keep_b = outs
                values = (values + recv_ref[own, wide].astype(F32)).astype(BF16)
                b0, b1 = place // 2, place % 2
                (send_a if b0 else keep_a)[b1, :, wide] = values[: quarter // 2]
                (send_b if b1 else keep_b)[b0, :, wide] = values[quarter // 2 :]
            else:
                out_ref[own, wide] = values.astype(BF16)


def attention_back(q, k, v, d, lse, tables, nat, first, recv=()):
    count, width = q.shape
    cols = width // 2
    items, pairs = count // SLOTS, cols // PAIR
    area = pairs * items * 2 * SLOTS * SLOTS
    final = bool(recv)
    args = [*on_chip((d, lse, nat)), *off_chip((*tables, q, k, v))]
    out_shape = [vmem((count, cols), BF16)] * 3
    if final:
        args += on_chip(recv)
        out_shape += [vmem((2, width // 8, 4 * cols), BF16)] * 4
    else:
        out_shape.append(vmem((width, 3 * cols), BF16))
    return pl.pallas_call(
        functools.partial(attention_back_kernel, final, first),
        in_specs=[CHIP] * 3 + [ANY] * 5 + [CHIP] * (len(args) - 8),
        out_specs=[CHIP] * len(out_shape),
        out_shape=out_shape,
        scratch_shapes=[pltpu.VMEM((count, cols), BF16)] * 3
        + [pltpu.VMEM((items, PAIR, SLOTS), F32)]
        + [pltpu.VMEM((items, SLOTS, PAIR), F32)] * 2
        + [pltpu.VMEM((SLOTS, PAIR), F32)] * 2
        + [pltpu.VMEM((count, 3 * PAIR), BF16), pltpu.SemaphoreType.DMA((2,)), pltpu.SemaphoreType.DMA((3 * pairs,))],
        compiler_params=params(20),
        cost_estimate=cost(20 * area * PAIR + 6 * count * width * cols, 16 * count * cols, area),
        name="attention_back_final" if final else "attention_back_other",
    )(*args)


def row_is_valid(me_ref, lens_ref, items, start, size):
    row = start + lax.broadcasted_iota(jnp.int32, (size, 1), 0)
    valid = row < 0
    for i in range(items):
        valid = valid | ((row >= i * SLOTS) & (row < i * SLOTS + lens_ref[me_ref[1] * items + i]))
    return valid


def split_store(values, cols, total, beside, b0, b1, outs):
    send_a, keep_a, send_b, keep_b = outs
    cut = total // 2
    if cols.start < cut:
        stop = min(cols.stop, cut)
        part = values[:, : stop - cols.start].astype(BF16)
        (send_a if b0 else keep_a)[b1, :, beside + cols.start : beside + stop] = part
    if cols.stop > cut:
        start = max(cols.start, cut)
        part = values[:, start - cols.start :].astype(BF16)
        (send_b if b1 else keep_b)[b0, :, beside + start - cut : beside + cols.stop - cut] = part


def ffn_kernel(final, column, beside, blocks, nf_ref, nft_ref, eb_ref, ebt_ref, wg_hbm, wu_hbm, wd_hbm, *rest):
    wg, wu, wd, hid, in_sems, out_sems = rest[-6:]
    if final:
        recv_ref, *rest = rest[:-6]
        hid_hbm, dg_ref, du_ref, *outs = rest[-7:]
    else:
        hid_hbm, dg_ref, du_ref, out_ref = rest[:-6]
    width = nft_ref.shape[0]
    chunk = pl.ds(column, CHUNK)
    arrive, sent = Copies(in_sems), Copies(out_sems)
    waits = [
        arrive.start(wg_hbm.at[:, chunk], wg),
        arrive.start(wu_hbm.at[:, chunk], wu),
        arrive.start(wd_hbm.at[chunk, :], wd),
    ]

    def products(own):
        made = []
        for ref, weight, multiply in ((nf_ref, wg, dot), (nf_ref, wu, dot), (eb_ref, wd, dot_nt)):
            if waits:
                waits.pop(0).wait()
            made.append(multiply(ref[own, :], weight[...]))
        return made

    def point(own, made):
        g, u, dh = made
        sig = 0.5 * jnp.tanh(0.5 * g) + 0.5
        silu = g * sig
        hid[own, :] = (silu * u).astype(BF16)
        du_ref[own, :] = (dh * silu).astype(BF16)
        dg_ref[own, :] = (dh * u * (sig + silu * (1.0 - sig))).astype(BF16)

    made = None
    for i in range(len(blocks) + 1):
        upcoming = products(blocks[i]) if i < len(blocks) else None
        if made is not None:
            point(blocks[i - 1], made)
        made = upcoming
    quarter = width // 4
    for place in range(4):
        if place == 1:
            sent.start(hid, hid_hbm)
        own = slice(place * quarter, place * quarter + quarter)
        grads = [dot(nft_ref[own, :], dg_ref[...]), dot(nft_ref[own, :], du_ref[...]), dot(ebt_ref[own, :], hid[...])]
        for j, values in enumerate(grads):
            cols = slice(j * CHUNK, (j + 1) * CHUNK)
            if final:
                split_store(values + recv_ref[own, cols].astype(F32), cols, 3 * CHUNK, beside, place // 2, place % 2, outs)
            else:
                out_ref[own, cols] = values.astype(BF16)
    sent.wait()


def ffn(nf, nft, eb, ebt, wg, wu, wd, chunk, recv=None, base=()):
    count, width = nf.shape
    final = recv is not None
    wide = 3 * CHUNK
    sizes = [512 * count // 1152, 384 * count // 1152]
    edges = [0, sizes[0], sum(sizes), count]
    blocks = [slice(i, j) for i, j in zip(edges, edges[1:])]
    weights = off_chip((wg, wu, wd)) if final else (wg, wu, wd)
    args = [*on_chip((nf, nft, eb, ebt)), *weights]
    out_shape = [hbm((count, CHUNK), BF16)] + [vmem((count, CHUNK), BF16)] * 2
    if final:
        args += [on_chip(recv), *on_chip(base)]
        out_shape += [vmem((2, width // 4, wd.shape[0] // CHUNK * wide // 2), BF16)] * 4
    else:
        out_shape.append(vmem((width, wide), BF16))
    return pl.pallas_call(
        functools.partial(ffn_kernel, final, chunk * CHUNK, chunk * wide // 2, blocks),
        in_specs=[CHIP] * 4 + [ANY] * 3 + [CHIP] * (len(args) - 7),
        out_specs=[ANY] + [CHIP] * (len(out_shape) - 1),
        out_shape=out_shape,
        input_output_aliases={8 + i: 3 + i for i in range(len(base))},
        scratch_shapes=[pltpu.VMEM((width, CHUNK), BF16)] * 2
        + [
            pltpu.VMEM((CHUNK, width), BF16),
            pltpu.VMEM((count, CHUNK), BF16),
            pltpu.SemaphoreType.DMA((3,)),
            pltpu.SemaphoreType.DMA((3,)),
        ],
        compiler_params=params(14),
        cost_estimate=cost(12 * count * width * CHUNK, 8 * count * width + 12 * width * CHUNK),
        name="ffn_final" if final else "ffn_other",
    )(*args)


def norm_back_rows(rows, d_normed, gain):
    inv = lax.rsqrt(jnp.mean(rows * rows, -1, keepdims=True) + EPS)
    unit = rows * inv
    weighted = d_normed * gain
    d_rows = inv * (weighted - unit * jnp.mean(weighted * unit, -1, keepdims=True))
    return d_rows, jnp.sum(d_normed * unit, 0, keepdims=True)


def ffn_back_kernel(
    dp, me_ref, gain_hbm, h1_hbm, eb_ref, o_ref, d_refs, wg_hbm, wu_hbm, wo_hbm,
    dh1_ref, do_ref, dgain_ref, there_ref, here_ref, gain_ref, h1_ref, weights, wo, turn, abt, in_sems,
):
    count, width = h1_ref.shape
    cols, half = wo_hbm[0].shape[0], wg_hbm[0].shape[1]
    arrive = Copies(in_sems)
    w_in = [arrive.start(w, weights.at[i]) for i, w in enumerate((*wg_hbm, *wu_hbm))]
    wo_in = [arrive.start(w, wo.at[i * cols : (i + 1) * cols, :]) for i, w in enumerate(wo_hbm)]
    blocks = row_blocks(count)
    h1_in = [arrive.start(h1_hbm.at[own, :], h1_ref.at[own, :]) for own in blocks]
    h1_in.append(arrive.start(gain_hbm, gain_ref))
    per = len(d_refs) // len(w_in)

    def product(i):
        total = None
        for j, w in enumerate(w_in):
            if i == 0:
                w.wait()
            left = jnp.concatenate([d[blocks[i], :] for d in d_refs[j * per : (j + 1) * per]], 1)
            term = dot_nt(left, weights[j])
            total = term if total is None else total + term
        return total

    dnf, gain_total = product(0), None
    for c in wo_in:
        c.wait()
    for c in h1_in:
        c.wait()
    for i, own in enumerate(blocks):
        upcoming = product(i + 1) if i + 1 < len(blocks) else None
        d_rows, gain_part = norm_back_rows(h1_ref[own, :], dnf, gain_ref[...][None, :])
        gain_total = gain_part if gain_total is None else gain_total + gain_part
        back = eb_ref[own, :].astype(F32) + d_rows
        dh1_ref[own, :] = back
        rounded = back.astype(BF16)
        do_ref[own, :] = dot_nt(rounded, wo[...]).astype(BF16)
        store_transposed(rounded, turn, abt.at[:, own], me_ref, dp)
        dnf = upcoming
    dgain_ref[...] = gain_total
    quarter = width // 4
    for start in range(0, width, quarter):
        own = slice(start, start + quarter)
        total = dot(abt[own, :], o_ref[...])
        there_ref[own, :] = total[:, cols:].astype(BF16)
        here_ref[own, :] = total[:, :cols].astype(BF16)


def ffn_back(dp, me, h1, eb, gain, wg, wu, wo, o, d):
    count, width = h1.shape
    half, cols = wg[0].shape[1], wo[0].shape[0]
    return pl.pallas_call(
        functools.partial(ffn_back_kernel, dp),
        in_specs=[SCALAR, ANY, ANY, CHIP, CHIP, [CHIP] * len(d), [ANY] * 2, [ANY] * 2, [ANY] * 2],
        out_specs=[CHIP] * 5,
        out_shape=[
            vmem((count, width), F32),
            vmem((count, 2 * cols), BF16),
            vmem((1, width), F32),
            vmem((width, cols), BF16),
            vmem((width, cols), BF16),
        ],
        scratch_shapes=[
            pltpu.VMEM((width,), F32),
            pltpu.VMEM((count, width), F32),
            pltpu.VMEM((4, width, half), BF16),
            pltpu.VMEM((2 * cols, width), BF16),
            pltpu.VMEM((width, ROWS), BF16),
            pltpu.VMEM((width, count), BF16),
            pltpu.SemaphoreType.DMA((7 + count // ROWS,)),
        ],
        compiler_params=params(20),
        cost_estimate=cost(4 * count * width * (2 * half + 2 * cols), 20 * count * width + 8 * count * half),
        name="ffn_back",
    )(
        me, *off_chip((gain, h1)), *on_chip((eb, o)), list(on_chip(d)),
        [off_chip(wg[0]), wg[1]], [off_chip(wu[0]), wu[1]], [off_chip(wo[0]), wo[1]],
    )


def finish_kernel(
    items, me_ref, lens_ref, gain_hbm, dh1_ref, d_refs, x_hbm, w_hbm, h1_hbm, wd_hbm, hid_hbm,
    gin_hbm, out_hbm, dgain_ref, gain_ref, weights, x, gin, h1, wd, hid, out, in_sems, out_sems
):
    arrive, sent = Copies(in_sems), Copies(out_sems)
    cols, per = w_hbm[0].shape[1], 3
    w_in = [
        arrive.start(w, weights.at[i // per, :, (i % per) * cols : (i % per + 1) * cols]) for i, w in enumerate(w_hbm)
    ]
    blocks = row_blocks(x.shape[0])
    x_in = [arrive.start(x_hbm.at[own, :], x.at[own, :]) for own in blocks] + [arrive.start(gain_hbm, gain_ref)]
    half, size = wd_hbm[0].shape[0], hid_hbm[0].shape[1]
    wd_in = [arrive.start(w, wd.at[i * half : (i + 1) * half, :]) for i, w in enumerate(wd_hbm)]
    row_in = [
        [arrive.start(h.at[own, :], hid.at[own, j * size : (j + 1) * size]) for j, h in enumerate(hid_hbm)]
        + [arrive.start(h1_hbm.at[own, :], h1.at[own, :])]
        for own in blocks
    ]

    def product(i):
        total = None
        for j in range(len(w_in) // per):
            if i == 0:
                for c in w_in[j * per : (j + 1) * per]:
                    c.wait()
            left = jnp.concatenate([d[blocks[i], :] for d in d_refs[j * per : (j + 1) * per]], 1)
            term = dot_nt(left, weights[j])
            total = term if total is None else total + term
        return total

    def down(i):
        if i == 0:
            for c in wd_in:
                c.wait()
        for c in row_in[i]:
            c.wait()
        return dot(hid[blocks[i], :], wd[...])

    dna, gain_total, total = product(0), None, None
    for c in x_in:
        c.wait()
    for i, own in enumerate(blocks):
        upcoming = product(i + 1) if i + 1 < len(blocks) else None
        if i + 1 == len(blocks):
            total = down(0)
        d_rows, gain_part = norm_back_rows(x[own, :].astype(F32), dna, gain_ref[...][None, :])
        gain_total = gain_part if gain_total is None else gain_total + gain_part
        gin[own, :] = dh1_ref[own, :] + d_rows
        sent.start(gin.at[own, :], gin_hbm.at[own, :])
        dna = upcoming
    dgain_ref[...] = gain_total
    for i, own in enumerate(blocks):
        upcoming = down(i + 1) if i + 1 < len(blocks) else None
        total = total + h1[own, :]
        out[own, :] = jnp.where(row_is_valid(me_ref, lens_ref, items, own.start, own.stop - own.start), total, 0.0).astype(BF16)
        sent.start(out.at[own, :], out_hbm.at[own, :])
        total = upcoming
    sent.wait()


def finish(me, lens, x, dh1, gain, weights, grads, h1, wd, hid):
    count, width = x.shape
    cols, half = weights[0].shape[1], wd[0].shape[0]
    deep, mine, steps = cols * len(weights), len(weights) // 2, count // ROWS
    return pl.pallas_call(
        functools.partial(finish_kernel, count // SLOTS),
        in_specs=[SCALAR, SCALAR, ANY, CHIP, [CHIP] * len(grads), ANY, [ANY] * len(weights), ANY, [ANY] * 2, [ANY] * len(hid)],
        out_specs=[ANY, ANY, CHIP],
        out_shape=[hbm((count, width), F32), hbm((count, width), BF16), vmem((1, width), F32)],
        scratch_shapes=[
            pltpu.VMEM((width,), F32),
            pltpu.VMEM((2, width, deep // 2), BF16),
            pltpu.VMEM((count, width), BF16),
            pltpu.VMEM((count, width), F32),
            pltpu.VMEM((count, width), F32),
            pltpu.VMEM((2 * half, width), BF16),
            pltpu.VMEM((count, 2 * half), BF16),
            pltpu.VMEM((count, width), BF16),
            pltpu.SemaphoreType.DMA((len(weights) + 3 + steps * (2 + len(hid)),)),
            pltpu.SemaphoreType.DMA((2 * steps,)),
        ],
        compiler_params=params(36),
        cost_estimate=cost(2 * count * width * (deep + 2 * half), 16 * count * width + 2 * count * (deep + 2 * half)),
        name="finish",
    )(
        me, lens, off_chip(gain), on_chip(dh1), list(on_chip(grads)), off_chip(x),
        [*off_chip(weights[:mine]), *weights[mine:]], off_chip(h1), [off_chip(wd[0]), wd[1]], list(off_chip(hid)),
    )


def second_kernel(keep_a, recv_a, keep_b, recv_b, send_a, send_b):
    send_a[...] = (keep_a[1].astype(F32) + recv_a[1].astype(F32)).astype(BF16)
    send_b[...] = (keep_b[1].astype(F32) + recv_b[1].astype(F32)).astype(BF16)


def third_kernel(keep_a, recv_a, last_a, keep_b, recv_b, last_b, keep_ref, send_refs):
    group, cut = keep_ref.shape[0], keep_a.shape[2]
    for z in range(len(send_refs) + 1):
        own = slice(z * group, z * group + group)
        for cols, keep, recv, last in (
            (slice(0, cut), keep_a, recv_a, last_a),
            (slice(cut, 2 * cut), keep_b, recv_b, last_b),
        ):
            total = keep[0, own, :].astype(F32) + recv[0, own, :].astype(F32) + last[own, :].astype(F32)
            if z:
                send_refs[z - 1][:, cols] = total.astype(BF16)
            else:
                keep_ref[:, cols] = total


def swap_dp(array, dp, relative):
    return lax.ppermute(array, "dp", [(i, i ^ relative) for i in range(dp)])


def first_swaps(pieces, dp):
    return swap_dp(pieces[0], dp, 1), swap_dp(pieces[2], dp, 2)


def second_swaps(pieces, recv, dp):
    _, keep_a, _, keep_b = pieces
    _, quarter, cut = keep_a.shape
    next_a, next_b = pl.pallas_call(
        second_kernel,
        in_specs=[CHIP] * 4,
        out_shape=[sds((quarter, cut), BF16)] * 2,
        compiler_params=params(8),
        cost_estimate=cost(quarter * cut * 2, quarter * cut * 12),
        name="second_sum",
    )(*on_chip((keep_a, recv[0], keep_b, recv[1])))
    return swap_dp(next_a, dp, 2), swap_dp(next_b, dp, 1)


def third_swaps(pieces, recv, last, dp):
    _, keep_a, _, keep_b = pieces
    _, quarter, cut = keep_a.shape
    far = dp // 4
    group = quarter // far
    kept, sends = pl.pallas_call(
        third_kernel,
        out_shape=[sds((group, 2 * cut), F32), [sds((group, 2 * cut), BF16)] * (far - 1)],
        compiler_params=params(12),
        cost_estimate=cost(quarter * cut * 4, quarter * cut * 16),
        name="third_sum",
    )(keep_a, recv[0], last[0], keep_b, recv[1], last[1])
    return kept, tuple(swap_dp(send, dp, 4 * (z + 1)) for z, send in enumerate(sends))


def third_rows_kernel(keep_a, recv_a, last_a, keep_b, recv_b, last_b, keep_ref, send_refs):
    group = keep_ref.shape[0]
    inner = keep_a.shape[1] // group
    for z in range(len(send_refs) + 1):
        keep, recv, last = (keep_a, recv_a, last_a) if z < inner else (keep_b, recv_b, last_b)
        own = slice(z % inner * group, z % inner * group + group)
        total = keep[0, own, :].astype(F32) + recv[0, own, :].astype(F32) + last[own, :].astype(F32)
        if z:
            send_refs[z - 1][...] = total.astype(BF16)
        else:
            keep_ref[...] = total


def third_rows_swaps(pieces, recv, last, dp):
    _, keep_a, _, keep_b = pieces
    _, rows, cols = keep_a.shape
    far = dp // 4
    group = 2 * rows // far
    kept, sends = pl.pallas_call(
        third_rows_kernel,
        in_specs=[CHIP] * 6,
        out_shape=[sds((group, cols), F32), [sds((group, cols), BF16)] * (far - 1)],
        compiler_params=params(12),
        cost_estimate=cost(rows * cols * 8, rows * cols * 20),
        name="third_rows_sum",
    )(*on_chip((keep_a, recv[0], last[0], keep_b, recv[1], last[1])))
    return kept, tuple(swap_dp(send, dp, 4 * (z + 1)) for z, send in enumerate(sends))


def near_kernel(keep_a, recv_a, last_a, keep_b, recv_b, last_b, keep_ref, send_ref):
    group, cut = keep_ref.shape[1], keep_a.shape[2]
    for z in range(4):
        own = slice(z * group, z * group + group)
        for cols, keep, recv, last in (
            (slice(0, cut), keep_a, recv_a, last_a),
            (slice(cut, 2 * cut), keep_b, recv_b, last_b),
        ):
            total = keep[0, own, :].astype(F32) + recv[0, own, :].astype(F32) + last[own, :].astype(F32)
            (send_ref if z % 2 else keep_ref)[z // 2, :, cols] = total.astype(BF16)


def far_kernel(keep, recv, send_ref):
    send_ref[...] = (keep[1].astype(F32) + recv[1].astype(F32)).astype(BF16)


def near_swap(pieces, recv, last, dp):
    _, keep_a, _, keep_b = pieces
    _, quarter, cut = keep_a.shape
    kept, send = pl.pallas_call(
        near_kernel,
        in_specs=[CHIP] * 6,
        out_shape=[sds((2, quarter // 4, 2 * cut), BF16)] * 2,
        compiler_params=params(12),
        cost_estimate=cost(quarter * cut * 4, quarter * cut * 16),
        name="near_sum",
    )(*on_chip((keep_a, recv[0], last[0], keep_b, recv[1], last[1])))
    return kept, swap_dp(send, dp, 4)


def far_swap(kept, recv, dp):
    send = pl.pallas_call(
        far_kernel,
        in_specs=[CHIP] * 2,
        out_shape=sds(kept.shape[1:], BF16),
        compiler_params=params(6),
        cost_estimate=cost(kept.size, 4 * kept.size),
        name="far_sum",
    )(*on_chip((kept, recv)))
    return swap_dp(send, dp, 8)


def last_kernel(kept, far_refs, outs):
    *qkv, out = outs
    cols = out.shape[1]

    def total(own):
        made = kept[:, own].astype(F32)
        for far in far_refs:
            made = made + far[:, own].astype(F32)
        return made

    for p in range(cols // PAIR):
        for j, ref in enumerate(qkv):
            ref[:, p * PAIR : (p + 1) * PAIR] = total(slice((3 * p + j) * PAIR, (3 * p + j + 1) * PAIR))
    out[...] = total(slice(3 * cols, 4 * cols))


def last_sum(kept, far):
    group, cols = kept.shape
    return pl.pallas_call(
        lambda kept, far_refs, *outs: last_kernel(kept, far_refs, outs),
        out_shape=[sds((group, cols // 4), F32)] * 4,
        compiler_params=params(6),
        name="last_sum",
    )(kept, list(far))


def total_of(kept, arrived):
    for part in arrived:
        kept = kept + part.astype(F32)
    return kept


fence = lax.optimization_barrier


def swap_sum(values, dp, relatives):
    count = 1 << len(relatives)
    terms = [values]
    for r in range(1, count):
        relative = sum(bit for i, bit in enumerate(relatives) if r >> i & 1)
        terms.append(swap_dp(values, dp, relative))
    while len(terms) > 1:
        terms = [terms[i] + terms[i + 1] for i in range(0, len(terms), 2)]
    return terms[0]


def local(
    dp, mp, tokens, lengths, gain_attn, w_query, w_key, w_value, w_out, gain_ffn, w_gate, w_up, w_down, cotangent
):
    count, width = tokens.shape
    me = jnp.stack([lax.axis_index("dp"), lax.axis_index("mp")]).astype(jnp.int32)
    gain_a, gain_f = gain_attn, gain_ffn

    def other(array):
        return lax.ppermute(array, "mp", [(0, 1), (1, 0)])

    wq, wk, wv, wo = ((w, other(w)) for w in (w_query, w_key, w_value, w_out))
    tables = tuple(jnp.asarray(t) for t in position_tables(count))

    na, nat, eb, ebt = prepare(dp, me, lengths, tokens, cotangent, gain_a)
    na, wq, wk, wv, w_gate, w_up, w_down = fence((na, wq, wk, wv, w_gate, w_up, w_down))
    wg, wu, wd = ((w, other(w)) for w in (w_gate, w_up, w_down))
    nat, ebt = finish_transposed(nat, me, dp), finish_transposed(ebt, me, dp)
    q, k, v, h1, o, lse, nf, nft = front(
        dp, me, na, tables, gain_f, ((wq[0], wk[0], wv[0]), (wq[1], wk[1], wv[1])), wo, tokens
    )
    nft = finish_transposed(nft, me, dp)

    half = w_gate.shape[1]
    chunks = half // CHUNK
    made, back = [], []
    for c in range(chunks):
        nf, made = fence((nf, made))
        *rest, there = ffn(nf, nft, eb, ebt, wg[1], wu[1], wd[1], c)
        made.append(rest)
        back.append(other(there))
    theirs = made
    made, piece = [], ()
    for c in range(chunks):
        nf, here, theirs, made, piece = fence((nf, back[c], theirs, made, piece))
        *rest, sa, ka, sb, kb = ffn(nf, nft, eb, ebt, wg[0], wu[0], wd[0], c, here, piece)
        made.append(rest)
        piece = (sa, ka, sb, kb)
    h1, made, theirs, piece = fence((h1, made, theirs, piece))
    recv = first_swaps(piece, dp)
    parts = made + theirs
    hid = [p[0] for p in parts]
    dh1, do, dgain_f, out_there, out_here = ffn_back(
        dp, me, h1, eb, gain_f, wg, wu, wo, o, [p[1] for p in parts] + [p[2] for p in parts]
    )
    out_there, out_here, do = fence((out_there, out_here, do))
    out_back = other(out_there)
    heads = w_query.shape[1] // PAIR
    *d1, qkv_there = attention_back(q, k, v, do, lse, tables, nat, heads)
    qkv_there, out_back, d1, recv, do = fence((qkv_there, out_back, d1, recv, do))
    qkv_back = other(qkv_there)
    last = second_swaps(piece, recv, dp)
    *d0, sa, ka, sb, kb = attention_back(q, k, v, do, lse, tables, nat, 0, (qkv_back, out_here, out_back))
    q_piece = (sa, ka, sb, kb)
    d0, q_piece, last = fence((d0, q_piece, last))
    two_steps = dp == 16
    recv_q = first_swaps(q_piece, dp)
    kept, near = (near_swap if two_steps else third_swaps)(piece, recv, last, dp)
    grad_input, output, dgain_a = finish(
        me, lengths, tokens, dh1, gain_a, (wq[0], wk[0], wv[0], wq[1], wk[1], wv[1]), (*d0, *d1), h1, wd, hid
    )
    dgain_a, recv_q, near = fence((dgain_a, recv_q, near))
    far = far_swap(kept, near, dp) if two_steps else None
    last_q = second_swaps(q_piece, recv_q, dp)
    gains = jnp.concatenate([dgain_a, dgain_f], 0)
    gains = swap_sum(gains + other(gains), dp, (1,))
    gains, last_q = fence((gains, last_q))
    kept_q, far_q = third_rows_swaps(q_piece, recv_q, last_q, dp)
    gains = swap_sum(gains, dp, (2,))
    gains, first_q = fence((gains, far_q[0]))
    far_q = (first_q, *far_q[1:])
    for bit in range(2, dp.bit_length() - 1):
        gains = swap_sum(gains, dp, (1 << bit,))
    total = total_of(kept[0].astype(F32), (near[0], far)) if two_steps else total_of(kept, near)
    gq, gk, gv, out_piece = last_sum(kept_q, far_q)
    side, wide = total.shape[1] // 2, 3 * CHUNK // 2
    ffn_pieces = [
        jnp.concatenate([total[:, c * wide : (c + 1) * wide], total[:, side + c * wide : side + (c + 1) * wide]], 1)
        for c in range(chunks)
    ]
    g_gate, g_up, g_down = (
        jnp.concatenate([p[:, i * CHUNK : (i + 1) * CHUNK] for p in ffn_pieces], 1) for i in range(3)
    )
    return (
        output, grad_input, gains[0], gq, gk, gv, out_piece.T, gains[1], g_gate, g_up, g_down.T,
    )


def solution(mesh):
    in_specs = (
        P(("dp", "mp"), None),
        P("dp"),
        P(),
        P(None, "mp"),
        P(None, "mp"),
        P(None, "mp"),
        P("mp", None),
        P(),
        P(None, "mp"),
        P(None, "mp"),
        P("mp", None),
        P(("dp", "mp"), None),
    )
    out_specs = (
        P(("dp", "mp"), None),
        P(("dp", "mp"), None),
        P(),
        P("dp", "mp"),
        P("dp", "mp"),
        P("dp", "mp"),
        P("mp", "dp"),
        P(),
        P("dp", "mp"),
        P("dp", "mp"),
        P("mp", "dp"),
    )
    body = functools.partial(local, mesh.shape["dp"], mesh.shape["mp"])
    return jax.shard_map(body, mesh=mesh, in_specs=in_specs, out_specs=out_specs, check_vma=False)
```

```python
import functools

import jax
import jax.numpy as jnp
import numpy as np
from jax import lax
from jax.experimental import pallas as pl
from jax.experimental.pallas import tpu as pltpu
from jax.sharding import PartitionSpec as P

HEAD = 64
PAIR = 2 * HEAD
SLOTS = 576
EPS = 1e-05
THETA = 10000.0
ROWS = 384
CHUNK = 512
F32 = jnp.float32
BF16 = jnp.bfloat16
NEG = -1e30
BLOCKS = ((512, 64), (256, 256), (0, 256))
MIB = 1 << 20


def hbm(shape, dtype):
    return pltpu.HBM(shape, dtype)


def vmem(shape, dtype):
    return pltpu.VMEM(shape, dtype)


def on_chip(tree):
    return jax.tree.map(lambda a: pltpu.with_memory_space_constraint(a, pltpu.VMEM), tree)


def off_chip(tree):
    return jax.tree.map(lambda a: pltpu.with_memory_space_constraint(a, pltpu.HBM), tree)


def copy(source, target, sem):
    made = pltpu.make_async_copy(source, target, sem)
    made.start()
    return made


ANY = pl.BlockSpec(memory_space=pl.ANY)
CHIP = pl.BlockSpec(memory_space=pltpu.VMEM)
SCALAR = pl.BlockSpec(memory_space=pltpu.SMEM)


def dot(left, right):
    return jnp.dot(left, right, preferred_element_type=F32)


def dot_nt(left, right):
    return lax.dot_general(left, right, (((1,), (1,)), ((), ())), preferred_element_type=F32)


def params(mib):
    return pltpu.CompilerParams(vmem_limit_bytes=mib * MIB)


def cost(flops, moved, special=0):
    return pl.CostEstimate(flops=int(flops), bytes_accessed=int(moved), transcendentals=int(special))


def sds(shape, dtype):
    return jax.ShapeDtypeStruct(shape, dtype)


def position_tables(row_count):
    inv_freq = np.float32(THETA) ** (
        -(np.float32(2.0) * np.arange(HEAD // 2, dtype=np.float32)) / np.float32(HEAD)
    )
    places = (np.arange(row_count) % SLOTS).astype(np.float32)
    angles = (places[:, None] * inv_freq[None, :].astype(np.float32)).astype(np.float32)
    cosine, sine = np.cos(angles), np.sin(angles)
    cos_t = np.tile(cosine, (1, PAIR // cosine.shape[1]))
    sin_t = np.tile(np.concatenate([-sine, sine], 1), (1, 2))
    return cos_t.astype(np.float32), sin_t.astype(np.float32)


def swap_halves(values):
    lane = lax.broadcasted_iota(jnp.int32, values.shape, 1)
    return jnp.where(
        lane % HEAD < HEAD // 2,
        pltpu.roll(values, PAIR - HEAD // 2, 1),
        pltpu.roll(values, HEAD // 2, 1),
    )


def relative_order(dp):
    return [b0 + 2 * b1 + 4 * z for b0 in range(2) for b1 in range(2) for z in range(dp // 4)]


def store_transposed(value, scratch, out_ref, me_ref, dp):
    width = value.shape[1]
    group = width // dp
    if group % 16:
        out_ref[...] = value.T
        return
    scratch[...] = value.T
    for place, relative in enumerate(relative_order(dp)):
        start = pl.multiple_of(group * jnp.bitwise_xor(me_ref[0], relative), 16)
        out_ref[group * place : group * place + group, :] = scratch[pl.ds(start, group), :]


def finish_transposed(array, me, dp):
    group = array.shape[0] // dp
    if group % 16 == 0:
        return array
    index = jnp.bitwise_xor(me[0], jnp.asarray(relative_order(dp), jnp.int32))
    return jnp.take(array.reshape(dp, group, -1), index, axis=0).reshape(array.shape)


class Copies:
    def __init__(self, sems):
        self.sems, self.made = sems, []

    def start(self, source, target):
        self.made.append(copy(source, target, self.sems.at[len(self.made)]))
        return self.made[-1]

    def wait(self):
        for c in self.made:
            c.wait()


def row_blocks(count):
    return [slice(start, start + ROWS) for start in range(0, count, ROWS)]


def prepare_kernel(
    items, dp, me_ref, lens_ref, gain_hbm, x_hbm, cot_hbm, na_ref, nat_ref, eb_ref, ebt_ref, gain_ref, x, cot, turn, sems
):
    arrive = Copies(sems)
    gain_in = arrive.start(gain_hbm, gain_ref)
    blocks = row_blocks(x.shape[0])
    inputs = [
        (arrive.start(x_hbm.at[own, :], x.at[own, :]), arrive.start(cot_hbm.at[own, :], cot.at[own, :]))
        for own in blocks
    ]
    gain_in.wait()
    for own, (x_in, cot_in) in zip(blocks, inputs):
        x_in.wait()
        rows = x[own, :].astype(F32)
        inv = lax.rsqrt(jnp.mean(rows * rows, -1, keepdims=True) + EPS)
        normed = (rows * inv * gain_ref[...][None, :]).astype(BF16)
        na_ref[own, :] = normed
        store_transposed(normed, turn.at[0], nat_ref.at[:, own], me_ref, dp)
        cot_in.wait()
        valid = row_is_valid(me_ref, lens_ref, items, own.start, own.stop - own.start)
        e = jnp.where(valid, cot[own, :].astype(F32), 0.0).astype(BF16)
        eb_ref[own, :] = e
        store_transposed(e, turn.at[1], ebt_ref.at[:, own], me_ref, dp)


def prepare(dp, me, lens, x, cot, gain):
    count, width = x.shape
    return pl.pallas_call(
        functools.partial(prepare_kernel, count // SLOTS, dp),
        in_specs=[SCALAR, SCALAR, ANY, ANY, ANY],
        out_specs=[CHIP] * 4,
        out_shape=[vmem((count, width), BF16), vmem((width, count), BF16)] * 2,
        scratch_shapes=[
            pltpu.VMEM((width,), F32),
            pltpu.VMEM((count, width), BF16),
            pltpu.VMEM((count, width), BF16),
            pltpu.VMEM((2, width, ROWS), BF16),
            pltpu.SemaphoreType.DMA((1 + 2 * (count // ROWS),)),
        ],
        compiler_params=params(14),
        cost_estimate=cost(10 * count * width, 12 * count * width),
        name="prepare",
    )(me, lens, *off_chip((gain, x, cot)))


def attention_tasks(items):
    return [(i, h, q0, qb) for i in range(items) for q0, qb in BLOCKS for h in range(2)]


def pipelined(tasks, first, second, third):
    made, ready = {}, {}
    for step in range(len(tasks) + 2):
        if step < len(tasks):
            made[step] = first(tasks[step])
        if 0 <= step - 1 < len(tasks):
            ready[step - 1] = second(tasks[step - 1], made.pop(step - 1))
        if 0 <= step - 2 < len(tasks):
            third(tasks[step - 2], ready.pop(step - 2))


def causal(shape):
    key = lax.broadcasted_iota(jnp.int32, shape, 0)
    query = lax.broadcasted_iota(jnp.int32, shape, 1)
    return key <= query


def attend(items, q_ref, k_ref, v_ref, own_cols, o_ref, lse_ref, pair, acc):
    side = lax.broadcasted_iota(jnp.int32, (SLOTS, PAIR), 1) // HEAD
    v_t = {}

    def scores(task):
        i, h, q0, qb = task
        base = i * SLOTS
        q = jnp.where(side[:qb] == h, q_ref[base + q0 : base + q0 + qb, own_cols], 0).astype(BF16)
        diag = dot_nt(k_ref[base + q0 : base + q0 + qb, own_cols], q)
        return diag, (dot_nt(k_ref[base : base + q0, own_cols], q) if q0 else None)

    def soften(task, made):
        i, h, q0, qb = task
        diag, past = made
        diag = jnp.where(causal(diag.shape), diag, NEG)
        top = jnp.max(diag, 0, keepdims=True)
        if q0:
            top = jnp.maximum(top, jnp.max(past, 0, keepdims=True))
        diag = jnp.exp(diag - top)
        total = jnp.sum(diag, 0, keepdims=True)
        if q0:
            past = jnp.exp(past - top)
            total = total + jnp.sum(past, 0, keepdims=True)
            past = past.astype(BF16)
        lse_ref[pair, 2 * i + h : 2 * i + h + 1, q0 : q0 + qb] = top + jnp.log(total)
        return diag.astype(BF16), past, total

    def mix(task, made):
        i, h, q0, qb = task
        diag, past, total = made
        if i not in v_t:
            v_t[i] = v_ref[i * SLOTS : (i + 1) * SLOTS, own_cols].T
        own = v_t[i][HEAD * h : HEAD * h + HEAD]
        out = dot(own[:, q0 : q0 + qb], diag)
        if q0:
            out = out + dot(own[:, :q0], past)
        acc[i, HEAD * h : HEAD * h + HEAD, q0 : q0 + qb] = out * (1.0 / total)

    pipelined(attention_tasks(items), scores, soften, mix)
    for i in range(items):
        o_ref[i * SLOTS : (i + 1) * SLOTS, own_cols] = acc[i].T.astype(BF16)


def front_kernel(
    dp, me_ref, gain_hbm, na_ref, cos_hbm, sin_hbm, w_hbm, wo_hbm, x_hbm,
    q_hbm, k_hbm, v_hbm, h1_hbm, o_ref, lse_ref, nf_ref, nft_ref,
    gain_ref, q_ref, k_ref, v_ref, h1_ref, acc, weights, wo, x, cosine, sine, turn, sems, out_sems,
):
    arrive = Copies(sems)
    leaving = ((q_ref, q_hbm), (k_ref, k_hbm), (v_ref, v_hbm))
    count, width = na_ref.shape
    items, cols = count // SLOTS, wo_hbm[0].shape[0]
    half = cols // PAIR
    weights_in = [
        [arrive.start(w[j], weights.at[j, :, i * cols : (i + 1) * cols]) for i, w in enumerate(w_hbm)] for j in range(3)
    ]
    early = [arrive.start(cos_hbm, cosine), arrive.start(sin_hbm, sine)]
    late = [arrive.start(w, wo.at[i * cols : (i + 1) * cols, :]) for i, w in enumerate(wo_hbm)]
    late += [arrive.start(x_hbm, x), arrive.start(gain_hbm, gain_ref)]
    blocks = row_blocks(count)
    targets = (q_ref, k_ref, v_ref)

    def project(task):
        j, own = task
        return dot(na_ref[own, :], weights[j])

    def place(task, made):
        j, own = task
        if j == 2:
            v_ref[own, :] = made.astype(BF16)
            return
        cos_v, sin_v = cosine[own, :], sine[own, :]
        for start in range(0, width, PAIR):
            cols_ = slice(start, start + PAIR)
            turned = made[:, cols_] * cos_v + swap_halves(made[:, cols_]) * sin_v
            targets[j][own, cols_] = (turned * HEAD**-0.5 if j == 0 else turned).astype(BF16)

    tasks = [(j, own) for j in range(3) for own in blocks]
    made = None
    for i in range(len(tasks) + 1):
        if i % len(blocks) == 0 and i < len(tasks):
            for c in weights_in[i // len(blocks)]:
                c.wait()
        upcoming = project(tasks[i]) if i < len(tasks) else None
        if made is not None:
            if i == 1:
                for c in early:
                    c.wait()
            place(tasks[i - 1], made)
        made = upcoming
    sent = [copy(source, target, out_sems.at[j]) for j, (source, target) in enumerate(leaving)]

    @pl.loop(0, 2 * half)
    def _(pair):
        own_cols = pl.ds(pl.multiple_of(pair * PAIR, PAIR), PAIR)
        attend(items, q_ref, k_ref, v_ref, own_cols, o_ref, lse_ref, pair, acc)

    for c in late:
        c.wait()
    branch = dot(o_ref[blocks[0], :], wo[...])
    for i, own in enumerate(blocks):
        upcoming = dot(o_ref[blocks[i + 1], :], wo[...]) if i + 1 < len(blocks) else None
        rows = x[own, :].astype(F32) + branch
        h1_ref[own, :] = rows
        inv = lax.rsqrt(jnp.mean(rows * rows, -1, keepdims=True) + EPS)
        normed = (rows * inv * gain_ref[...][None, :]).astype(BF16)
        nf_ref[own, :] = normed
        store_transposed(normed, turn, nft_ref.at[:, own], me_ref, dp)
        branch = upcoming
        sent.append(copy(h1_ref.at[own, :], h1_hbm.at[own, :], out_sems.at[3 + i]))
    for c in sent:
        c.wait()


def front(dp, me, na, tables, gain, w, wo, x):
    count, width = na.shape
    items, cols = count // SLOTS, wo[0].shape[0]
    half = cols // PAIR
    area = 2 * half * items * 2 * SLOTS * SLOTS
    return pl.pallas_call(
        functools.partial(front_kernel, dp),
        in_specs=[SCALAR, ANY, CHIP, ANY, ANY, [[ANY] * 3] * 2, [ANY] * 2, ANY],
        out_specs=[ANY] * 4 + [CHIP] * 4,
        out_shape=[hbm((count, width), BF16)] * 3
        + [
            hbm((count, width), F32), vmem((count, width), BF16),
            vmem((2 * half, 2 * items, SLOTS), F32),
            vmem((count, width), BF16), vmem((width, count), BF16),
        ],
        scratch_shapes=[pltpu.VMEM((width,), F32)]
        + [pltpu.VMEM((count, width), BF16)] * 3
        + [
            pltpu.VMEM((count, width), F32),
            pltpu.VMEM((items, PAIR, SLOTS), F32),
            pltpu.VMEM((3, width, 2 * cols), BF16),
            pltpu.VMEM((2 * cols, width), BF16),
            pltpu.VMEM((count, width), BF16),
            pltpu.VMEM((count, PAIR), F32),
            pltpu.VMEM((count, PAIR), F32),
            pltpu.VMEM((width, ROWS), BF16),
            pltpu.SemaphoreType.DMA((12,)),
            pltpu.SemaphoreType.DMA((3 + count // ROWS,)),
        ],
        compiler_params=params(28),
        cost_estimate=cost(8 * count * width * width + 8 * area * PAIR, 24 * count * width, area),
        name="front",
    )(me, off_chip(gain), on_chip(na), *off_chip(tables), [list(off_chip(w[0])), list(w[1])], [off_chip(wo[0]), wo[1]], off_chip(x))


def attention_back_kernel(
    final, first, d_ref, lse_ref, nat_ref, cos_hbm, sin_hbm, q_hbm, k_hbm, v_hbm, *rest
):
    q_ref, k_ref, v_ref, dq_t, dk_acc, dv_acc, cosine, sine, right, sems, row_sems = rest[-11:]
    if final:
        recv_ref, here_ref, there_ref, dq_ref, dk_ref, dv_ref, *outs = rest[:-11]
    else:
        dq_ref, dk_ref, dv_ref, out_ref = rest[:-11]
    count, cols = dq_ref.shape
    items = count // SLOTS
    arrive = Copies(sems)
    arrive.start(cos_hbm.at[:SLOTS, :], cosine)
    arrive.start(sin_hbm.at[:SLOTS, :], sine)
    arriving = ((q_hbm, q_ref), (k_hbm, k_ref), (v_hbm, v_ref))
    for p in range(cols // PAIR):
        source_cols = slice((p + first) * PAIR, (p + first + 1) * PAIR)
        for j, (source, target) in enumerate(arriving):
            copy(source.at[:, source_cols], target.at[:, p * PAIR : (p + 1) * PAIR], row_sems.at[3 * p + j])
    arrive.wait()
    side = lax.broadcasted_iota(jnp.int32, (SLOTS, PAIR), 1) // HEAD
    quarter = nat_ref.shape[0] // 4

    if final:
        send_a, keep_a, send_b, keep_b = outs
        for place in range(4):
            own = slice(place * quarter, place * quarter + quarter)
            values = (here_ref[own, :].astype(F32) + there_ref[own, :].astype(F32)).astype(BF16)
            b0, b1 = place // 2, place % 2
            (send_a if b0 else keep_a)[b1, :, 3 * cols :] = values[: quarter // 2]
            (send_b if b1 else keep_b)[b0, :, 3 * cols :] = values[quarter // 2 :]

    @pl.loop(0, cols // PAIR)
    def _(pair):
        own_cols = pl.ds(pl.multiple_of(pair * PAIR, PAIR), PAIR)
        from_cols = pl.ds(pl.multiple_of((pair + first) * PAIR, PAIR), PAIR)
        for j, (source, target) in enumerate(arriving):
            pltpu.make_async_copy(source.at[:, from_cols], target.at[:, own_cols], row_sems.at[3 * pair + j]).wait()
        k_t = {}

        def scores(task):
            i, h, q0, qb = task
            base, end = i * SLOTS, i * SLOTS + q0 + qb
            q = jnp.where(side[:qb] == h, q_ref[base + q0 : end, own_cols], 0).astype(BF16)
            d = jnp.where(side[:qb] == h, d_ref[base + q0 : end, from_cols], 0).astype(BF16)
            return q, d, dot_nt(k_ref[base:end, own_cols], q), dot_nt(v_ref[base:end, own_cols], d)

        def soften(task, made):
            i, h, q0, qb = task
            q, d, s, dp = made
            lse = lse_ref[pair + first, 2 * i + h : 2 * i + h + 1, q0 : q0 + qb]
            p = jnp.exp(s[q0:] - lse)
            p = jnp.where(causal(p.shape), p, 0.0)
            if q0:
                p = jnp.concatenate([jnp.exp(s[:q0] - lse), p], 0)
            ds = (p * (dp - jnp.sum(p * dp, 0, keepdims=True))).astype(BF16)
            return q, d, p.astype(BF16), ds

        def mix(task, made):
            i, h, q0, qb = task
            q, d, p, ds = made
            end = q0 + qb
            if i not in k_t:
                k_t[i] = k_ref[i * SLOTS : (i + 1) * SLOTS, own_cols].T
            dv, dk = dot(p, d), dot(ds, q)
            if end == SLOTS and h == 0:
                dv_acc[i] = dv
                dk_acc[i] = dk
            else:
                dv_acc[i, :end, :] += dv
                dk_acc[i, :end, :] += dk
            dq_t[i, HEAD * h : HEAD * h + HEAD, q0:end] = dot(k_t[i][HEAD * h : HEAD * h + HEAD, :end], ds)

        pipelined(attention_tasks(items), scores, soften, mix)
        cos_v, sin_v = cosine[...], sine[...]
        for i in range(items):
            own = slice(i * SLOTS, (i + 1) * SLOTS)
            dq = dq_t[i].T * HEAD**-0.5
            dq = (dq * cos_v - swap_halves(dq) * sin_v).astype(BF16)
            dk = dk_acc[i]
            dk = (dk * cos_v - swap_halves(dk) * sin_v).astype(BF16)
            dv = dv_acc[i].astype(BF16)
            for j, (ref, value) in enumerate(((dq_ref, dq), (dk_ref, dk), (dv_ref, dv))):
                ref[own, own_cols] = value
                right[own, j * PAIR : (j + 1) * PAIR] = value
        wide = pl.ds(pl.multiple_of(pair * 3 * PAIR, PAIR), 3 * PAIR)
        for place in range(4):
            own = slice(place * quarter, place * quarter + quarter)
            values = dot(nat_ref[own, :], right[...])
            if final:
                send_a, keep_a, send_b, keep_b = outs
                values = (values + recv_ref[own, wide].astype(F32)).astype(BF16)
                b0, b1 = place // 2, place % 2
                (send_a if b0 else keep_a)[b1, :, wide] = values[: quarter // 2]
                (send_b if b1 else keep_b)[b0, :, wide] = values[quarter // 2 :]
            else:
                out_ref[own, wide] = values.astype(BF16)


def attention_back(q, k, v, d, lse, tables, nat, first, recv=()):
    count, width = q.shape
    cols = width // 2
    items, pairs = count // SLOTS, cols // PAIR
    area = pairs * items * 2 * SLOTS * SLOTS
    final = bool(recv)
    args = [*on_chip((d, lse, nat)), *off_chip((*tables, q, k, v))]
    out_shape = [vmem((count, cols), BF16)] * 3
    if final:
        args += on_chip(recv)
        out_shape += [vmem((2, width // 8, 4 * cols), BF16)] * 4
    else:
        out_shape.append(vmem((width, 3 * cols), BF16))
    return pl.pallas_call(
        functools.partial(attention_back_kernel, final, first),
        in_specs=[CHIP] * 3 + [ANY] * 5 + [CHIP] * (len(args) - 8),
        out_specs=[CHIP] * len(out_shape),
        out_shape=out_shape,
        scratch_shapes=[pltpu.VMEM((count, cols), BF16)] * 3
        + [pltpu.VMEM((items, PAIR, SLOTS), F32)]
        + [pltpu.VMEM((items, SLOTS, PAIR), F32)] * 2
        + [pltpu.VMEM((SLOTS, PAIR), F32)] * 2
        + [pltpu.VMEM((count, 3 * PAIR), BF16), pltpu.SemaphoreType.DMA((2,)), pltpu.SemaphoreType.DMA((3 * pairs,))],
        compiler_params=params(20),
        cost_estimate=cost(20 * area * PAIR + 6 * count * width * cols, 16 * count * cols, area),
        name="attention_back_final" if final else "attention_back_other",
    )(*args)


def row_is_valid(me_ref, lens_ref, items, start, size):
    row = start + lax.broadcasted_iota(jnp.int32, (size, 1), 0)
    valid = row < 0
    for i in range(items):
        valid = valid | ((row >= i * SLOTS) & (row < i * SLOTS + lens_ref[me_ref[1] * items + i]))
    return valid


def split_store(values, cols, total, beside, b0, b1, outs):
    send_a, keep_a, send_b, keep_b = outs
    cut = total // 2
    if cols.start < cut:
        stop = min(cols.stop, cut)
        part = values[:, : stop - cols.start].astype(BF16)
        (send_a if b0 else keep_a)[b1, :, beside + cols.start : beside + stop] = part
    if cols.stop > cut:
        start = max(cols.start, cut)
        part = values[:, start - cols.start :].astype(BF16)
        (send_b if b1 else keep_b)[b0, :, beside + start - cut : beside + cols.stop - cut] = part


def ffn_kernel(final, column, beside, blocks, nf_ref, nft_ref, eb_ref, ebt_ref, wg_hbm, wu_hbm, wd_hbm, *rest):
    wg, wu, wd, hid, in_sems, out_sems = rest[-6:]
    if final:
        recv_ref, *rest = rest[:-6]
        hid_hbm, dg_ref, du_ref, *outs = rest[-7:]
    else:
        hid_hbm, dg_ref, du_ref, out_ref = rest[:-6]
    width = nft_ref.shape[0]
    chunk = pl.ds(column, CHUNK)
    arrive, sent = Copies(in_sems), Copies(out_sems)
    waits = [
        arrive.start(wg_hbm.at[:, chunk], wg),
        arrive.start(wu_hbm.at[:, chunk], wu),
        arrive.start(wd_hbm.at[chunk, :], wd),
    ]

    def products(own):
        made = []
        for ref, weight, multiply in ((nf_ref, wg, dot), (nf_ref, wu, dot), (eb_ref, wd, dot_nt)):
            if waits:
                waits.pop(0).wait()
            made.append(multiply(ref[own, :], weight[...]))
        return made

    def point(own, made):
        g, u, dh = made
        sig = 0.5 * jnp.tanh(0.5 * g) + 0.5
        silu = g * sig
        hid[own, :] = (silu * u).astype(BF16)
        du_ref[own, :] = (dh * silu).astype(BF16)
        dg_ref[own, :] = (dh * u * (sig + silu * (1.0 - sig))).astype(BF16)

    made = None
    for i in range(len(blocks) + 1):
        upcoming = products(blocks[i]) if i < len(blocks) else None
        if made is not None:
            point(blocks[i - 1], made)
        made = upcoming
    quarter = width // 4
    for place in range(4):
        if place == 1:
            sent.start(hid, hid_hbm)
        own = slice(place * quarter, place * quarter + quarter)
        grads = [dot(nft_ref[own, :], dg_ref[...]), dot(nft_ref[own, :], du_ref[...]), dot(ebt_ref[own, :], hid[...])]
        for j, values in enumerate(grads):
            cols = slice(j * CHUNK, (j + 1) * CHUNK)
            if final:
                split_store(values + recv_ref[own, cols].astype(F32), cols, 3 * CHUNK, beside, place // 2, place % 2, outs)
            else:
                out_ref[own, cols] = values.astype(BF16)
    sent.wait()


def ffn(nf, nft, eb, ebt, wg, wu, wd, chunk, recv=None, base=()):
    count, width = nf.shape
    final = recv is not None
    wide = 3 * CHUNK
    sizes = [512 * count // 1152, 384 * count // 1152]
    edges = [0, sizes[0], sum(sizes), count]
    blocks = [slice(i, j) for i, j in zip(edges, edges[1:])]
    weights = off_chip((wg, wu, wd)) if final else (wg, wu, wd)
    args = [*on_chip((nf, nft, eb, ebt)), *weights]
    out_shape = [hbm((count, CHUNK), BF16)] + [vmem((count, CHUNK), BF16)] * 2
    if final:
        args += [on_chip(recv), *on_chip(base)]
        out_shape += [vmem((2, width // 4, wd.shape[0] // CHUNK * wide // 2), BF16)] * 4
    else:
        out_shape.append(vmem((width, wide), BF16))
    return pl.pallas_call(
        functools.partial(ffn_kernel, final, chunk * CHUNK, chunk * wide // 2, blocks),
        in_specs=[CHIP] * 4 + [ANY] * 3 + [CHIP] * (len(args) - 7),
        out_specs=[ANY] + [CHIP] * (len(out_shape) - 1),
        out_shape=out_shape,
        input_output_aliases={8 + i: 3 + i for i in range(len(base))},
        scratch_shapes=[pltpu.VMEM((width, CHUNK), BF16)] * 2
        + [
            pltpu.VMEM((CHUNK, width), BF16),
            pltpu.VMEM((count, CHUNK), BF16),
            pltpu.SemaphoreType.DMA((3,)),
            pltpu.SemaphoreType.DMA((3,)),
        ],
        compiler_params=params(14),
        cost_estimate=cost(12 * count * width * CHUNK, 8 * count * width + 12 * width * CHUNK),
        name="ffn_final" if final else "ffn_other",
    )(*args)


def norm_back_rows(rows, d_normed, gain):
    inv = lax.rsqrt(jnp.mean(rows * rows, -1, keepdims=True) + EPS)
    unit = rows * inv
    weighted = d_normed * gain
    d_rows = inv * (weighted - unit * jnp.mean(weighted * unit, -1, keepdims=True))
    return d_rows, jnp.sum(d_normed * unit, 0, keepdims=True)


def ffn_back_kernel(
    dp, me_ref, gain_hbm, h1_hbm, eb_ref, o_ref, d_refs, wg_hbm, wu_hbm, wo_hbm,
    dh1_ref, do_ref, dgain_ref, there_ref, here_ref, gain_ref, h1_ref, weights, wo, turn, abt, in_sems,
):
    count, width = h1_ref.shape
    cols, half = wo_hbm[0].shape[0], wg_hbm[0].shape[1]
    arrive = Copies(in_sems)
    w_in = [arrive.start(w, weights.at[i]) for i, w in enumerate((*wg_hbm, *wu_hbm))]
    wo_in = [arrive.start(w, wo.at[i * cols : (i + 1) * cols, :]) for i, w in enumerate(wo_hbm)]
    blocks = row_blocks(count)
    h1_in = [arrive.start(h1_hbm.at[own, :], h1_ref.at[own, :]) for own in blocks]
    h1_in.append(arrive.start(gain_hbm, gain_ref))
    per = len(d_refs) // len(w_in)

    def product(i):
        total = None
        for j, w in enumerate(w_in):
            if i == 0:
                w.wait()
            left = jnp.concatenate([d[blocks[i], :] for d in d_refs[j * per : (j + 1) * per]], 1)
            term = dot_nt(left, weights[j])
            total = term if total is None else total + term
        return total

    dnf, gain_total = product(0), None
    for c in wo_in:
        c.wait()
    for c in h1_in:
        c.wait()
    for i, own in enumerate(blocks):
        upcoming = product(i + 1) if i + 1 < len(blocks) else None
        d_rows, gain_part = norm_back_rows(h1_ref[own, :], dnf, gain_ref[...][None, :])
        gain_total = gain_part if gain_total is None else gain_total + gain_part
        back = eb_ref[own, :].astype(F32) + d_rows
        dh1_ref[own, :] = back
        rounded = back.astype(BF16)
        do_ref[own, :] = dot_nt(rounded, wo[...]).astype(BF16)
        store_transposed(rounded, turn, abt.at[:, own], me_ref, dp)
        dnf = upcoming
    dgain_ref[...] = gain_total
    quarter = width // 4
    for start in range(0, width, quarter):
        own = slice(start, start + quarter)
        total = dot(abt[own, :], o_ref[...])
        there_ref[own, :] = total[:, cols:].astype(BF16)
        here_ref[own, :] = total[:, :cols].astype(BF16)


def ffn_back(dp, me, h1, eb, gain, wg, wu, wo, o, d):
    count, width = h1.shape
    half, cols = wg[0].shape[1], wo[0].shape[0]
    return pl.pallas_call(
        functools.partial(ffn_back_kernel, dp),
        in_specs=[SCALAR, ANY, ANY, CHIP, CHIP, [CHIP] * len(d), [ANY] * 2, [ANY] * 2, [ANY] * 2],
        out_specs=[CHIP] * 5,
        out_shape=[
            vmem((count, width), F32),
            vmem((count, 2 * cols), BF16),
            vmem((1, width), F32),
            vmem((width, cols), BF16),
            vmem((width, cols), BF16),
        ],
        scratch_shapes=[
            pltpu.VMEM((width,), F32),
            pltpu.VMEM((count, width), F32),
            pltpu.VMEM((4, width, half), BF16),
            pltpu.VMEM((2 * cols, width), BF16),
            pltpu.VMEM((width, ROWS), BF16),
            pltpu.VMEM((width, count), BF16),
            pltpu.SemaphoreType.DMA((7 + count // ROWS,)),
        ],
        compiler_params=params(20),
        cost_estimate=cost(4 * count * width * (2 * half + 2 * cols), 20 * count * width + 8 * count * half),
        name="ffn_back",
    )(
        me, *off_chip((gain, h1)), *on_chip((eb, o)), list(on_chip(d)),
        [off_chip(wg[0]), wg[1]], [off_chip(wu[0]), wu[1]], [off_chip(wo[0]), wo[1]],
    )


def finish_kernel(
    items, me_ref, lens_ref, gain_hbm, dh1_ref, d_refs, x_hbm, w_hbm, h1_hbm, wd_hbm, hid_hbm,
    gin_hbm, out_hbm, dgain_ref, gain_ref, weights, x, gin, h1, wd, hid, out, in_sems, out_sems
):
    arrive, sent = Copies(in_sems), Copies(out_sems)
    cols, per = w_hbm[0].shape[1], 3
    w_in = [
        arrive.start(w, weights.at[i // per, :, (i % per) * cols : (i % per + 1) * cols]) for i, w in enumerate(w_hbm)
    ]
    blocks = row_blocks(x.shape[0])
    x_in = [arrive.start(x_hbm.at[own, :], x.at[own, :]) for own in blocks] + [arrive.start(gain_hbm, gain_ref)]
    half, size = wd_hbm[0].shape[0], hid_hbm[0].shape[1]
    wd_in = [arrive.start(w, wd.at[i * half : (i + 1) * half, :]) for i, w in enumerate(wd_hbm)]
    own = blocks[0]
    row_in = [arrive.start(h.at[own, :], hid.at[:, j * size : (j + 1) * size]) for j, h in enumerate(hid_hbm)]
    row_in.append(arrive.start(h1_hbm.at[own, :], h1))

    def product(i):
        total = None
        for j in range(len(w_in) // per):
            if i == 0:
                for c in w_in[j * per : (j + 1) * per]:
                    c.wait()
            left = jnp.concatenate([d[blocks[i], :] for d in d_refs[j * per : (j + 1) * per]], 1)
            term = dot_nt(left, weights[j])
            total = term if total is None else total + term
        return total

    dna, gain_total, total = product(0), None, None
    for c in x_in:
        c.wait()
    for i, own in enumerate(blocks):
        upcoming = product(i + 1) if i + 1 < len(blocks) else None
        if i + 1 == len(blocks):
            for c in wd_in + row_in:
                c.wait()
            total = h1[...] + dot(hid[...], wd[...])
        d_rows, gain_part = norm_back_rows(x[own, :].astype(F32), dna, gain_ref[...][None, :])
        gain_total = gain_part if gain_total is None else gain_total + gain_part
        gin[own, :] = dh1_ref[own, :] + d_rows
        sent.start(gin.at[own, :], gin_hbm.at[own, :])
        dna = upcoming
    dgain_ref[...] = gain_total
    own = blocks[0]
    out[...] = jnp.where(row_is_valid(me_ref, lens_ref, items, own.start, own.stop), total, 0.0).astype(BF16)
    sent.start(out, out_hbm.at[own, :])
    sent.wait()


def finish(me, lens, x, dh1, gain, weights, grads, h1, wd, hid):
    count, width = x.shape
    cols, half = weights[0].shape[1], wd[0].shape[0]
    deep, mine, steps = cols * len(weights), len(weights) // 2, count // ROWS
    return pl.pallas_call(
        functools.partial(finish_kernel, count // SLOTS),
        in_specs=[SCALAR, SCALAR, ANY, CHIP, [CHIP] * len(grads), ANY, [ANY] * len(weights), ANY, [ANY] * 2, [ANY] * len(hid)],
        out_specs=[ANY, ANY, CHIP],
        out_shape=[hbm((count, width), F32), hbm((count, width), BF16), vmem((1, width), F32)],
        scratch_shapes=[
            pltpu.VMEM((width,), F32),
            pltpu.VMEM((2, width, deep // 2), BF16),
            pltpu.VMEM((count, width), BF16),
            pltpu.VMEM((count, width), F32),
            pltpu.VMEM((ROWS, width), F32),
            pltpu.VMEM((2 * half, width), BF16),
            pltpu.VMEM((ROWS, 2 * half), BF16),
            pltpu.VMEM((ROWS, width), BF16),
            pltpu.SemaphoreType.DMA((len(weights) + 3 + steps * (2 + len(hid)),)),
            pltpu.SemaphoreType.DMA((2 * steps,)),
        ],
        compiler_params=params(28),
        cost_estimate=cost(2 * count * width * (deep + 2 * half), 16 * count * width + 2 * count * (deep + 2 * half)),
        name="finish",
    )(
        me, lens, off_chip(gain), on_chip(dh1), list(on_chip(grads)), off_chip(x),
        [*off_chip(weights[:mine]), *weights[mine:]], off_chip(h1), [off_chip(wd[0]), wd[1]], list(off_chip(hid)),
    )


def output_kernel(items, blocks, me_ref, lens_ref, h1_hbm, wd_hbm, hid_hbm, *rest):
    out_hbm, h1, wd, hid, out, in_sems, out_sems = rest[-7:]
    arrive, sent = Copies(in_sems), Copies(out_sems)
    half, size = wd_hbm[0].shape[0], hid_hbm[0].shape[1]
    wd_in = [arrive.start(w, wd.at[i * half : (i + 1) * half, :]) for i, w in enumerate(wd_hbm)]
    row_in = [
        [arrive.start(h.at[own, :], hid.at[own, j * size : (j + 1) * size]) for j, h in enumerate(hid_hbm)]
        + [arrive.start(h1_hbm.at[own, :], h1.at[own, :])]
        for own in blocks
    ]

    def down(i):
        for c in (wd_in if i == 0 else []) + row_in[i]:
            c.wait()
        return dot(hid[blocks[i], :], wd[...])

    total = down(0)
    for i, own in enumerate(blocks):
        upcoming = down(i + 1) if i + 1 < len(blocks) else None
        total = total + h1[own, :]
        out[own, :] = jnp.where(row_is_valid(me_ref, lens_ref, items, own.start, own.stop - own.start), total, 0.0).astype(BF16)
        sent.start(out.at[own, :], out_hbm.at[own, :])
        total = upcoming
    sent.wait()


def layer_output(me, lens, h1, wd, hid, rows, base=None):
    count, width = h1.shape
    half = wd[0].shape[0]
    blocks = [slice(i, i + ROWS) for i in range(rows.start, rows.stop, ROWS)]
    args = [me, lens, off_chip(h1), [off_chip(wd[0]), wd[1]], list(off_chip(hid))]
    if base is not None:
        args.append(base)
    return pl.pallas_call(
        functools.partial(output_kernel, count // SLOTS, blocks),
        in_specs=[SCALAR, SCALAR, ANY, [ANY] * 2, [ANY] * len(hid)] + [ANY] * (len(args) - 5),
        out_specs=ANY,
        out_shape=hbm((count, width), BF16),
        input_output_aliases={} if base is None else {3 + len(wd) + len(hid): 0},
        scratch_shapes=[
            pltpu.VMEM((count, width), F32),
            pltpu.VMEM((2 * half, width), BF16),
            pltpu.VMEM((count, 2 * half), BF16),
            pltpu.VMEM((count, width), BF16),
            pltpu.SemaphoreType.DMA((2 + len(blocks) * (1 + len(hid)),)),
            pltpu.SemaphoreType.DMA((len(blocks),)),
        ],
        compiler_params=params(22),
        cost_estimate=cost(2 * count * width * half, 3 * count * width + 2 * count * half),
        name="layer_output",
    )(*args)


def second_kernel(keep_a, recv_a, keep_b, recv_b, send_a, send_b):
    send_a[...] = (keep_a[1].astype(F32) + recv_a[1].astype(F32)).astype(BF16)
    send_b[...] = (keep_b[1].astype(F32) + recv_b[1].astype(F32)).astype(BF16)


def third_kernel(keep_a, recv_a, last_a, keep_b, recv_b, last_b, keep_ref, send_refs):
    group, cut = keep_ref.shape[0], keep_a.shape[2]
    for z in range(len(send_refs) + 1):
        own = slice(z * group, z * group + group)
        for cols, keep, recv, last in (
            (slice(0, cut), keep_a, recv_a, last_a),
            (slice(cut, 2 * cut), keep_b, recv_b, last_b),
        ):
            total = keep[0, own, :].astype(F32) + recv[0, own, :].astype(F32) + last[own, :].astype(F32)
            if z:
                send_refs[z - 1][:, cols] = total.astype(BF16)
            else:
                keep_ref[:, cols] = total


def swap_dp(array, dp, relative):
    return lax.ppermute(array, "dp", [(i, i ^ relative) for i in range(dp)])


def first_swaps(pieces, dp):
    return swap_dp(pieces[0], dp, 1), swap_dp(pieces[2], dp, 2)


def second_swaps(pieces, recv, dp):
    _, keep_a, _, keep_b = pieces
    _, quarter, cut = keep_a.shape
    next_a, next_b = pl.pallas_call(
        second_kernel,
        in_specs=[CHIP] * 4,
        out_shape=[sds((quarter, cut), BF16)] * 2,
        compiler_params=params(8),
        cost_estimate=cost(quarter * cut * 2, quarter * cut * 12),
        name="second_sum",
    )(*on_chip((keep_a, recv[0], keep_b, recv[1])))
    return swap_dp(next_a, dp, 2), swap_dp(next_b, dp, 1)


def third_swaps(pieces, recv, last, dp):
    _, keep_a, _, keep_b = pieces
    _, quarter, cut = keep_a.shape
    far = dp // 4
    group = quarter // far
    kept, sends = pl.pallas_call(
        third_kernel,
        out_shape=[sds((group, 2 * cut), F32), [sds((group, 2 * cut), BF16)] * (far - 1)],
        compiler_params=params(12),
        cost_estimate=cost(quarter * cut * 4, quarter * cut * 16),
        name="third_sum",
    )(keep_a, recv[0], last[0], keep_b, recv[1], last[1])
    return kept, tuple(swap_dp(send, dp, 4 * (z + 1)) for z, send in enumerate(sends))


def third_rows_kernel(keep_a, recv_a, last_a, keep_b, recv_b, last_b, keep_ref, send_refs):
    group = keep_ref.shape[0]
    inner = keep_a.shape[1] // group
    for z in range(len(send_refs) + 1):
        keep, recv, last = (keep_a, recv_a, last_a) if z < inner else (keep_b, recv_b, last_b)
        own = slice(z % inner * group, z % inner * group + group)
        total = keep[0, own, :].astype(F32) + recv[0, own, :].astype(F32) + last[own, :].astype(F32)
        if z:
            send_refs[z - 1][...] = total.astype(BF16)
        else:
            keep_ref[...] = total


def third_rows_swaps(pieces, recv, last, dp):
    _, keep_a, _, keep_b = pieces
    _, rows, cols = keep_a.shape
    far = dp // 4
    group = 2 * rows // far
    kept, sends = pl.pallas_call(
        third_rows_kernel,
        in_specs=[CHIP] * 6,
        out_shape=[sds((group, cols), F32), [sds((group, cols), BF16)] * (far - 1)],
        compiler_params=params(12),
        cost_estimate=cost(rows * cols * 8, rows * cols * 20),
        name="third_rows_sum",
    )(*on_chip((keep_a, recv[0], last[0], keep_b, recv[1], last[1])))
    return kept, tuple(swap_dp(send, dp, 4 * (z + 1)) for z, send in enumerate(sends))


def near_kernel(keep_a, recv_a, last_a, keep_b, recv_b, last_b, keep_ref, send_ref):
    group, cut = keep_ref.shape[1], keep_a.shape[2]
    for z in range(4):
        own = slice(z * group, z * group + group)
        for cols, keep, recv, last in (
            (slice(0, cut), keep_a, recv_a, last_a),
            (slice(cut, 2 * cut), keep_b, recv_b, last_b),
        ):
            total = keep[0, own, :].astype(F32) + recv[0, own, :].astype(F32) + last[own, :].astype(F32)
            (send_ref if z % 2 else keep_ref)[z // 2, :, cols] = total.astype(BF16)


def far_kernel(keep, recv, send_ref):
    send_ref[...] = (keep[1].astype(F32) + recv[1].astype(F32)).astype(BF16)


def near_swap(pieces, recv, last, dp):
    _, keep_a, _, keep_b = pieces
    _, quarter, cut = keep_a.shape
    kept, send = pl.pallas_call(
        near_kernel,
        in_specs=[CHIP] * 6,
        out_shape=[sds((2, quarter // 4, 2 * cut), BF16)] * 2,
        compiler_params=params(12),
        cost_estimate=cost(quarter * cut * 4, quarter * cut * 16),
        name="near_sum",
    )(*on_chip((keep_a, recv[0], last[0], keep_b, recv[1], last[1])))
    return kept, swap_dp(send, dp, 4)


def far_swap(kept, recv, dp):
    send = pl.pallas_call(
        far_kernel,
        in_specs=[CHIP] * 2,
        out_shape=sds(kept.shape[1:], BF16),
        compiler_params=params(6),
        cost_estimate=cost(kept.size, 4 * kept.size),
        name="far_sum",
    )(*on_chip((kept, recv)))
    return swap_dp(send, dp, 8)


def last_kernel(kept, far_refs, outs):
    *qkv, out = outs
    cols = out.shape[1]

    def total(own):
        made = kept[:, own].astype(F32)
        for far in far_refs:
            made = made + far[:, own].astype(F32)
        return made

    for p in range(cols // PAIR):
        for j, ref in enumerate(qkv):
            ref[:, p * PAIR : (p + 1) * PAIR] = total(slice((3 * p + j) * PAIR, (3 * p + j + 1) * PAIR))
    out[...] = total(slice(3 * cols, 4 * cols))


def last_sum(kept, far):
    group, cols = kept.shape
    return pl.pallas_call(
        lambda kept, far_refs, *outs: last_kernel(kept, far_refs, outs),
        out_shape=[sds((group, cols // 4), F32)] * 4,
        compiler_params=params(6),
        name="last_sum",
    )(kept, list(far))


def total_of(kept, arrived):
    for part in arrived:
        kept = kept + part.astype(F32)
    return kept


fence = lax.optimization_barrier


def swap_sum(values, dp, relatives):
    count = 1 << len(relatives)
    terms = [values]
    for r in range(1, count):
        relative = sum(bit for i, bit in enumerate(relatives) if r >> i & 1)
        terms.append(swap_dp(values, dp, relative))
    while len(terms) > 1:
        terms = [terms[i] + terms[i + 1] for i in range(0, len(terms), 2)]
    return terms[0]


def local(
    dp, mp, tokens, lengths, gain_attn, w_query, w_key, w_value, w_out, gain_ffn, w_gate, w_up, w_down, cotangent
):
    count, width = tokens.shape
    me = jnp.stack([lax.axis_index("dp"), lax.axis_index("mp")]).astype(jnp.int32)
    gain_a, gain_f = gain_attn, gain_ffn

    def other(array):
        return lax.ppermute(array, "mp", [(0, 1), (1, 0)])

    wq, wk, wv, wo = ((w, other(w)) for w in (w_query, w_key, w_value, w_out))
    tables = tuple(jnp.asarray(t) for t in position_tables(count))

    na, nat, eb, ebt = prepare(dp, me, lengths, tokens, cotangent, gain_a)
    na, wq, wk, wv, w_gate, w_up, w_down = fence((na, wq, wk, wv, w_gate, w_up, w_down))
    wg, wu, wd = ((w, other(w)) for w in (w_gate, w_up, w_down))
    nat, ebt = finish_transposed(nat, me, dp), finish_transposed(ebt, me, dp)
    q, k, v, h1, o, lse, nf, nft = front(
        dp, me, na, tables, gain_f, ((wq[0], wk[0], wv[0]), (wq[1], wk[1], wv[1])), wo, tokens
    )
    nft = finish_transposed(nft, me, dp)

    half = w_gate.shape[1]
    chunks = half // CHUNK
    made, back = [], []
    for c in range(chunks):
        nf, made = fence((nf, made))
        *rest, there = ffn(nf, nft, eb, ebt, wg[1], wu[1], wd[1], c)
        made.append(rest)
        back.append(other(there))
    theirs = made
    made, piece = [], ()
    for c in range(chunks):
        nf, here, theirs, made, piece = fence((nf, back[c], theirs, made, piece))
        *rest, sa, ka, sb, kb = ffn(nf, nft, eb, ebt, wg[0], wu[0], wd[0], c, here, piece)
        made.append(rest)
        piece = (sa, ka, sb, kb)
    h1, made, theirs, piece = fence((h1, made, theirs, piece))
    recv = first_swaps(piece, dp)
    parts = made + theirs
    hid = [p[0] for p in parts]
    dh1, do, dgain_f, out_there, out_here = ffn_back(
        dp, me, h1, eb, gain_f, wg, wu, wo, o, [p[1] for p in parts] + [p[2] for p in parts]
    )
    out_there, out_here, do = fence((out_there, out_here, do))
    out_back = other(out_there)
    heads = w_query.shape[1] // PAIR
    *d1, qkv_there = attention_back(q, k, v, do, lse, tables, nat, heads)
    qkv_there, out_back, d1, recv, do = fence((qkv_there, out_back, d1, recv, do))
    qkv_back = other(qkv_there)
    last = second_swaps(piece, recv, dp)
    *d0, sa, ka, sb, kb = attention_back(q, k, v, do, lse, tables, nat, 0, (qkv_back, out_here, out_back))
    q_piece = (sa, ka, sb, kb)
    d0, q_piece, last = fence((d0, q_piece, last))
    two_steps = dp == 16
    recv_q = first_swaps(q_piece, dp)
    kept, near = (near_swap if two_steps else third_swaps)(piece, recv, last, dp)
    grad_input, output, dgain_a = finish(
        me, lengths, tokens, dh1, gain_a, (wq[0], wk[0], wv[0], wq[1], wk[1], wv[1]), (*d0, *d1), h1, wd, hid
    )
    dgain_a, recv_q, near, h1 = fence((dgain_a, recv_q, near, h1))
    far = far_swap(kept, near, dp) if two_steps else None
    last_q = second_swaps(q_piece, recv_q, dp)
    gains = jnp.concatenate([dgain_a, dgain_f], 0)
    gains = swap_sum(gains + other(gains), dp, (1,))
    output = layer_output(me, lengths, h1, wd, hid, slice(ROWS, count), output)
    gains, last_q, output = fence((gains, last_q, output))
    kept_q, far_q = third_rows_swaps(q_piece, recv_q, last_q, dp)
    gains = swap_sum(gains, dp, (2,))
    gains, first_q, far = fence((gains, far_q[0], far))
    far_q = (first_q, *far_q[1:])
    far_bits = [1 << bit for bit in range(2, dp.bit_length() - 1)]
    for bits in (far_bits,) if two_steps else ((bit,) for bit in far_bits):
        gains = swap_sum(gains, dp, bits)
    total = total_of(kept[0].astype(F32), (near[0], far)) if two_steps else total_of(kept, near)
    gq, gk, gv, out_piece = last_sum(kept_q, far_q)
    side, wide = total.shape[1] // 2, 3 * CHUNK // 2
    ffn_pieces = [
        jnp.concatenate([total[:, c * wide : (c + 1) * wide], total[:, side + c * wide : side + (c + 1) * wide]], 1)
        for c in range(chunks)
    ]
    g_gate, g_up, g_down = (
        jnp.concatenate([p[:, i * CHUNK : (i + 1) * CHUNK] for p in ffn_pieces], 1) for i in range(3)
    )
    return (
        output, grad_input, gains[0], gq, gk, gv, out_piece.T, gains[1], g_gate, g_up, g_down.T,
    )


def solution(mesh):
    in_specs = (
        P(("dp", "mp"), None),
        P("dp"),
        P(),
        P(None, "mp"),
        P(None, "mp"),
        P(None, "mp"),
        P("mp", None),
        P(),
        P(None, "mp"),
        P(None, "mp"),
        P("mp", None),
        P(("dp", "mp"), None),
    )
    out_specs = (
        P(("dp", "mp"), None),
        P(("dp", "mp"), None),
        P(),
        P("dp", "mp"),
        P("dp", "mp"),
        P("dp", "mp"),
        P("mp", "dp"),
        P(),
        P("dp", "mp"),
        P("dp", "mp"),
        P("mp", "dp"),
    )
    body = functools.partial(local, mesh.shape["dp"], mesh.shape["mp"])
    return jax.shard_map(body, mesh=mesh, in_specs=in_specs, out_specs=out_specs, check_vma=False)
```

```python
import functools

import jax
import jax.numpy as jnp
import numpy as np
from jax import lax
from jax.experimental import pallas as pl
from jax.experimental.pallas import tpu as pltpu
from jax.sharding import PartitionSpec as P

HEAD = 64
PAIR = 2 * HEAD
SLOTS = 576
EPS = 1e-05
THETA = 10000.0
ROWS = 384
CHUNK = 512
F32 = jnp.float32
BF16 = jnp.bfloat16
NEG = -1e30
BLOCKS = ((512, 64), (256, 256), (0, 256))
MIB = 1 << 20


def hbm(shape, dtype):
    return pltpu.HBM(shape, dtype)


def vmem(shape, dtype):
    return pltpu.VMEM(shape, dtype)


def on_chip(tree):
    return jax.tree.map(lambda a: pltpu.with_memory_space_constraint(a, pltpu.VMEM), tree)


def off_chip(tree):
    return jax.tree.map(lambda a: pltpu.with_memory_space_constraint(a, pltpu.HBM), tree)


def copy(source, target, sem):
    made = pltpu.make_async_copy(source, target, sem)
    made.start()
    return made


ANY = pl.BlockSpec(memory_space=pl.ANY)
CHIP = pl.BlockSpec(memory_space=pltpu.VMEM)
SCALAR = pl.BlockSpec(memory_space=pltpu.SMEM)


def dot(left, right):
    return jnp.dot(left, right, preferred_element_type=F32)


def dot_nt(left, right):
    return lax.dot_general(left, right, (((1,), (1,)), ((), ())), preferred_element_type=F32)


def params(mib):
    return pltpu.CompilerParams(vmem_limit_bytes=mib * MIB)


def cost(flops, moved, special=0):
    return pl.CostEstimate(flops=int(flops), bytes_accessed=int(moved), transcendentals=int(special))


def sds(shape, dtype):
    return jax.ShapeDtypeStruct(shape, dtype)


def position_tables(row_count):
    inv_freq = np.float32(THETA) ** (
        -(np.float32(2.0) * np.arange(HEAD // 2, dtype=np.float32)) / np.float32(HEAD)
    )
    places = (np.arange(row_count) % SLOTS).astype(np.float32)
    angles = (places[:, None] * inv_freq[None, :].astype(np.float32)).astype(np.float32)
    cosine, sine = np.cos(angles), np.sin(angles)
    cos_t = np.tile(cosine, (1, PAIR // cosine.shape[1]))
    sin_t = np.tile(np.concatenate([-sine, sine], 1), (1, 2))
    return cos_t.astype(np.float32), sin_t.astype(np.float32)


def swap_halves(values):
    lane = lax.broadcasted_iota(jnp.int32, values.shape, 1)
    return jnp.where(
        lane % HEAD < HEAD // 2,
        pltpu.roll(values, PAIR - HEAD // 2, 1),
        pltpu.roll(values, HEAD // 2, 1),
    )


def relative_order(dp):
    return [b0 + 2 * b1 + 4 * z for b0 in range(2) for b1 in range(2) for z in range(dp // 4)]


def store_transposed(value, scratch, out_ref, me_ref, dp):
    width = value.shape[1]
    group = width // dp
    if group % 16:
        out_ref[...] = value.T
        return
    scratch[...] = value.T
    for place, relative in enumerate(relative_order(dp)):
        start = pl.multiple_of(group * jnp.bitwise_xor(me_ref[0], relative), 16)
        out_ref[group * place : group * place + group, :] = scratch[pl.ds(start, group), :]


def finish_transposed(array, me, dp):
    group = array.shape[0] // dp
    if group % 16 == 0:
        return array
    index = jnp.bitwise_xor(me[0], jnp.asarray(relative_order(dp), jnp.int32))
    return jnp.take(array.reshape(dp, group, -1), index, axis=0).reshape(array.shape)


class Copies:
    def __init__(self, sems):
        self.sems, self.made = sems, []

    def start(self, source, target):
        self.made.append(copy(source, target, self.sems.at[len(self.made)]))
        return self.made[-1]

    def wait(self):
        for c in self.made:
            c.wait()


def row_blocks(count):
    return [slice(start, start + ROWS) for start in range(0, count, ROWS)]


def prepare_kernel(
    items, dp, me_ref, lens_ref, gain_hbm, x_hbm, cot_hbm, na_ref, nat_ref, eb_ref, ebt_ref, gain_ref, x, cot, turn, sems
):
    arrive = Copies(sems)
    gain_in = arrive.start(gain_hbm, gain_ref)
    blocks = row_blocks(x.shape[0])
    inputs = [
        (arrive.start(x_hbm.at[own, :], x.at[own, :]), arrive.start(cot_hbm.at[own, :], cot.at[own, :]))
        for own in blocks
    ]
    gain_in.wait()
    for own, (x_in, cot_in) in zip(blocks, inputs):
        x_in.wait()
        rows = x[own, :].astype(F32)
        inv = lax.rsqrt(jnp.mean(rows * rows, -1, keepdims=True) + EPS)
        normed = (rows * inv * gain_ref[...][None, :]).astype(BF16)
        na_ref[own, :] = normed
        store_transposed(normed, turn.at[0], nat_ref.at[:, own], me_ref, dp)
        cot_in.wait()
        valid = row_is_valid(me_ref, lens_ref, items, own.start, own.stop - own.start)
        e = jnp.where(valid, cot[own, :].astype(F32), 0.0).astype(BF16)
        eb_ref[own, :] = e
        store_transposed(e, turn.at[1], ebt_ref.at[:, own], me_ref, dp)


def prepare(dp, me, lens, x, cot, gain):
    count, width = x.shape
    return pl.pallas_call(
        functools.partial(prepare_kernel, count // SLOTS, dp),
        in_specs=[SCALAR, SCALAR, ANY, ANY, ANY],
        out_specs=[CHIP] * 4,
        out_shape=[vmem((count, width), BF16), vmem((width, count), BF16)] * 2,
        scratch_shapes=[
            pltpu.VMEM((width,), F32),
            pltpu.VMEM((count, width), BF16),
            pltpu.VMEM((count, width), BF16),
            pltpu.VMEM((2, width, ROWS), BF16),
            pltpu.SemaphoreType.DMA((1 + 2 * (count // ROWS),)),
        ],
        compiler_params=params(14),
        cost_estimate=cost(10 * count * width, 12 * count * width),
        name="prepare",
    )(me, lens, *off_chip((gain, x, cot)))


def attention_tasks(items):
    return [(i, h, q0, qb) for i in range(items) for q0, qb in BLOCKS for h in range(2)]


def pipelined(tasks, first, second, third):
    made, ready = {}, {}
    for step in range(len(tasks) + 2):
        if step < len(tasks):
            made[step] = first(tasks[step])
        if 0 <= step - 1 < len(tasks):
            ready[step - 1] = second(tasks[step - 1], made.pop(step - 1))
        if 0 <= step - 2 < len(tasks):
            third(tasks[step - 2], ready.pop(step - 2))


def causal(shape):
    key = lax.broadcasted_iota(jnp.int32, shape, 0)
    query = lax.broadcasted_iota(jnp.int32, shape, 1)
    return key <= query


def attend(items, q_ref, k_ref, v_ref, own_cols, o_ref, lse_ref, pair, acc):
    side = lax.broadcasted_iota(jnp.int32, (SLOTS, PAIR), 1) // HEAD
    v_t = {}

    def scores(task):
        i, h, q0, qb = task
        base = i * SLOTS
        q = jnp.where(side[:qb] == h, q_ref[base + q0 : base + q0 + qb, own_cols], 0).astype(BF16)
        diag = dot_nt(k_ref[base + q0 : base + q0 + qb, own_cols], q)
        return diag, (dot_nt(k_ref[base : base + q0, own_cols], q) if q0 else None)

    def soften(task, made):
        i, h, q0, qb = task
        diag, past = made
        diag = jnp.where(causal(diag.shape), diag, NEG)
        top = jnp.max(diag, 0, keepdims=True)
        if q0:
            top = jnp.maximum(top, jnp.max(past, 0, keepdims=True))
        diag = jnp.exp(diag - top)
        total = jnp.sum(diag, 0, keepdims=True)
        if q0:
            past = jnp.exp(past - top)
            total = total + jnp.sum(past, 0, keepdims=True)
            past = past.astype(BF16)
        lse_ref[pair, 2 * i + h : 2 * i + h + 1, q0 : q0 + qb] = top + jnp.log(total)
        return diag.astype(BF16), past, total

    def mix(task, made):
        i, h, q0, qb = task
        diag, past, total = made
        if i not in v_t:
            v_t[i] = v_ref[i * SLOTS : (i + 1) * SLOTS, own_cols].T
        own = v_t[i][HEAD * h : HEAD * h + HEAD]
        out = dot(own[:, q0 : q0 + qb], diag)
        if q0:
            out = out + dot(own[:, :q0], past)
        acc[i, HEAD * h : HEAD * h + HEAD, q0 : q0 + qb] = out * (1.0 / total)

    pipelined(attention_tasks(items), scores, soften, mix)
    for i in range(items):
        o_ref[i * SLOTS : (i + 1) * SLOTS, own_cols] = acc[i].T.astype(BF16)


def front_kernel(
    dp, me_ref, gain_hbm, na_ref, cos_hbm, sin_hbm, w_hbm, wo_hbm, x_hbm,
    q_hbm, k_hbm, v_hbm, h1_hbm, o_ref, lse_ref, nf_ref, nft_ref,
    gain_ref, q_ref, k_ref, v_ref, h1_ref, acc, weights, wo, x, cosine, sine, turn, sems, out_sems,
):
    arrive = Copies(sems)
    leaving = ((q_ref, q_hbm), (k_ref, k_hbm), (v_ref, v_hbm))
    count, width = na_ref.shape
    items, cols = count // SLOTS, wo_hbm[0].shape[0]
    half = cols // PAIR
    weights_in = [
        [arrive.start(w[j], weights.at[j, :, i * cols : (i + 1) * cols]) for i, w in enumerate(w_hbm)] for j in range(3)
    ]
    early = [arrive.start(cos_hbm, cosine), arrive.start(sin_hbm, sine)]
    late = [arrive.start(w, wo.at[i * cols : (i + 1) * cols, :]) for i, w in enumerate(wo_hbm)]
    late += [arrive.start(x_hbm, x), arrive.start(gain_hbm, gain_ref)]
    blocks = row_blocks(count)
    targets = (q_ref, k_ref, v_ref)

    def project(task):
        j, own = task
        return dot(na_ref[own, :], weights[j])

    def place(task, made):
        j, own = task
        if j == 2:
            v_ref[own, :] = made.astype(BF16)
            return
        cos_v, sin_v = cosine[own, :], sine[own, :]
        for start in range(0, width, PAIR):
            cols_ = slice(start, start + PAIR)
            turned = made[:, cols_] * cos_v + swap_halves(made[:, cols_]) * sin_v
            targets[j][own, cols_] = (turned * HEAD**-0.5 if j == 0 else turned).astype(BF16)

    tasks = [(j, own) for j in range(3) for own in blocks]
    made = None
    for i in range(len(tasks) + 1):
        if i % len(blocks) == 0 and i < len(tasks):
            for c in weights_in[i // len(blocks)]:
                c.wait()
        upcoming = project(tasks[i]) if i < len(tasks) else None
        if made is not None:
            if i == 1:
                for c in early:
                    c.wait()
            place(tasks[i - 1], made)
        made = upcoming
    sent = [copy(source, target, out_sems.at[j]) for j, (source, target) in enumerate(leaving)]

    @pl.loop(0, 2 * half)
    def _(pair):
        own_cols = pl.ds(pl.multiple_of(pair * PAIR, PAIR), PAIR)
        attend(items, q_ref, k_ref, v_ref, own_cols, o_ref, lse_ref, pair, acc)

    for c in late:
        c.wait()
    branch = dot(o_ref[blocks[0], :], wo[...])
    for i, own in enumerate(blocks):
        upcoming = dot(o_ref[blocks[i + 1], :], wo[...]) if i + 1 < len(blocks) else None
        rows = x[own, :].astype(F32) + branch
        h1_ref[own, :] = rows
        inv = lax.rsqrt(jnp.mean(rows * rows, -1, keepdims=True) + EPS)
        normed = (rows * inv * gain_ref[...][None, :]).astype(BF16)
        nf_ref[own, :] = normed
        store_transposed(normed, turn, nft_ref.at[:, own], me_ref, dp)
        branch = upcoming
        sent.append(copy(h1_ref.at[own, :], h1_hbm.at[own, :], out_sems.at[3 + i]))
    for c in sent:
        c.wait()


def front(dp, me, na, tables, gain, w, wo, x):
    count, width = na.shape
    items, cols = count // SLOTS, wo[0].shape[0]
    half = cols // PAIR
    area = 2 * half * items * 2 * SLOTS * SLOTS
    return pl.pallas_call(
        functools.partial(front_kernel, dp),
        in_specs=[SCALAR, ANY, CHIP, ANY, ANY, [[ANY] * 3] * 2, [ANY] * 2, ANY],
        out_specs=[ANY] * 4 + [CHIP] * 4,
        out_shape=[hbm((count, width), BF16)] * 3
        + [
            hbm((count, width), F32), vmem((count, width), BF16),
            vmem((2 * half, 2 * items, SLOTS), F32),
            vmem((count, width), BF16), vmem((width, count), BF16),
        ],
        scratch_shapes=[pltpu.VMEM((width,), F32)]
        + [pltpu.VMEM((count, width), BF16)] * 3
        + [
            pltpu.VMEM((count, width), F32),
            pltpu.VMEM((items, PAIR, SLOTS), F32),
            pltpu.VMEM((3, width, 2 * cols), BF16),
            pltpu.VMEM((2 * cols, width), BF16),
            pltpu.VMEM((count, width), BF16),
            pltpu.VMEM((count, PAIR), F32),
            pltpu.VMEM((count, PAIR), F32),
            pltpu.VMEM((width, ROWS), BF16),
            pltpu.SemaphoreType.DMA((12,)),
            pltpu.SemaphoreType.DMA((3 + count // ROWS,)),
        ],
        compiler_params=params(28),
        cost_estimate=cost(8 * count * width * width + 8 * area * PAIR, 24 * count * width, area),
        name="front",
    )(me, off_chip(gain), on_chip(na), *off_chip(tables), [list(off_chip(w[0])), list(w[1])], [off_chip(wo[0]), wo[1]], off_chip(x))


def attention_back_kernel(
    final, first, d_ref, lse_ref, nat_ref, cos_hbm, sin_hbm, q_hbm, k_hbm, v_hbm, *rest
):
    q_ref, k_ref, v_ref, dq_t, dk_acc, dv_acc, cosine, sine, right, sems, row_sems = rest[-11:]
    if final:
        recv_ref, here_ref, there_ref, dq_ref, dk_ref, dv_ref, *outs = rest[:-11]
    else:
        dq_ref, dk_ref, dv_ref, out_ref = rest[:-11]
    count, cols = dq_ref.shape
    items = count // SLOTS
    arrive = Copies(sems)
    arrive.start(cos_hbm.at[:SLOTS, :], cosine)
    arrive.start(sin_hbm.at[:SLOTS, :], sine)
    arriving = ((q_hbm, q_ref), (k_hbm, k_ref), (v_hbm, v_ref))
    for p in range(cols // PAIR):
        source_cols = slice((p + first) * PAIR, (p + first + 1) * PAIR)
        for j, (source, target) in enumerate(arriving):
            copy(source.at[:, source_cols], target.at[:, p * PAIR : (p + 1) * PAIR], row_sems.at[3 * p + j])
    arrive.wait()
    side = lax.broadcasted_iota(jnp.int32, (SLOTS, PAIR), 1) // HEAD
    quarter = nat_ref.shape[0] // 4

    if final:
        send_a, keep_a, send_b, keep_b = outs
        for place in range(4):
            own = slice(place * quarter, place * quarter + quarter)
            values = (here_ref[own, :].astype(F32) + there_ref[own, :].astype(F32)).astype(BF16)
            b0, b1 = place // 2, place % 2
            (send_a if b0 else keep_a)[b1, :, 3 * cols :] = values[: quarter // 2]
            (send_b if b1 else keep_b)[b0, :, 3 * cols :] = values[quarter // 2 :]

    @pl.loop(0, cols // PAIR)
    def _(pair):
        own_cols = pl.ds(pl.multiple_of(pair * PAIR, PAIR), PAIR)
        from_cols = pl.ds(pl.multiple_of((pair + first) * PAIR, PAIR), PAIR)
        for j, (source, target) in enumerate(arriving):
            pltpu.make_async_copy(source.at[:, from_cols], target.at[:, own_cols], row_sems.at[3 * pair + j]).wait()
        k_t = {}

        def scores(task):
            i, h, q0, qb = task
            base, end = i * SLOTS, i * SLOTS + q0 + qb
            q = jnp.where(side[:qb] == h, q_ref[base + q0 : end, own_cols], 0).astype(BF16)
            d = jnp.where(side[:qb] == h, d_ref[base + q0 : end, from_cols], 0).astype(BF16)
            return q, d, dot_nt(k_ref[base:end, own_cols], q), dot_nt(v_ref[base:end, own_cols], d)

        def soften(task, made):
            i, h, q0, qb = task
            q, d, s, dp = made
            lse = lse_ref[pair + first, 2 * i + h : 2 * i + h + 1, q0 : q0 + qb]
            p = jnp.exp(s[q0:] - lse)
            p = jnp.where(causal(p.shape), p, 0.0)
            if q0:
                p = jnp.concatenate([jnp.exp(s[:q0] - lse), p], 0)
            ds = (p * (dp - jnp.sum(p * dp, 0, keepdims=True))).astype(BF16)
            return q, d, p.astype(BF16), ds

        def mix(task, made):
            i, h, q0, qb = task
            q, d, p, ds = made
            end = q0 + qb
            if i not in k_t:
                k_t[i] = k_ref[i * SLOTS : (i + 1) * SLOTS, own_cols].T
            dv, dk = dot(p, d), dot(ds, q)
            if end == SLOTS and h == 0:
                dv_acc[i] = dv
                dk_acc[i] = dk
            else:
                dv_acc[i, :end, :] += dv
                dk_acc[i, :end, :] += dk
            dq_t[i, HEAD * h : HEAD * h + HEAD, q0:end] = dot(k_t[i][HEAD * h : HEAD * h + HEAD, :end], ds)

        pipelined(attention_tasks(items), scores, soften, mix)
        cos_v, sin_v = cosine[...], sine[...]
        for i in range(items):
            own = slice(i * SLOTS, (i + 1) * SLOTS)
            dq = dq_t[i].T * HEAD**-0.5
            dq = (dq * cos_v - swap_halves(dq) * sin_v).astype(BF16)
            dk = dk_acc[i]
            dk = (dk * cos_v - swap_halves(dk) * sin_v).astype(BF16)
            dv = dv_acc[i].astype(BF16)
            for j, (ref, value) in enumerate(((dq_ref, dq), (dk_ref, dk), (dv_ref, dv))):
                ref[own, own_cols] = value
                right[own, j * PAIR : (j + 1) * PAIR] = value
        wide = pl.ds(pl.multiple_of(pair * 3 * PAIR, PAIR), 3 * PAIR)
        for place in range(4):
            own = slice(place * quarter, place * quarter + quarter)
            values = dot(nat_ref[own, :], right[...])
            if final:
                send_a, keep_a, send_b, keep_b = outs
                values = (values + recv_ref[own, wide].astype(F32)).astype(BF16)
                b0, b1 = place // 2, place % 2
                (send_a if b0 else keep_a)[b1, :, wide] = values[: quarter // 2]
                (send_b if b1 else keep_b)[b0, :, wide] = values[quarter // 2 :]
            else:
                out_ref[own, wide] = values.astype(BF16)


def attention_back(q, k, v, d, lse, tables, nat, first, recv=()):
    count, width = q.shape
    cols = width // 2
    items, pairs = count // SLOTS, cols // PAIR
    area = pairs * items * 2 * SLOTS * SLOTS
    final = bool(recv)
    args = [*on_chip((d, lse, nat)), *off_chip((*tables, q, k, v))]
    out_shape = [vmem((count, cols), BF16)] * 3
    if final:
        args += on_chip(recv)
        out_shape += [vmem((2, width // 8, 4 * cols), BF16)] * 4
    else:
        out_shape.append(vmem((width, 3 * cols), BF16))
    return pl.pallas_call(
        functools.partial(attention_back_kernel, final, first),
        in_specs=[CHIP] * 3 + [ANY] * 5 + [CHIP] * (len(args) - 8),
        out_specs=[CHIP] * len(out_shape),
        out_shape=out_shape,
        scratch_shapes=[pltpu.VMEM((count, cols), BF16)] * 3
        + [pltpu.VMEM((items, PAIR, SLOTS), F32)]
        + [pltpu.VMEM((items, SLOTS, PAIR), F32)] * 2
        + [pltpu.VMEM((SLOTS, PAIR), F32)] * 2
        + [pltpu.VMEM((count, 3 * PAIR), BF16), pltpu.SemaphoreType.DMA((2,)), pltpu.SemaphoreType.DMA((3 * pairs,))],
        compiler_params=params(20),
        cost_estimate=cost(20 * area * PAIR + 6 * count * width * cols, 16 * count * cols, area),
        name="attention_back_final" if final else "attention_back_other",
    )(*args)


def row_is_valid(me_ref, lens_ref, items, start, size):
    row = start + lax.broadcasted_iota(jnp.int32, (size, 1), 0)
    valid = row < 0
    for i in range(items):
        valid = valid | ((row >= i * SLOTS) & (row < i * SLOTS + lens_ref[me_ref[1] * items + i]))
    return valid


def split_store(values, cols, total, beside, b0, b1, outs):
    send_a, keep_a, send_b, keep_b = outs
    cut = total // 2
    if cols.start < cut:
        stop = min(cols.stop, cut)
        part = values[:, : stop - cols.start].astype(BF16)
        (send_a if b0 else keep_a)[b1, :, beside + cols.start : beside + stop] = part
    if cols.stop > cut:
        start = max(cols.start, cut)
        part = values[:, start - cols.start :].astype(BF16)
        (send_b if b1 else keep_b)[b0, :, beside + start - cut : beside + cols.stop - cut] = part


def ffn_kernel(final, column, beside, blocks, nf_ref, nft_ref, eb_ref, ebt_ref, wg_hbm, wu_hbm, wd_hbm, *rest):
    wg, wu, wd, hid, in_sems, out_sems = rest[-6:]
    if final:
        recv_ref, *rest = rest[:-6]
        hid_hbm, dg_ref, du_ref, *outs = rest[-7:]
    else:
        hid_hbm, dg_ref, du_ref, out_ref = rest[:-6]
    width = nft_ref.shape[0]
    chunk = pl.ds(column, CHUNK)
    arrive, sent = Copies(in_sems), Copies(out_sems)
    waits = [
        arrive.start(wg_hbm.at[:, chunk], wg),
        arrive.start(wu_hbm.at[:, chunk], wu),
        arrive.start(wd_hbm.at[chunk, :], wd),
    ]

    def products(own):
        made = []
        for ref, weight, multiply in ((nf_ref, wg, dot), (nf_ref, wu, dot), (eb_ref, wd, dot_nt)):
            if waits:
                waits.pop(0).wait()
            made.append(multiply(ref[own, :], weight[...]))
        return made

    def point(own, made):
        g, u, dh = made
        sig = 0.5 * jnp.tanh(0.5 * g) + 0.5
        silu = g * sig
        hid[own, :] = (silu * u).astype(BF16)
        du_ref[own, :] = (dh * silu).astype(BF16)
        dg_ref[own, :] = (dh * u * (sig + silu * (1.0 - sig))).astype(BF16)

    made = None
    for i in range(len(blocks) + 1):
        upcoming = products(blocks[i]) if i < len(blocks) else None
        if made is not None:
            point(blocks[i - 1], made)
        made = upcoming
    quarter = width // 4
    for place in range(4):
        if place == 1:
            sent.start(hid, hid_hbm)
        own = slice(place * quarter, place * quarter + quarter)
        grads = [dot(nft_ref[own, :], dg_ref[...]), dot(nft_ref[own, :], du_ref[...]), dot(ebt_ref[own, :], hid[...])]
        for j, values in enumerate(grads):
            cols = slice(j * CHUNK, (j + 1) * CHUNK)
            if final:
                split_store(values + recv_ref[own, cols].astype(F32), cols, 3 * CHUNK, beside, place // 2, place % 2, outs)
            else:
                out_ref[own, cols] = values.astype(BF16)
    sent.wait()


def ffn(nf, nft, eb, ebt, wg, wu, wd, chunk, recv=None, base=()):
    count, width = nf.shape
    final = recv is not None
    wide = 3 * CHUNK
    sizes = [512 * count // 1152, 384 * count // 1152]
    edges = [0, sizes[0], sum(sizes), count]
    blocks = [slice(i, j) for i, j in zip(edges, edges[1:])]
    weights = off_chip((wg, wu, wd)) if final else (wg, wu, wd)
    args = [*on_chip((nf, nft, eb, ebt)), *weights]
    out_shape = [hbm((count, CHUNK), BF16)] + [vmem((count, CHUNK), BF16)] * 2
    if final:
        args += [on_chip(recv), *on_chip(base)]
        out_shape += [vmem((2, width // 4, wd.shape[0] // CHUNK * wide // 2), BF16)] * 4
    else:
        out_shape.append(vmem((width, wide), BF16))
    return pl.pallas_call(
        functools.partial(ffn_kernel, final, chunk * CHUNK, chunk * wide // 2, blocks),
        in_specs=[CHIP] * 4 + [ANY] * 3 + [CHIP] * (len(args) - 7),
        out_specs=[ANY] + [CHIP] * (len(out_shape) - 1),
        out_shape=out_shape,
        input_output_aliases={8 + i: 3 + i for i in range(len(base))},
        scratch_shapes=[pltpu.VMEM((width, CHUNK), BF16)] * 2
        + [
            pltpu.VMEM((CHUNK, width), BF16),
            pltpu.VMEM((count, CHUNK), BF16),
            pltpu.SemaphoreType.DMA((3,)),
            pltpu.SemaphoreType.DMA((3,)),
        ],
        compiler_params=params(14),
        cost_estimate=cost(12 * count * width * CHUNK, 8 * count * width + 12 * width * CHUNK),
        name="ffn_final" if final else "ffn_other",
    )(*args)


def norm_back_rows(rows, d_normed, gain):
    inv = lax.rsqrt(jnp.mean(rows * rows, -1, keepdims=True) + EPS)
    unit = rows * inv
    weighted = d_normed * gain
    d_rows = inv * (weighted - unit * jnp.mean(weighted * unit, -1, keepdims=True))
    return d_rows, jnp.sum(d_normed * unit, 0, keepdims=True)


def ffn_back_kernel(
    dp, me_ref, gain_hbm, h1_hbm, eb_ref, o_ref, d_refs, wg_hbm, wu_hbm, wo_hbm,
    dh1_ref, do_ref, dgain_ref, there_ref, here_ref, gain_ref, h1_ref, weights, wo, turn, abt, in_sems,
):
    count, width = h1_ref.shape
    cols, half = wo_hbm[0].shape[0], wg_hbm[0].shape[1]
    arrive = Copies(in_sems)
    w_in = [arrive.start(w, weights.at[i]) for i, w in enumerate((*wg_hbm, *wu_hbm))]
    wo_in = [arrive.start(w, wo.at[i * cols : (i + 1) * cols, :]) for i, w in enumerate(wo_hbm)]
    blocks = row_blocks(count)
    h1_in = [arrive.start(h1_hbm.at[own, :], h1_ref.at[own, :]) for own in blocks]
    h1_in.append(arrive.start(gain_hbm, gain_ref))
    per = len(d_refs) // len(w_in)

    def product(i):
        total = None
        for j, w in enumerate(w_in):
            if i == 0:
                w.wait()
            left = jnp.concatenate([d[blocks[i], :] for d in d_refs[j * per : (j + 1) * per]], 1)
            term = dot_nt(left, weights[j])
            total = term if total is None else total + term
        return total

    dnf, gain_total = product(0), None
    for c in wo_in:
        c.wait()
    for c in h1_in:
        c.wait()
    for i, own in enumerate(blocks):
        upcoming = product(i + 1) if i + 1 < len(blocks) else None
        d_rows, gain_part = norm_back_rows(h1_ref[own, :], dnf, gain_ref[...][None, :])
        gain_total = gain_part if gain_total is None else gain_total + gain_part
        back = eb_ref[own, :].astype(F32) + d_rows
        dh1_ref[own, :] = back
        rounded = back.astype(BF16)
        do_ref[own, :] = dot_nt(rounded, wo[...]).astype(BF16)
        store_transposed(rounded, turn, abt.at[:, own], me_ref, dp)
        dnf = upcoming
    dgain_ref[...] = gain_total
    quarter = width // 4
    for start in range(0, width, quarter):
        own = slice(start, start + quarter)
        total = dot(abt[own, :], o_ref[...])
        there_ref[own, :] = total[:, cols:].astype(BF16)
        here_ref[own, :] = total[:, :cols].astype(BF16)


def ffn_back(dp, me, h1, eb, gain, wg, wu, wo, o, d):
    count, width = h1.shape
    half, cols = wg[0].shape[1], wo[0].shape[0]
    return pl.pallas_call(
        functools.partial(ffn_back_kernel, dp),
        in_specs=[SCALAR, ANY, ANY, CHIP, CHIP, [CHIP] * len(d), [ANY] * 2, [ANY] * 2, [ANY] * 2],
        out_specs=[CHIP] * 5,
        out_shape=[
            vmem((count, width), F32),
            vmem((count, 2 * cols), BF16),
            vmem((1, width), F32),
            vmem((width, cols), BF16),
            vmem((width, cols), BF16),
        ],
        scratch_shapes=[
            pltpu.VMEM((width,), F32),
            pltpu.VMEM((count, width), F32),
            pltpu.VMEM((4, width, half), BF16),
            pltpu.VMEM((2 * cols, width), BF16),
            pltpu.VMEM((width, ROWS), BF16),
            pltpu.VMEM((width, count), BF16),
            pltpu.SemaphoreType.DMA((7 + count // ROWS,)),
        ],
        compiler_params=params(20),
        cost_estimate=cost(4 * count * width * (2 * half + 2 * cols), 20 * count * width + 8 * count * half),
        name="ffn_back",
    )(
        me, *off_chip((gain, h1)), *on_chip((eb, o)), list(on_chip(d)),
        [off_chip(wg[0]), wg[1]], [off_chip(wu[0]), wu[1]], [off_chip(wo[0]), wo[1]],
    )


def finish_kernel(
    items, me_ref, lens_ref, gain_hbm, dh1_ref, d_refs, x_hbm, w_hbm, h1_hbm, wd_hbm, hid_hbm,
    gin_hbm, out_hbm, dgain_ref, gain_ref, weights, x, gin, h1, wd, hid, out, in_sems, out_sems
):
    arrive, sent = Copies(in_sems), Copies(out_sems)
    cols, per = w_hbm[0].shape[1], 3
    w_in = [
        arrive.start(w, weights.at[i // per, :, (i % per) * cols : (i % per + 1) * cols]) for i, w in enumerate(w_hbm)
    ]
    blocks = row_blocks(x.shape[0])
    x_in = [arrive.start(x_hbm.at[own, :], x.at[own, :]) for own in blocks] + [arrive.start(gain_hbm, gain_ref)]
    half, size = wd_hbm[0].shape[0], hid_hbm[0].shape[1]
    wd_in = [arrive.start(w, wd.at[i * half : (i + 1) * half, :]) for i, w in enumerate(wd_hbm)]
    own = blocks[0]
    row_in = [arrive.start(h.at[own, :], hid.at[:, j * size : (j + 1) * size]) for j, h in enumerate(hid_hbm)]
    row_in.append(arrive.start(h1_hbm.at[own, :], h1))

    def product(i):
        total = None
        for j in range(len(w_in) // per):
            if i == 0:
                for c in w_in[j * per : (j + 1) * per]:
                    c.wait()
            left = jnp.concatenate([d[blocks[i], :] for d in d_refs[j * per : (j + 1) * per]], 1)
            term = dot_nt(left, weights[j])
            total = term if total is None else total + term
        return total

    dna, gain_total, total = product(0), None, None
    for c in x_in:
        c.wait()
    for i, own in enumerate(blocks):
        upcoming = product(i + 1) if i + 1 < len(blocks) else None
        if i + 1 == len(blocks):
            for c in wd_in + row_in:
                c.wait()
            total = h1[...] + dot(hid[...], wd[...])
        d_rows, gain_part = norm_back_rows(x[own, :].astype(F32), dna, gain_ref[...][None, :])
        gain_total = gain_part if gain_total is None else gain_total + gain_part
        gin[own, :] = dh1_ref[own, :] + d_rows
        sent.start(gin.at[own, :], gin_hbm.at[own, :])
        dna = upcoming
    dgain_ref[...] = gain_total
    own = blocks[0]
    out[...] = jnp.where(row_is_valid(me_ref, lens_ref, items, own.start, own.stop), total, 0.0).astype(BF16)
    sent.start(out, out_hbm.at[own, :])
    sent.wait()


def finish(me, lens, x, dh1, gain, weights, grads, h1, wd, hid):
    count, width = x.shape
    cols, half = weights[0].shape[1], wd[0].shape[0]
    deep, mine, steps = cols * len(weights), len(weights) // 2, count // ROWS
    return pl.pallas_call(
        functools.partial(finish_kernel, count // SLOTS),
        in_specs=[SCALAR, SCALAR, ANY, CHIP, [CHIP] * len(grads), ANY, [ANY] * len(weights), ANY, [ANY] * 2, [ANY] * len(hid)],
        out_specs=[ANY, ANY, CHIP],
        out_shape=[hbm((count, width), F32), hbm((count, width), BF16), vmem((1, width), F32)],
        scratch_shapes=[
            pltpu.VMEM((width,), F32),
            pltpu.VMEM((2, width, deep // 2), BF16),
            pltpu.VMEM((count, width), BF16),
            pltpu.VMEM((count, width), F32),
            pltpu.VMEM((ROWS, width), F32),
            pltpu.VMEM((2 * half, width), BF16),
            pltpu.VMEM((ROWS, 2 * half), BF16),
            pltpu.VMEM((ROWS, width), BF16),
            pltpu.SemaphoreType.DMA((len(weights) + 3 + steps * (2 + len(hid)),)),
            pltpu.SemaphoreType.DMA((2 * steps,)),
        ],
        compiler_params=params(28),
        cost_estimate=cost(2 * count * width * (deep + 2 * half), 16 * count * width + 2 * count * (deep + 2 * half)),
        name="finish",
    )(
        me, lens, off_chip(gain), on_chip(dh1), list(on_chip(grads)), off_chip(x),
        [*off_chip(weights[:mine]), *weights[mine:]], off_chip(h1), [off_chip(wd[0]), wd[1]], list(off_chip(hid)),
    )


def output_kernel(items, blocks, me_ref, lens_ref, h1_hbm, wd_hbm, hid_hbm, *rest):
    out_hbm, h1, wd, hid, out, in_sems, out_sems = rest[-7:]
    arrive, sent = Copies(in_sems), Copies(out_sems)
    half, size = wd_hbm[0].shape[0], hid_hbm[0].shape[1]
    wd_in = [arrive.start(w, wd.at[i * half : (i + 1) * half, :]) for i, w in enumerate(wd_hbm)]
    row_in = [
        [arrive.start(h.at[own, :], hid.at[own, j * size : (j + 1) * size]) for j, h in enumerate(hid_hbm)]
        + [arrive.start(h1_hbm.at[own, :], h1.at[own, :])]
        for own in blocks
    ]

    def down(i):
        for c in (wd_in if i == 0 else []) + row_in[i]:
            c.wait()
        return dot(hid[blocks[i], :], wd[...])

    total = down(0)
    for i, own in enumerate(blocks):
        upcoming = down(i + 1) if i + 1 < len(blocks) else None
        total = total + h1[own, :]
        out[own, :] = jnp.where(row_is_valid(me_ref, lens_ref, items, own.start, own.stop - own.start), total, 0.0).astype(BF16)
        sent.start(out.at[own, :], out_hbm.at[own, :])
        total = upcoming
    sent.wait()


def layer_output(me, lens, h1, wd, hid, rows, base=None):
    count, width = h1.shape
    half = wd[0].shape[0]
    blocks = [slice(i, i + ROWS) for i in range(rows.start, rows.stop, ROWS)]
    args = [me, lens, off_chip(h1), [off_chip(wd[0]), wd[1]], list(off_chip(hid))]
    if base is not None:
        args.append(base)
    return pl.pallas_call(
        functools.partial(output_kernel, count // SLOTS, blocks),
        in_specs=[SCALAR, SCALAR, ANY, [ANY] * 2, [ANY] * len(hid)] + [ANY] * (len(args) - 5),
        out_specs=ANY,
        out_shape=hbm((count, width), BF16),
        input_output_aliases={} if base is None else {3 + len(wd) + len(hid): 0},
        scratch_shapes=[
            pltpu.VMEM((count, width), F32),
            pltpu.VMEM((2 * half, width), BF16),
            pltpu.VMEM((count, 2 * half), BF16),
            pltpu.VMEM((count, width), BF16),
            pltpu.SemaphoreType.DMA((2 + len(blocks) * (1 + len(hid)),)),
            pltpu.SemaphoreType.DMA((len(blocks),)),
        ],
        compiler_params=params(22),
        cost_estimate=cost(2 * count * width * half, 3 * count * width + 2 * count * half),
        name="layer_output",
    )(*args)


def second_kernel(keep_a, recv_a, keep_b, recv_b, send_a, send_b):
    send_a[...] = (keep_a[1].astype(F32) + recv_a[1].astype(F32)).astype(BF16)
    send_b[...] = (keep_b[1].astype(F32) + recv_b[1].astype(F32)).astype(BF16)


def third_kernel(keep_a, recv_a, last_a, keep_b, recv_b, last_b, keep_ref, send_refs):
    group, cut = keep_ref.shape[0], keep_a.shape[2]
    for z in range(len(send_refs) + 1):
        own = slice(z * group, z * group + group)
        for cols, keep, recv, last in (
            (slice(0, cut), keep_a, recv_a, last_a),
            (slice(cut, 2 * cut), keep_b, recv_b, last_b),
        ):
            total = keep[0, own, :].astype(F32) + recv[0, own, :].astype(F32) + last[own, :].astype(F32)
            if z:
                send_refs[z - 1][:, cols] = total.astype(BF16)
            else:
                keep_ref[:, cols] = total


def swap_dp(array, dp, relative):
    return lax.ppermute(array, "dp", [(i, i ^ relative) for i in range(dp)])


def first_swaps(pieces, dp):
    return swap_dp(pieces[0], dp, 1), swap_dp(pieces[2], dp, 2)


def second_swaps(pieces, recv, dp):
    _, keep_a, _, keep_b = pieces
    _, quarter, cut = keep_a.shape
    next_a, next_b = pl.pallas_call(
        second_kernel,
        in_specs=[CHIP] * 4,
        out_shape=[sds((quarter, cut), BF16)] * 2,
        compiler_params=params(8),
        cost_estimate=cost(quarter * cut * 2, quarter * cut * 12),
        name="second_sum",
    )(*on_chip((keep_a, recv[0], keep_b, recv[1])))
    return swap_dp(next_a, dp, 2), swap_dp(next_b, dp, 1)


def third_swaps(pieces, recv, last, dp):
    _, keep_a, _, keep_b = pieces
    _, quarter, cut = keep_a.shape
    far = dp // 4
    group = quarter // far
    kept, sends = pl.pallas_call(
        third_kernel,
        out_shape=[sds((group, 2 * cut), F32), [sds((group, 2 * cut), BF16)] * (far - 1)],
        compiler_params=params(12),
        cost_estimate=cost(quarter * cut * 4, quarter * cut * 16),
        name="third_sum",
    )(keep_a, recv[0], last[0], keep_b, recv[1], last[1])
    return kept, tuple(swap_dp(send, dp, 4 * (z + 1)) for z, send in enumerate(sends))


def third_rows_kernel(keep_a, recv_a, last_a, keep_b, recv_b, last_b, keep_ref, send_refs):
    group = keep_ref.shape[0]
    inner = keep_a.shape[1] // group
    for z in range(len(send_refs) + 1):
        keep, recv, last = (keep_a, recv_a, last_a) if z < inner else (keep_b, recv_b, last_b)
        own = slice(z % inner * group, z % inner * group + group)
        total = keep[0, own, :].astype(F32) + recv[0, own, :].astype(F32) + last[own, :].astype(F32)
        if z:
            send_refs[z - 1][...] = total.astype(BF16)
        else:
            keep_ref[...] = total


def third_rows_swaps(pieces, recv, last, dp):
    _, keep_a, _, keep_b = pieces
    _, rows, cols = keep_a.shape
    far = dp // 4
    group = 2 * rows // far
    kept, sends = pl.pallas_call(
        third_rows_kernel,
        in_specs=[CHIP] * 6,
        out_shape=[sds((group, cols), F32), [sds((group, cols), BF16)] * (far - 1)],
        compiler_params=params(12),
        cost_estimate=cost(rows * cols * 8, rows * cols * 20),
        name="third_rows_sum",
    )(*on_chip((keep_a, recv[0], last[0], keep_b, recv[1], last[1])))
    return kept, tuple(swap_dp(send, dp, 4 * (z + 1)) for z, send in enumerate(sends))


def near_kernel(keep_a, recv_a, last_a, keep_b, recv_b, last_b, keep_ref, send_ref):
    group, cut = keep_ref.shape[1], keep_a.shape[2]
    for z in range(4):
        own = slice(z * group, z * group + group)
        for cols, keep, recv, last in (
            (slice(0, cut), keep_a, recv_a, last_a),
            (slice(cut, 2 * cut), keep_b, recv_b, last_b),
        ):
            total = keep[0, own, :].astype(F32) + recv[0, own, :].astype(F32) + last[own, :].astype(F32)
            (send_ref if z % 2 else keep_ref)[z // 2, :, cols] = total.astype(BF16)


def far_kernel(keep, recv, send_ref):
    send_ref[...] = (keep[1].astype(F32) + recv[1].astype(F32)).astype(BF16)


def near_swap(pieces, recv, last, dp):
    _, keep_a, _, keep_b = pieces
    _, quarter, cut = keep_a.shape
    kept, send = pl.pallas_call(
        near_kernel,
        in_specs=[CHIP] * 6,
        out_shape=[sds((2, quarter // 4, 2 * cut), BF16)] * 2,
        compiler_params=params(12),
        cost_estimate=cost(quarter * cut * 4, quarter * cut * 16),
        name="near_sum",
    )(*on_chip((keep_a, recv[0], last[0], keep_b, recv[1], last[1])))
    return kept, swap_dp(send, dp, 4)


def far_swap(kept, recv, dp):
    send = pl.pallas_call(
        far_kernel,
        in_specs=[CHIP] * 2,
        out_shape=sds(kept.shape[1:], BF16),
        compiler_params=params(6),
        cost_estimate=cost(kept.size, 4 * kept.size),
        name="far_sum",
    )(*on_chip((kept, recv)))
    return swap_dp(send, dp, 8)


def last_kernel(kept, far_refs, outs):
    *qkv, out = outs
    cols = out.shape[1]

    def total(own):
        made = kept[:, own].astype(F32)
        for far in far_refs:
            made = made + far[:, own].astype(F32)
        return made

    for p in range(cols // PAIR):
        for j, ref in enumerate(qkv):
            ref[:, p * PAIR : (p + 1) * PAIR] = total(slice((3 * p + j) * PAIR, (3 * p + j + 1) * PAIR))
    out[...] = total(slice(3 * cols, 4 * cols))


def last_sum(kept, far):
    group, cols = kept.shape
    return pl.pallas_call(
        lambda kept, far_refs, *outs: last_kernel(kept, far_refs, outs),
        out_shape=[sds((group, cols // 4), F32)] * 4,
        compiler_params=params(6),
        name="last_sum",
    )(kept, list(far))


def total_of(kept, arrived):
    for part in arrived:
        kept = kept + part.astype(F32)
    return kept


fence = lax.optimization_barrier


def swap_sum(values, dp, relatives):
    count = 1 << len(relatives)
    terms = [values]
    for r in range(1, count):
        relative = sum(bit for i, bit in enumerate(relatives) if r >> i & 1)
        terms.append(swap_dp(values, dp, relative))
    while len(terms) > 1:
        terms = [terms[i] + terms[i + 1] for i in range(0, len(terms), 2)]
    return terms[0]


def local(
    dp, mp, tokens, lengths, gain_attn, w_query, w_key, w_value, w_out, gain_ffn, w_gate, w_up, w_down, cotangent
):
    count, width = tokens.shape
    me = jnp.stack([lax.axis_index("dp"), lax.axis_index("mp")]).astype(jnp.int32)
    gain_a, gain_f = gain_attn, gain_ffn

    def other(array):
        return lax.ppermute(array, "mp", [(0, 1), (1, 0)])

    wq, wk, wv, wo = ((w, other(w)) for w in (w_query, w_key, w_value, w_out))
    tables = tuple(jnp.asarray(t) for t in position_tables(count))

    na, nat, eb, ebt = prepare(dp, me, lengths, tokens, cotangent, gain_a)
    na, wq, wk, wv, w_gate, w_up, w_down = fence((na, wq, wk, wv, w_gate, w_up, w_down))
    wg, wu, wd = ((w, other(w)) for w in (w_gate, w_up, w_down))
    nat, ebt = finish_transposed(nat, me, dp), finish_transposed(ebt, me, dp)
    q, k, v, h1, o, lse, nf, nft = front(
        dp, me, na, tables, gain_f, ((wq[0], wk[0], wv[0]), (wq[1], wk[1], wv[1])), wo, tokens
    )
    nft = finish_transposed(nft, me, dp)

    half = w_gate.shape[1]
    chunks = half // CHUNK
    made, back = [], []
    for c in range(chunks):
        nf, made = fence((nf, made))
        *rest, there = ffn(nf, nft, eb, ebt, wg[1], wu[1], wd[1], c)
        made.append(rest)
        back.append(other(there))
    theirs = made
    made, piece = [], ()
    for c in range(chunks):
        nf, here, theirs, made, piece = fence((nf, back[c], theirs, made, piece))
        *rest, sa, ka, sb, kb = ffn(nf, nft, eb, ebt, wg[0], wu[0], wd[0], c, here, piece)
        made.append(rest)
        piece = (sa, ka, sb, kb)
    h1, made, theirs, piece = fence((h1, made, theirs, piece))
    recv = first_swaps(piece, dp)
    parts = made + theirs
    hid = [p[0] for p in parts]
    dh1, do, dgain_f, out_there, out_here = ffn_back(
        dp, me, h1, eb, gain_f, wg, wu, wo, o, [p[1] for p in parts] + [p[2] for p in parts]
    )
    out_there, out_here, do = fence((out_there, out_here, do))
    out_back = other(out_there)
    heads = w_query.shape[1] // PAIR
    *d1, qkv_there = attention_back(q, k, v, do, lse, tables, nat, heads)
    qkv_there, out_back, d1, recv, do = fence((qkv_there, out_back, d1, recv, do))
    qkv_back = other(qkv_there)
    last = second_swaps(piece, recv, dp)
    *d0, sa, ka, sb, kb = attention_back(q, k, v, do, lse, tables, nat, 0, (qkv_back, out_here, out_back))
    q_piece = (sa, ka, sb, kb)
    d0, q_piece, last = fence((d0, q_piece, last))
    two_steps = dp == 16
    recv_q = first_swaps(q_piece, dp)
    kept, near = (near_swap if two_steps else third_swaps)(piece, recv, last, dp)
    grad_input, output, dgain_a = finish(
        me, lengths, tokens, dh1, gain_a, (wq[0], wk[0], wv[0], wq[1], wk[1], wv[1]), (*d0, *d1), h1, wd, hid
    )
    dgain_a, recv_q, near, h1 = fence((dgain_a, recv_q, near, h1))
    far = far_swap(kept, near, dp) if two_steps else None
    last_q = second_swaps(q_piece, recv_q, dp)
    gains = jnp.concatenate([dgain_a, dgain_f], 0)
    gains = swap_sum(gains + other(gains), dp, (1,))
    output = layer_output(me, lengths, h1, wd, hid, slice(ROWS, count), output)
    gains, last_q, output = fence((gains, last_q, output))
    kept_q, far_q = third_rows_swaps(q_piece, recv_q, last_q, dp)
    gains = swap_sum(gains, dp, (2,))
    gains, far = fence((gains, far))
    far_bits = [1 << bit for bit in range(2, dp.bit_length() - 1)]
    for bits in (far_bits,) if two_steps else ((bit,) for bit in far_bits):
        gains = swap_sum(gains, dp, bits)
    total = total_of(kept[0].astype(F32), (near[0], far)) if two_steps else total_of(kept, near)
    gq, gk, gv, out_piece = last_sum(kept_q, far_q)
    side, wide = total.shape[1] // 2, 3 * CHUNK // 2
    ffn_pieces = [
        jnp.concatenate([total[:, c * wide : (c + 1) * wide], total[:, side + c * wide : side + (c + 1) * wide]], 1)
        for c in range(chunks)
    ]
    g_gate, g_up, g_down = (
        jnp.concatenate([p[:, i * CHUNK : (i + 1) * CHUNK] for p in ffn_pieces], 1) for i in range(3)
    )
    return (
        output, grad_input, gains[0], gq, gk, gv, out_piece.T, gains[1], g_gate, g_up, g_down.T,
    )


def solution(mesh):
    in_specs = (
        P(("dp", "mp"), None),
        P("dp"),
        P(),
        P(None, "mp"),
        P(None, "mp"),
        P(None, "mp"),
        P("mp", None),
        P(),
        P(None, "mp"),
        P(None, "mp"),
        P("mp", None),
        P(("dp", "mp"), None),
    )
    out_specs = (
        P(("dp", "mp"), None),
        P(("dp", "mp"), None),
        P(),
        P("dp", "mp"),
        P("dp", "mp"),
        P("dp", "mp"),
        P("mp", "dp"),
        P(),
        P("dp", "mp"),
        P("dp", "mp"),
        P("mp", "dp"),
    )
    body = functools.partial(local, mesh.shape["dp"], mesh.shape["mp"])
    return jax.shard_map(body, mesh=mesh, in_specs=in_specs, out_specs=out_specs, check_vma=False)
```
